32 devices in a mesh: group: 4 (over z), expert: 8 (over y, x, core).
Axes of the slice: x: 2, y: 2, z: 4, core: 2. Of those that a mesh axis runs over, the one named last changes fastest.
Arguments:
- group_logits: float32 [4096, 4], P(('group', 'expert')), may hold values from -6 to 6
- expert_logits: float32 [4096, 32], P(('group', 'expert')), may hold values from -6 to 6
- expert_ids: int32 [4096, 2], P(('group', 'expert')), may hold values from 0 to 31, all different within a row; in each aligned block of 128 rows (0 to 127, 128 to 255, ...) at most 16 rows name the same one
- cotangent: bfloat16 [4096, 3584], P(('group', 'expert')), may hold values from -6 to 6
- hidden_saved: bfloat16 [32, 512, 1024], P(('group', 'expert')), may hold values from -0.1875 to 0.1875
- w_down: bfloat16 [32, 1024, 3584], P(('group', 'expert')), may hold values from -0.1875 to 0.1875
Outputs:
- hidden_grad: bfloat16 [32, 512, 1024], P(('group', 'expert'))
- d_group_logits: float32 [4096, 4], P(('group', 'expert'))
- d_expert_logits: float32 [4096, 32], P(('group', 'expert'))
The draws below stay inside these ranges and needn't reach their ends.
Inputs may be any that keep to these rules, and one draw needn't show every extreme that they name: `expert_ids`: within the 128 tokens of one device no expert is named by more than 16 choices, a bound that some block reaches; the 2 experts of a token differ.
All inputs are finite; a program needn't handle non-finite values.
Results may differ from the reference program's by a relative error of at most 0.0045.
Values may be sent and summed in bfloat16 or wider, within the bound.
No kernel may reach another device: no remote copies, remote signals or barrier semaphores. Data moves between devices by JAX's collectives and lax.ppermute only.
A program may use at most 64 MiB of HBM per device.

```python
import math
import jax
import jax.numpy as jnp
import numpy as np
from jax import lax

D = 3584
F = 1024
TOP = 2
ITERS = 5
TOK_DEV = 128
GROUPS = 4
EXP_GROUP = 8
EXPERTS = 32
TOKENS = 4096
CAP = 16
SLOTS = 512
N_GROUP = 4
N_EXPERT = 8


def ramped(key, row_count, column_count):
    base_key = jax.random.fold_in(key, 11)
    sign_key = jax.random.fold_in(key, 12)
    base_values = 1.5 * jax.random.normal(base_key, (row_count, column_count), jnp.float32)
    column_signs = jnp.where(jax.random.uniform(sign_key, (column_count,), jnp.float32) < 0.5, 1.0, -1.0)
    ramp_values = jnp.log1p(2.0 * jnp.arange(row_count, dtype=jnp.float32) / max(row_count - 1, 1))
    return jnp.clip(base_values + column_signs[None, :] * ramp_values[:, None], -6.0, 6.0)


def draw_group_logits(key, part):
    return ramped(key, TOKENS, GROUPS)


def draw_expert_logits(key, part):
    return ramped(jax.random.fold_in(key, 5), TOKENS, EXPERTS)


def block_scale(key, dims, split, smallest, largest):
    level, own = 1.0, jax.random.fold_in(key, 6)
    for axis_at, blocks in split:
        draws = jnp.exp(jax.random.uniform(jax.random.fold_in(own, axis_at), (blocks,), jnp.float32, smallest / len(split), largest / len(split)))
        level = level * jnp.repeat(draws, dims[axis_at] // blocks).reshape([-1 if axis == axis_at else 1 for axis in range(len(dims))])
    return level


def shared_out(key, own, number, rows, count, top, most, slope):
    ranking = jax.random.permutation(key, count)
    packed, ordinary = portions_of(count, rows * top, most, slope, True), portions_of(count, rows * top, most, slope, False)
    places = jnp.arange(count)

    def named(tallies, turn):
        used = int((tallies > 0).sum())
        fixed = max(1, used // 4)
        shifted = fixed + (places - fixed + turn * (used - fixed)) % max(1, count - fixed)
        return jnp.zeros((count,), jnp.int32).at[ranking[jnp.where(places < fixed, places, shifted)]].set(jnp.asarray(tallies, jnp.int32))

    tallies = jnp.where(number % 4 == 0, named(packed, number // 4), named(ordinary, number - number // 4 - 1))
    mixed = jax.random.permutation(jax.random.fold_in(own, 3), count)
    source_of, taker = mixed[0:count // 2 * 2:2], mixed[1:count // 2 * 2:2]
    margin = jnp.minimum(tallies[source_of] - 1, most - tallies[taker]) // 2
    margin = jnp.where((source_of == ranking[0]) | (taker == ranking[0]) | (tallies[taker] == 0), 0, jnp.maximum(margin, 0))
    shifted = jax.random.randint(jax.random.fold_in(own, 4), (count // 2,), 0, 1 << 20) % (margin + 1)
    tallies = tallies.at[source_of].add(-shifted).at[taker].add(shifted)
    items = jnp.searchsorted(jnp.cumsum(tallies), jnp.arange(rows * top), side="right").astype(jnp.int32)
    listing = items.reshape(top, rows).T
    listing = listing[jax.random.permutation(jax.random.fold_in(own, 1), rows)]
    turn = jax.random.randint(jax.random.fold_in(own, 2), (rows, 1), 0, top)
    return jnp.take_along_axis(listing, (jnp.arange(top)[None, :] + turn) % top, axis=1)


def portions_of(count, total, most, slope, full):
    weights = [(1 << 20) // math.isqrt(grade ** slope) + 1 for grade in range(1, count + 1)]
    largest = most if full else min(most, max(-(-total // count), total * weights[0] // sum(weights)))
    least = 1 if total - largest >= count - 1 else 0
    holding, rest = [largest] + [least] * (count - 1), total - largest - least * (count - 1)
    while rest > 0:
        free = [i for i in range(1, count) if holding[i] < largest] or [i for i in range(1, count) if holding[i] < most]
        pool, budget = sum([weights[i] for i in free]), rest
        for i in free:
            extra = min(most - holding[i], max(1, budget * weights[i] // pool), rest)
            holding[i] = holding[i] + extra
            rest = rest - extra
    return np.array(holding)


def bell_draw(key, extent, deviation, most, cuts=(), held_as=jnp.bfloat16):
    entries = jax.random.normal(key, extent, jnp.float32) * deviation
    if len(cuts) > 0:
        entries = block_scale(key, extent, cuts, -0.22, 0.18) * entries
    return jnp.clip(entries, min=-most, max=most).astype(held_as)


def setup_inputs(seed: int = 0) -> dict:
    seeds = jax.random.split(jax.random.key(seed), 7)
    group_logits = draw_group_logits(jax.random.fold_in(seeds[6], 71), 0)
    expert_logits = draw_expert_logits(jax.random.fold_in(seeds[6], 71), 0)
    expert_ids_keys = jax.random.split(jax.random.fold_in(seeds[2], 1), TOKENS // TOK_DEV)
    expert_ids_turns = jax.random.permutation(jax.random.fold_in(seeds[2], 3), TOKENS // TOK_DEV)
    expert_ids = jax.vmap(lambda own, number: shared_out(jax.random.fold_in(seeds[2], 2), own, number, TOK_DEV, EXPERTS, TOP, CAP, 2))(expert_ids_keys, expert_ids_turns).reshape((TOKENS, TOP))
    cotangent = bell_draw(seeds[3], (TOKENS, D), 1.0, 6.0, ((0, 32),))
    hidden_saved = bell_draw(seeds[4], (EXPERTS, SLOTS, F), (1.0 / F ** 0.5), 0.1875, ((0, 32),))
    w_down = bell_draw(seeds[5], (EXPERTS, F, D), F ** -0.5, 0.1875, ((0, 32),))
    return dict(group_logits=group_logits, expert_logits=expert_logits, expert_ids=expert_ids, cotangent=cotangent, hidden_saved=hidden_saved, w_down=w_down)


SOFTCAP = 4.0


def capped(logits):
    return jnp.exp(SOFTCAP * jnp.tanh(logits / SOFTCAP))


def squashing(logits):
    bounded = jnp.tanh(logits / SOFTCAP)
    return 1.0 - bounded * bounded


def balance_level(level_in, target, column_sum):
    scaled = level_in * (target / column_sum)
    return scaled, jnp.sum(scaled, -1, keepdims=True)


def adjoint_local(out_grad, level_in, target, column_sum):
    scaled, row_total = balance_level(level_in, target, column_sum)
    level_out = scaled / row_total
    scaled_grad = (out_grad - jnp.sum(out_grad * level_out, -1, keepdims=True)) / row_total
    return scaled_grad, jnp.sum(scaled_grad * level_in, 0)


def adjoint_finish(scaled_grad, inner, target, column_sum):
    return (target / column_sum) * (scaled_grad - inner / column_sum)


def reference(group_logits, expert_logits, expert_ids, cotangent, hidden_saved, w_down):
    group_aff = capped(group_logits)
    expert_aff = capped(expert_logits).reshape(TOKENS, GROUPS, EXP_GROUP)
    target_group = TOKENS / GROUPS
    target_expert = TOKENS / EXP_GROUP

    def forward(current, unused):
        group_in, expert_in = current
        group_cols = jnp.sum(group_in, 0)
        expert_cols = jnp.sum(expert_in, 0)
        scaled_g, rowsum_g = balance_level(group_in, target_group, group_cols)
        scaled_e, rowsum_e = balance_level(expert_in, target_expert, expert_cols)
        return (scaled_g / rowsum_g, scaled_e / rowsum_e), (group_in, expert_in, group_cols, expert_cols)

    (group_prob, expert_prob), stored = lax.scan(forward, (group_aff, expert_aff), None, length=ITERS)

    flat_ids = expert_ids.reshape(-1)
    group_of = expert_ids // EXP_GROUP
    pick_group = jnp.take_along_axis(group_prob, group_of, 1)
    pick_expert = jnp.take_along_axis(expert_prob.reshape(TOKENS, EXPERTS), expert_ids, 1)
    pair_prob = pick_group * pick_expert
    total_prob = jnp.sum(pair_prob, 1, keepdims=True)
    gate_prob = pair_prob / total_prob
    gate_sent = gate_prob.astype(jnp.bfloat16).reshape(-1)

    devices = N_GROUP * N_EXPERT
    per_device = TOK_DEV * TOP
    counted = flat_ids.shape[0]
    serial = jnp.arange(counted, dtype=jnp.int32)
    owner_device = serial // per_device
    picked = (flat_ids.reshape(devices, per_device)[:, :, None] == jnp.arange(EXPERTS, dtype=jnp.int32)[None, None, :]).astype(jnp.int32)
    positions = jnp.sum((jnp.cumsum(picked, 1) - picked) * picked, 2).reshape(-1).astype(jnp.int32)
    column_slot = (owner_device * CAP + positions).astype(jnp.int32)
    source = jnp.full((EXPERTS, SLOTS), -1, jnp.int32).at[flat_ids, column_slot].set(serial)
    gate_slots = jnp.zeros((EXPERTS, SLOTS), jnp.bfloat16).at[flat_ids, column_slot].set(gate_sent)

    def expert_step(operands):
        source_row, weight, saved_hidden, gate_values = operands
        is_live = source_row >= 0
        fetched = cotangent[jnp.maximum(source_row, 0) // TOP]
        expert_rows = jnp.where(is_live[:, None], fetched, jnp.zeros_like(fetched))
        unscaled = jnp.dot(expert_rows, weight.T, preferred_element_type=jnp.float32)
        slot_grad = jnp.sum(unscaled * saved_hidden.astype(jnp.float32), 1)
        grad_rows = (gate_values.astype(jnp.float32)[:, None] * unscaled).astype(jnp.bfloat16)
        return grad_rows, slot_grad

    hidden_grad, slot_grads = lax.map(expert_step, (source, w_down, hidden_saved, gate_slots))

    gate_grad = slot_grads[flat_ids, column_slot].reshape(TOKENS, TOP)
    pair_grad = (gate_grad - jnp.sum(gate_prob * gate_grad, 1, keepdims=True)) / total_prob
    group_pick = (group_of[:, :, None] == jnp.arange(GROUPS, dtype=jnp.int32)[None, None, :]).astype(jnp.float32)
    seed_group = jnp.sum(group_pick * (pair_grad * pick_expert)[:, :, None], 1)
    expert_pick = (expert_ids[:, :, None] == jnp.arange(EXPERTS, dtype=jnp.int32)[None, None, :]).astype(jnp.float32)
    seed_expert = jnp.sum(expert_pick * (pair_grad * pick_group)[:, :, None], 1).reshape(TOKENS, GROUPS, EXP_GROUP)

    def backward(carried, stored_step):
        grad_g, grad_e = carried
        group_in, expert_in, group_cols, expert_cols = stored_step
        scaled_g, inner_g = adjoint_local(grad_g, group_in, target_group, group_cols)
        scaled_e, inner_e = adjoint_local(grad_e, expert_in, target_expert, expert_cols)
        next_g = adjoint_finish(scaled_g, inner_g, target_group, group_cols)
        next_e = adjoint_finish(scaled_e, inner_e, target_expert, expert_cols)
        return (next_g, next_e), None

    (grad_group, grad_expert), unused = lax.scan(backward, (seed_group, seed_expert), stored, reverse=True)
    d_group_logits = grad_group * group_aff * squashing(group_logits)
    d_expert_logits = (grad_expert * expert_aff).reshape(TOKENS, EXPERTS) * squashing(expert_logits)
    return (hidden_grad, d_group_logits, d_expert_logits)
```

```python
from functools import partial

import jax
import jax.numpy as jnp
from jax import lax
from jax.experimental import pallas as pl
from jax.experimental.pallas import tpu as pltpu
from jax.sharding import PartitionSpec as P

ITERS = 5
SOFTCAP = 4.0
LANES = 128
SUBLANES = 8
AXES = ("group", "expert")
REPLICATED_BYTES = 1 << 20


def capped(logits):
    return jnp.exp(SOFTCAP * jnp.tanh(logits / SOFTCAP))


def squashing(logits):
    bounded = jnp.tanh(logits / SOFTCAP)
    return 1.0 - bounded * bounded


def balance_level(level_in, target, column_sum):
    scaled = level_in * (target / column_sum)
    return (scaled, jnp.sum(scaled, -1, keepdims=True))


def adjoint_local(out_grad, level_in, target, column_sum):
    scaled, row_total = balance_level(level_in, target, column_sum)
    level_out = scaled / row_total
    scaled_grad = (out_grad - jnp.sum(out_grad * level_out, -1, keepdims=True)) / row_total
    return (scaled_grad, jnp.sum(scaled_grad * level_in, 0))


def adjoint_finish(scaled_grad, inner, target, column_sum):
    return target / column_sum * (scaled_grad - inner / column_sum)


def balance_step(targets, current, unused):
    target_group, target_expert = targets
    group_in, expert_in = current
    group_cols, expert_cols = lax.psum((jnp.sum(group_in, 0), jnp.sum(expert_in, 0)), AXES)
    scaled_g, rowsum_g = balance_level(group_in, target_group, group_cols)
    scaled_e, rowsum_e = balance_level(expert_in, target_expert, expert_cols)
    return (
        (scaled_g / rowsum_g, scaled_e / rowsum_e),
        (group_in, expert_in, group_cols, expert_cols),
    )


def adjoint_step(targets, carried, stored_step):
    target_group, target_expert = targets
    grad_g, grad_e = carried
    group_in, expert_in, group_cols, expert_cols = stored_step
    scaled_g, inner_g = adjoint_local(grad_g, group_in, target_group, group_cols)
    scaled_e, inner_e = adjoint_local(grad_e, expert_in, target_expert, expert_cols)
    inner_g, inner_e = lax.psum((inner_g, inner_e), AXES)
    next_g = adjoint_finish(scaled_g, inner_g, target_group, group_cols)
    next_e = adjoint_finish(scaled_e, inner_e, target_expert, expert_cols)
    return ((next_g, next_e), None)


def slots_of(expert_ids, experts, capacity):
    flat_ids = expert_ids.reshape(-1)
    picked = (flat_ids[:, None] == jnp.arange(experts, dtype=jnp.int32)[None, :]).astype(jnp.int32)
    positions = jnp.sum((jnp.cumsum(picked, 0) - picked) * picked, 1)
    return flat_ids * capacity + positions


def distributed(group_logits, expert_logits, expert_ids, cotangent, hidden_saved, w_down):
    groups = lax.axis_size("group")
    per_group = lax.axis_size("expert")
    experts = groups * per_group
    tokens_here, top_count = expert_ids.shape
    model_width = cotangent.shape[1]
    capacity = hidden_saved.shape[1] // experts
    slots = experts * capacity
    targets = (float(tokens_here * per_group), float(tokens_here * groups))
    slot_index = slots_of(expert_ids, experts, capacity)
    serial = jnp.arange(slot_index.shape[0], dtype=jnp.int32)
    source_index = jnp.zeros((slots,), jnp.int32).at[slot_index].set(serial)
    filled = jnp.zeros((slots,), jnp.int32).at[slot_index].set(1)
    fetched = jnp.take(cotangent, source_index // top_count, axis=0)
    send_rows = jnp.where(filled[:, None] > 0, fetched, jnp.zeros_like(fetched))
    expert_rows = lax.all_to_all(send_rows, AXES, split_axis=0, concat_axis=0, tiled=True)
    group_of = expert_ids // per_group
    group_aff = capped(group_logits)
    expert_aff = capped(expert_logits).reshape(tokens_here, groups, per_group)
    (group_prob, expert_prob), stored = lax.scan(
        partial(balance_step, targets), (group_aff, expert_aff), None, length=ITERS
    )
    pick_group = jnp.take_along_axis(group_prob, group_of, 1)
    pick_expert = jnp.take_along_axis(expert_prob.reshape(tokens_here, experts), expert_ids, 1)
    pair_prob = pick_group * pick_expert
    total_prob = jnp.sum(pair_prob, 1, keepdims=True)
    gate_prob = pair_prob / total_prob
    gate_sent = (
        jnp.zeros((slots,), jnp.bfloat16)
        .at[slot_index]
        .set(gate_prob.astype(jnp.bfloat16).reshape(-1))
    )
    got_gates = lax.all_to_all(gate_sent, AXES, split_axis=0, concat_axis=0, tiled=True)
    unscaled = lax.dot_general(
        expert_rows, w_down[0], (((1,), (1,)), ((), ())), preferred_element_type=jnp.float32
    )
    slot_grad = jnp.sum(unscaled * hidden_saved[0].astype(jnp.float32), 1)
    grad_rows = (got_gates.reshape(-1, 1).astype(jnp.float32) * unscaled).astype(jnp.bfloat16)
    answers = lax.all_to_all(slot_grad, AXES, split_axis=0, concat_axis=0, tiled=True)
    gate_grad = answers[slot_index].reshape(tokens_here, top_count)
    pair_grad = (gate_grad - jnp.sum(gate_prob * gate_grad, 1, keepdims=True)) / total_prob
    group_pick = (
        group_of[:, :, None] == jnp.arange(groups, dtype=jnp.int32)[None, None, :]
    ).astype(jnp.float32)
    seed_group = jnp.sum(group_pick * (pair_grad * pick_expert)[:, :, None], 1)
    expert_pick = (
        expert_ids[:, :, None] == jnp.arange(experts, dtype=jnp.int32)[None, None, :]
    ).astype(jnp.float32)
    seed_expert = jnp.sum(expert_pick * (pair_grad * pick_group)[:, :, None], 1).reshape(
        tokens_here, groups, per_group
    )
    (grad_group, grad_expert), unused = lax.scan(
        partial(adjoint_step, targets), (seed_group, seed_expert), stored, reverse=True
    )
    d_group_logits = grad_group * group_aff * squashing(group_logits)
    d_expert_logits = (grad_expert * expert_aff).reshape(tokens_here, experts) * squashing(
        expert_logits
    )
    return (grad_rows[None], d_group_logits, d_expert_logits)


def pack_kernel(ids_ref, rows_ref, out_ref, place_ref, *, experts, capacity):
    tokens, top_count = ids_ref.shape
    slots = experts * capacity

    @pl.when(pl.program_id(0) == 0)
    def _():
        ids = ids_ref[...]
        columns = lax.broadcasted_iota(jnp.int32, (tokens, LANES), 1)
        chosen = [ids[:, k : k + 1] == columns for k in range(top_count)]
        picked = sum(c.astype(jnp.float32) for c in chosen)
        row = lax.broadcasted_iota(jnp.int32, (tokens, tokens), 0)
        column = lax.broadcasted_iota(jnp.int32, (tokens, tokens), 1)
        earlier = (column < row).astype(jnp.bfloat16)
        before = jnp.dot(
            earlier, picked.astype(jnp.bfloat16), preferred_element_type=jnp.float32
        )
        slot_at = lax.broadcasted_iota(jnp.int32, (tokens, slots), 1)
        place = jnp.zeros((tokens, slots), jnp.float32)
        for k in range(top_count):
            position = jnp.sum(jnp.where(chosen[k], before, 0.0), 1, keepdims=True)
            slot = ids[:, k : k + 1] * capacity + position.astype(jnp.int32)
            place = place + (slot == slot_at).astype(jnp.float32)
        place_ref[...] = place.astype(jnp.bfloat16)

    out_ref[...] = lax.dot_general(
        place_ref[...],
        rows_ref[...],
        (((0,), (0,)), ((), ())),
        preferred_element_type=jnp.float32,
    ).astype(out_ref.dtype)


def pack_rows(expert_ids, cotangent, experts, capacity):
    tokens, width = cotangent.shape
    slots = experts * capacity
    block = 512 if width % 512 == 0 else width
    return pl.pallas_call(
        partial(pack_kernel, experts=experts, capacity=capacity),
        out_shape=jax.ShapeDtypeStruct((slots, width), cotangent.dtype),
        grid=(width // block,),
        in_specs=[
            pl.BlockSpec(expert_ids.shape, lambda i: (0, 0)),
            pl.BlockSpec((tokens, block), lambda i: (0, i)),
        ],
        out_specs=pl.BlockSpec((slots, block), lambda i: (0, i)),
        scratch_shapes=[pltpu.VMEM((tokens, slots), jnp.bfloat16)],
        cost_estimate=pl.CostEstimate(
            flops=2 * tokens * slots * width,
            bytes_accessed=2 * width * (tokens + slots),
            transcendentals=0,
        ),
        name="pack_rows",
    )(expert_ids, cotangent)


def tile_rows(g):
    return pl.ds(SUBLANES * (g + 1), SUBLANES)


def forward_kernel(
    me_ref, all_ref, level_ref, inverse_ref, column_ref, seed_q_ref, seed_p_ref, where_ref,
    gate_ref, own_ref, dense_ref, before_ref, *, groups, top_count, capacity, targets
):
    devices = all_ref.shape[0]
    tiles = groups + 1
    tile = (SUBLANES, LANES)
    row_id = lax.broadcasted_iota(jnp.int32, tile, 0)
    zero = jnp.zeros(tile, jnp.float32)

    def totals(sums):
        out = []
        for i in range(tiles):
            column = jnp.sum(sums[i], 1, keepdims=True) + zero
            out.append(jnp.where(row_id < groups, column, 1.0) if i == 0 else column)
        return out

    def start(d, sums):
        new = []
        for i in range(tiles):
            rows = pl.ds(SUBLANES * i, SUBLANES)
            level = capped(all_ref[d, rows, :])
            if i == 0:
                level = jnp.where(row_id < groups, level, 0.0)
            level_ref[0, d, rows, :] = level
            new.append(sums[i] + level)
        named = [all_ref[d, groups + k : groups + k + 1, :].astype(jnp.int32) for k in range(top_count)]
        for g in range(groups):
            expert = row_id + g * SUBLANES
            hit = named[0] == expert
            for k in range(1, top_count):
                hit = hit | (named[k] == expert)
            dense_ref[d, pl.ds(SUBLANES * g, SUBLANES), :] = hit.astype(jnp.float32)
        return tuple(new)

    sums = lax.fori_loop(0, devices, start, (zero,) * tiles, unroll=2)

    for k in range(ITERS):
        columns = totals(sums)
        factors = []
        for i in range(tiles):
            column_ref[k, pl.ds(SUBLANES * i, SUBLANES), :] = columns[i]
            factors.append(targets[min(i, 1)] / columns[i])

        def step(d, sums, k=k, factors=factors):
            new = []
            for i in range(tiles):
                rows = pl.ds(SUBLANES * i, SUBLANES)
                scaled = level_ref[k, d, rows, :] * factors[i]
                inverse = 1.0 / jnp.sum(scaled, 0, keepdims=True)
                inverse_ref[k, d, pl.ds(i, 1), :] = inverse
                level = scaled * inverse
                level_ref[k + 1, d, rows, :] = level
                new.append(sums[i] + level)
            return tuple(new)

        sums = lax.fori_loop(0, devices, step, (zero,) * tiles, unroll=4)

    experts = groups * SUBLANES
    earlier = (
        lax.broadcasted_iota(jnp.int32, (LANES, LANES), 0)
        < lax.broadcasted_iota(jnp.int32, (LANES, LANES), 1)
    ).astype(jnp.bfloat16)
    before_ref[...] = jnp.dot(
        dense_ref[...].reshape(devices * experts, LANES).astype(jnp.bfloat16),
        earlier,
        preferred_element_type=jnp.float32,
    ).reshape(devices, experts, LANES)

    per_block = LANES // capacity
    slot_id = lax.broadcasted_iota(jnp.int32, (capacity, LANES), 0)
    me = me_ref[0]

    def finish(d, unused):
        picks = []
        total = jnp.zeros((1, LANES), jnp.float32)
        for g in range(groups):
            hit = dense_ref[d, pl.ds(SUBLANES * g, SUBLANES), :]
            pick_p = hit * level_ref[ITERS, d, g : g + 1, :]
            pick_q = hit * level_ref[ITERS, d, tile_rows(g), :]
            pair = pick_p * pick_q
            total = total + jnp.sum(pair, 0, keepdims=True)
            picks.append((pick_p, pick_q, pair))
        hit_me = dense_ref[d, pl.ds(me, 1), :]
        before_me = before_ref[d, pl.ds(me, 1), :].astype(jnp.int32)
        for g in range(groups):
            rows = pl.ds(SUBLANES * g, SUBLANES)
            pick_p, pick_q, pair = picks[g]
            seed_q_ref[d, rows, :] = pick_p / total
            seed_p_ref[d, rows, :] = pick_q / total
            dense_ref[d, rows, :] = pair / total
            position = before_ref[d, rows, :].astype(jnp.int32)
            lane = lax.rem(d, per_block) * capacity + position
            where_ref[d, rows, :] = jnp.minimum(lane, LANES - 1)
        gate_me = dense_ref[d, pl.ds(me, 1), :].astype(jnp.bfloat16).astype(jnp.float32)
        taken = jnp.where((before_me == slot_id) & (hit_me > 0.0), gate_me, 0.0)
        gate_ref[pl.ds(d * capacity, capacity), :] = jnp.sum(taken, 1, keepdims=True) + jnp.zeros(
            (capacity, LANES), jnp.float32
        )
        return unused

    lax.fori_loop(0, devices, finish, 0)
    for i in range(tiles):
        rows = pl.ds(SUBLANES * i, SUBLANES)
        own_ref[rows, :] = level_ref[0, me, rows, :] * squashing(all_ref[me, rows, :])


def forward(me, everyone, groups, top_count, capacity, targets):
    devices, rows, lanes = everyone.shape
    experts = groups * SUBLANES
    f32 = jnp.float32
    shapes = [
        ((ITERS + 1, devices, rows, lanes), f32),
        ((ITERS, devices, SUBLANES, lanes), f32),
        ((ITERS, rows, lanes), f32),
        ((devices, experts, lanes), f32),
        ((devices, experts, lanes), f32),
        ((devices, experts, lanes), jnp.int32),
        ((devices * capacity, lanes), f32),
        ((rows, lanes), f32),
    ]
    vmem = pl.BlockSpec(memory_space=pltpu.VMEM)
    return pl.pallas_call(
        partial(
            forward_kernel, groups=groups, top_count=top_count, capacity=capacity, targets=targets
        ),
        out_shape=[jax.ShapeDtypeStruct(s, d) for s, d in shapes],
        in_specs=[pl.BlockSpec(memory_space=pltpu.SMEM), vmem],
        out_specs=[vmem] * len(shapes),
        scratch_shapes=[
            pltpu.VMEM((devices, experts, lanes), f32),
            pltpu.VMEM((devices, experts, lanes), f32),
        ],
        cost_estimate=pl.CostEstimate(flops=10_000_000, bytes_accessed=8_000_000, transcendentals=0),
        name="forward",
    )(me, everyone)


def product_kernel(rows_ref, weight_ref, saved_ref, gate_ref, grad_ref, slot_ref, sum_ref):
    unscaled = lax.dot_general(
        rows_ref[...],
        weight_ref[...],
        (((1,), (1,)), ((), ())),
        preferred_element_type=jnp.float32,
    )
    grad_ref[...] = (gate_ref[:, :1] * unscaled).astype(grad_ref.dtype)
    partial_sums = unscaled * saved_ref[...].astype(jnp.float32)
    folded = partial_sums[:, :LANES]
    for j in range(1, partial_sums.shape[1] // LANES):
        folded = folded + partial_sums[:, j * LANES : (j + 1) * LANES]
    first = pl.program_id(0) == 0

    @pl.when(first)
    def _():
        sum_ref[...] = folded

    @pl.when(jnp.logical_not(first))
    def _():
        sum_ref[...] = sum_ref[...] + folded

    @pl.when(pl.program_id(0) == pl.num_programs(0) - 1)
    def _():
        for j in range(slot_ref.shape[1] // LANES):
            turned = sum_ref[j * LANES : (j + 1) * LANES, :].T
            slot_ref[:, j * LANES : (j + 1) * LANES] = jnp.sum(turned, 0, keepdims=True)


def product(rows, weight, saved, gates):
    slots, width = rows.shape
    hidden = weight.shape[0]
    block = 256 if hidden % 256 == 0 else hidden
    return pl.pallas_call(
        product_kernel,
        out_shape=[
            jax.ShapeDtypeStruct((slots, hidden), jnp.bfloat16),
            jax.ShapeDtypeStruct((1, slots), jnp.float32),
        ],
        grid=(hidden // block,),
        in_specs=[
            pl.BlockSpec((slots, width), lambda i: (0, 0)),
            pl.BlockSpec((block, width), lambda i: (i, 0)),
            pl.BlockSpec((slots, block), lambda i: (0, i)),
            pl.BlockSpec((slots, LANES), lambda i: (0, 0)),
        ],
        out_specs=[
            pl.BlockSpec((slots, block), lambda i: (0, i)),
            pl.BlockSpec((1, slots), lambda i: (0, 0)),
        ],
        scratch_shapes=[pltpu.VMEM((slots, LANES), jnp.float32)],
        cost_estimate=pl.CostEstimate(
            flops=2 * slots * width * hidden,
            bytes_accessed=2 * (slots * width + hidden * width + 2 * slots * hidden),
            transcendentals=0,
        ),
        name="product",
    )(rows, weight, saved, gates)


def adjoint_kernel(
    me_ref, slot_ref, level_ref, inverse_ref, column_ref, seed_q_ref, seed_p_ref, where_ref,
    own_ref, group_ref, expert_ref, carry_ref, *, groups, capacity, targets
):
    devices = level_ref.shape[1]
    tiles = groups + 1
    tile = (SUBLANES, LANES)
    row_id = lax.broadcasted_iota(jnp.int32, tile, 0)
    zero = jnp.zeros(tile, jnp.float32)
    per_block = LANES // capacity

    def seeds(d):
        block = pl.ds(pl.multiple_of(lax.div(d, per_block) * LANES, LANES), LANES)
        grads = []
        mixed = jnp.zeros((1, LANES), jnp.float32)
        for g in range(groups):
            rows = pl.ds(SUBLANES * g, SUBLANES)
            grad = jnp.take_along_axis(slot_ref[rows, block], where_ref[d, rows, :], axis=1)
            gate = seed_q_ref[d, rows, :] * level_ref[ITERS, d, tile_rows(g), :]
            mixed = mixed + jnp.sum(gate * grad, 0, keepdims=True)
            grads.append(grad)
        out = [zero]
        for g in range(groups):
            rows = pl.ds(SUBLANES * g, SUBLANES)
            grad = grads[g] - mixed
            out.append(seed_q_ref[d, rows, :] * grad)
            level = jnp.sum(seed_p_ref[d, rows, :] * grad, 0, keepdims=True)
            out[0] = jnp.where(row_id == g, level, out[0])
        return out

    def factors_of(k):
        out = []
        for i in range(tiles):
            column = column_ref[k, pl.ds(SUBLANES * i, SUBLANES), :]
            factor = targets[min(i, 1)] / column
            if i == 0:
                factor = jnp.where(row_id < groups, factor, 0.0)
            out.append((factor, column))
        return out

    inner = None
    for k in reversed(range(ITERS)):
        if inner is not None:
            scale = []
            for i, (factor, column) in enumerate(factors_of(k + 1)):
                total = jnp.sum(inner[i], 1, keepdims=True) + zero
                scale.append((factor, total / column))

        def step(d, sums, k=k):
            if k == ITERS - 1:
                grads = seeds(d)
            else:
                grads = [
                    scale[i][0] * (carry_ref[d, pl.ds(SUBLANES * i, SUBLANES), :] - scale[i][1])
                    for i in range(tiles)
                ]
            new = []
            for i in range(tiles):
                rows = pl.ds(SUBLANES * i, SUBLANES)
                along = jnp.sum(grads[i] * level_ref[k + 1, d, rows, :], 0, keepdims=True)
                scaled = (grads[i] - along) * inverse_ref[k, d, pl.ds(i, 1), :]
                carry_ref[d, rows, :] = scaled
                new.append(sums[i] + scaled * level_ref[k, d, rows, :])
            return tuple(new)

        inner = lax.fori_loop(0, devices, step, (zero,) * tiles, unroll=4)

    me = me_ref[0]
    for i, (factor, column) in enumerate(factors_of(0)):
        rows = pl.ds(SUBLANES * i, SUBLANES)
        total = jnp.sum(inner[i], 1, keepdims=True) + zero
        carry_ref[0, rows, :] = (
            factor * (carry_ref[me, rows, :] - total / column) * own_ref[rows, :]
        )
    turned = carry_ref[0, :, :].T
    group_ref[...] = turned[:, :groups]
    expert_ref[...] = turned[:, SUBLANES:]


def adjoint(me, slot_grads, saved, own, groups, capacity, targets):
    level = saved[0]
    rows, lanes = level.shape[2:]
    vmem = pl.BlockSpec(memory_space=pltpu.VMEM)
    return pl.pallas_call(
        partial(adjoint_kernel, groups=groups, capacity=capacity, targets=targets),
        out_shape=[
            jax.ShapeDtypeStruct((lanes, groups), jnp.float32),
            jax.ShapeDtypeStruct((lanes, groups * SUBLANES), jnp.float32),
        ],
        in_specs=[pl.BlockSpec(memory_space=pltpu.SMEM)] + [vmem] * (2 + len(saved)),
        out_specs=[vmem, vmem],
        scratch_shapes=[pltpu.VMEM(level.shape[1:], jnp.float32)],
        cost_estimate=pl.CostEstimate(flops=10_000_000, bytes_accessed=8_000_000, transcendentals=0),
        name="adjoint",
    )(me, slot_grads, *saved, own)


def spread(block):
    copies = jnp.broadcast_to(block[None], (lax.axis_size(AXES),) + block.shape)
    return lax.all_to_all(copies, AXES, split_axis=0, concat_axis=0)


def replicated(group_logits, expert_logits, expert_ids, cotangent, hidden_saved, w_down):
    groups = lax.axis_size("group")
    per_group = lax.axis_size("expert")
    experts = groups * per_group
    tokens_here, top_count = expert_ids.shape
    capacity = hidden_saved.shape[1] // experts
    targets = (float(tokens_here * per_group), float(tokens_here * groups))
    me = (lax.axis_index("group") * per_group + lax.axis_index("expert")).reshape(1)
    spare = SUBLANES - groups - top_count
    mine = jnp.concatenate(
        [
            group_logits,
            expert_ids.astype(jnp.float32),
            jnp.zeros((tokens_here, spare), jnp.float32),
            expert_logits,
        ],
        1,
    ).T
    everyone = spread(mine)
    send_rows = pack_rows(expert_ids, cotangent, experts, capacity)
    expert_rows = lax.all_to_all(send_rows, AXES, split_axis=0, concat_axis=0, tiled=True)
    *saved, gates, own = forward(me, everyone, groups, top_count, capacity, targets)
    hidden_grad, slot_grad = product(expert_rows, w_down[0], hidden_saved[0], gates)
    slot_grads = spread(slot_grad).reshape(experts, -1)
    d_group, d_expert = adjoint(me, slot_grads, saved, own, groups, capacity, targets)
    return (hidden_grad[None], d_group, d_expert)


def per_device(group_logits, expert_logits, expert_ids, cotangent, hidden_saved, w_down):
    groups = lax.axis_size("group")
    per_group = lax.axis_size("expert")
    tokens_here, top_count = expert_ids.shape
    capacity = hidden_saved.shape[1] // (groups * per_group)
    everyone_bytes = 4 * tokens_here * (groups * per_group) * (groups * per_group + SUBLANES)
    fits = (
        tokens_here == LANES
        and per_group == SUBLANES
        and groups + top_count <= SUBLANES
        and LANES % capacity == 0
        and capacity % SUBLANES == 0
        and everyone_bytes <= REPLICATED_BYTES
    )
    form = replicated if fits else distributed
    return form(group_logits, expert_logits, expert_ids, cotangent, hidden_saved, w_down)


def solution(mesh):
    rows = P(AXES, None)
    blocks = P(AXES, None, None)
    return jax.shard_map(
        per_device,
        mesh=mesh,
        in_specs=(rows, rows, rows, rows, blocks, blocks),
        out_specs=(blocks, rows, rows),
        check_vma=False,
    )
```

```python
from functools import partial

import jax
import jax.numpy as jnp
from jax import lax
from jax.experimental import pallas as pl
from jax.experimental.pallas import tpu as pltpu
from jax.sharding import Mesh
from jax.sharding import PartitionSpec as P

ITERS = 5
SOFTCAP = 4.0
LANES = 128
SUBLANES = 8
AXES = ("half", "plane", "expert")
NEAR = ("plane", "expert")
REPLICATED_BYTES = 1 << 20


def capped(logits):
    return jnp.exp(SOFTCAP * jnp.tanh(logits / SOFTCAP))


def squashing(logits):
    bounded = jnp.tanh(logits / SOFTCAP)
    return 1.0 - bounded * bounded


def balance_level(level_in, target, column_sum):
    scaled = level_in * (target / column_sum)
    return (scaled, jnp.sum(scaled, -1, keepdims=True))


def adjoint_local(out_grad, level_in, target, column_sum):
    scaled, row_total = balance_level(level_in, target, column_sum)
    level_out = scaled / row_total
    scaled_grad = (out_grad - jnp.sum(out_grad * level_out, -1, keepdims=True)) / row_total
    return (scaled_grad, jnp.sum(scaled_grad * level_in, 0))


def adjoint_finish(scaled_grad, inner, target, column_sum):
    return target / column_sum * (scaled_grad - inner / column_sum)


def balance_step(targets, current, unused):
    target_group, target_expert = targets
    group_in, expert_in = current
    group_cols, expert_cols = lax.psum((jnp.sum(group_in, 0), jnp.sum(expert_in, 0)), AXES)
    scaled_g, rowsum_g = balance_level(group_in, target_group, group_cols)
    scaled_e, rowsum_e = balance_level(expert_in, target_expert, expert_cols)
    return (
        (scaled_g / rowsum_g, scaled_e / rowsum_e),
        (group_in, expert_in, group_cols, expert_cols),
    )


def adjoint_step(targets, carried, stored_step):
    target_group, target_expert = targets
    grad_g, grad_e = carried
    group_in, expert_in, group_cols, expert_cols = stored_step
    scaled_g, inner_g = adjoint_local(grad_g, group_in, target_group, group_cols)
    scaled_e, inner_e = adjoint_local(grad_e, expert_in, target_expert, expert_cols)
    inner_g, inner_e = lax.psum((inner_g, inner_e), AXES)
    next_g = adjoint_finish(scaled_g, inner_g, target_group, group_cols)
    next_e = adjoint_finish(scaled_e, inner_e, target_expert, expert_cols)
    return ((next_g, next_e), None)


def slots_of(expert_ids, experts, capacity):
    flat_ids = expert_ids.reshape(-1)
    picked = (flat_ids[:, None] == jnp.arange(experts, dtype=jnp.int32)[None, :]).astype(jnp.int32)
    positions = jnp.sum((jnp.cumsum(picked, 0) - picked) * picked, 1)
    return flat_ids * capacity + positions


def distributed(group_logits, expert_logits, expert_ids, cotangent, hidden_saved, w_down):
    groups = lax.axis_size(("half", "plane"))
    per_group = lax.axis_size("expert")
    experts = groups * per_group
    tokens_here, top_count = expert_ids.shape
    capacity = hidden_saved.shape[1] // experts
    slots = experts * capacity
    targets = (float(tokens_here * per_group), float(tokens_here * groups))
    slot_index = slots_of(expert_ids, experts, capacity)
    serial = jnp.arange(slot_index.shape[0], dtype=jnp.int32)
    source_index = jnp.zeros((slots,), jnp.int32).at[slot_index].set(serial)
    filled = jnp.zeros((slots,), jnp.int32).at[slot_index].set(1)
    fetched = jnp.take(cotangent, source_index // top_count, axis=0)
    send_rows = jnp.where(filled[:, None] > 0, fetched, jnp.zeros_like(fetched))
    expert_rows = lax.all_to_all(send_rows, AXES, split_axis=0, concat_axis=0, tiled=True)
    group_of = expert_ids // per_group
    group_aff = capped(group_logits)
    expert_aff = capped(expert_logits).reshape(tokens_here, groups, per_group)
    (group_prob, expert_prob), stored = lax.scan(
        partial(balance_step, targets), (group_aff, expert_aff), None, length=ITERS
    )
    pick_group = jnp.take_along_axis(group_prob, group_of, 1)
    pick_expert = jnp.take_along_axis(expert_prob.reshape(tokens_here, experts), expert_ids, 1)
    pair_prob = pick_group * pick_expert
    total_prob = jnp.sum(pair_prob, 1, keepdims=True)
    gate_prob = pair_prob / total_prob
    gate_sent = (
        jnp.zeros((slots,), jnp.bfloat16)
        .at[slot_index]
        .set(gate_prob.astype(jnp.bfloat16).reshape(-1))
    )
    got_gates = lax.all_to_all(gate_sent, AXES, split_axis=0, concat_axis=0, tiled=True)
    unscaled = lax.dot_general(
        expert_rows, w_down[0], (((1,), (1,)), ((), ())), preferred_element_type=jnp.float32
    )
    slot_grad = jnp.sum(unscaled * hidden_saved[0].astype(jnp.float32), 1)
    grad_rows = (got_gates.reshape(-1, 1).astype(jnp.float32) * unscaled).astype(jnp.bfloat16)
    answers = lax.all_to_all(slot_grad, AXES, split_axis=0, concat_axis=0, tiled=True)
    gate_grad = answers[slot_index].reshape(tokens_here, top_count)
    pair_grad = (gate_grad - jnp.sum(gate_prob * gate_grad, 1, keepdims=True)) / total_prob
    group_pick = (
        group_of[:, :, None] == jnp.arange(groups, dtype=jnp.int32)[None, None, :]
    ).astype(jnp.float32)
    seed_group = jnp.sum(group_pick * (pair_grad * pick_expert)[:, :, None], 1)
    expert_pick = (
        expert_ids[:, :, None] == jnp.arange(experts, dtype=jnp.int32)[None, None, :]
    ).astype(jnp.float32)
    seed_expert = jnp.sum(expert_pick * (pair_grad * pick_group)[:, :, None], 1).reshape(
        tokens_here, groups, per_group
    )
    (grad_group, grad_expert), unused = lax.scan(
        partial(adjoint_step, targets), (seed_group, seed_expert), stored, reverse=True
    )
    d_group_logits = grad_group * group_aff * squashing(group_logits)
    d_expert_logits = (grad_expert * expert_aff).reshape(tokens_here, experts) * squashing(
        expert_logits
    )
    return (grad_rows[None], d_group_logits, d_expert_logits)


def place_rows(ids, first, experts, capacity):
    lanes = ids[0].shape[1]
    expert = lax.broadcasted_iota(jnp.int32, (experts, lanes), 0)
    hits = [(row - first) == expert for row in ids]
    picked = sum(hit.astype(jnp.float32) for hit in hits)
    earlier = (
        lax.broadcasted_iota(jnp.int32, (lanes, lanes), 0)
        < lax.broadcasted_iota(jnp.int32, (lanes, lanes), 1)
    ).astype(jnp.bfloat16)
    before = jnp.dot(picked.astype(jnp.bfloat16), earlier, preferred_element_type=jnp.float32)
    slot_of = (expert * capacity).astype(jnp.float32) + before
    slot_at = lax.broadcasted_iota(jnp.int32, (experts * capacity, lanes), 0)
    place = jnp.zeros((experts * capacity, lanes), jnp.float32)
    for row, hit in zip(ids, hits):
        slot = jnp.sum(jnp.where(hit, slot_of, 0.0), 0, keepdims=True).astype(jnp.int32)
        here = (row >= first) & (row < first + experts)
        slot = jnp.where(here, slot, -1)
        place = place + (slot == slot_at).astype(jnp.float32)
    return place.astype(jnp.bfloat16)


def mine_kernel(group_ref, ids_ref, expert_ref, out_ref):
    groups, top_count = group_ref.shape[0], ids_ref.shape[0]
    out_ref[:SUBLANES, :] = jnp.zeros((SUBLANES, out_ref.shape[1]), jnp.float32)
    out_ref[:groups, :] = group_ref[...]
    out_ref[groups : groups + top_count, :] = ids_ref[...].astype(jnp.float32)
    out_ref[SUBLANES:, :] = expert_ref[...]


def pack_kernel(small_ref, rows_ref, *refs, near, capacity, first_id, top_count):
    out_ref, place_ref = refs[-2:]

    @pl.when(pl.program_id(0) == 0)
    def _():
        ids = [
            small_ref[first_id + k : first_id + k + 1, :].astype(jnp.int32)
            for k in range(top_count)
        ]
        place_ref[...] = place_rows(ids, lax.axis_index("half") * near, near, capacity)

    out_ref[...] = jnp.dot(
        place_ref[...], rows_ref[...], preferred_element_type=jnp.float32
    ).astype(out_ref.dtype)


def pack_rows(small, rows, near, capacity, first_id, top_count, after):
    tokens, width = rows.shape
    slots = near * capacity
    block = max(n for n in range(LANES, 8 * LANES, LANES) if width % n == 0)
    return pl.pallas_call(
        partial(
            pack_kernel, near=near, capacity=capacity, first_id=first_id, top_count=top_count
        ),
        out_shape=jax.ShapeDtypeStruct((slots, width), rows.dtype),
        grid=(width // block,),
        in_specs=[
            pl.BlockSpec(small.shape, lambda i: (0, 0)),
            pl.BlockSpec((tokens, block), lambda i: (0, i)),
        ]
        + [pl.BlockSpec(memory_space=pl.ANY)] * len(after),
        out_specs=pl.BlockSpec((slots, block), lambda i: (0, i)),
        scratch_shapes=[pltpu.VMEM((slots, tokens), rows.dtype)],
        cost_estimate=pl.CostEstimate(
            flops=2 * tokens * slots * width,
            bytes_accessed=2 * width * (tokens + slots),
            transcendentals=0,
        ),
        name="pack_rows",
    )(small, rows, *after)


def tile_rows(g):
    return pl.ds(SUBLANES * (g + 1), SUBLANES)


def forward_kernel(
    all_ref, *refs, groups, top_count, capacity, targets, extra
):
    (level_ref, inverse_ref, column_ref, seed_q_ref, seed_p_ref, where_ref,
     gate_ref, own_ref, dense_ref, before_ref) = refs[extra:]
    near, halves = all_ref.shape[:2]
    devices = near * halves
    tiles = groups + 1
    half = lax.axis_index("half")
    inner = lax.axis_index("plane") * lax.axis_size("expert") + lax.axis_index("expert")

    def block(d):
        return lax.rem(d, near), (lax.div(d, near) != half).astype(jnp.int32)

    tile = (SUBLANES, LANES)
    row_id = lax.broadcasted_iota(jnp.int32, tile, 0)
    zero = jnp.zeros(tile, jnp.float32)

    def totals(sums):
        out = []
        for i in range(tiles):
            column = jnp.sum(sums[i], 1, keepdims=True) + zero
            out.append(jnp.where(row_id < groups, column, 1.0) if i == 0 else column)
        return out

    def start(d, sums):
        new = []
        member, shifted = block(d)
        for i in range(tiles):
            rows = pl.ds(SUBLANES * i, SUBLANES)
            level = capped(all_ref[member, shifted, rows, :])
            if i == 0:
                level = jnp.where(row_id < groups, level, 0.0)
            level_ref[0, d, rows, :] = level
            new.append(sums[i] + level)
        named = [
            all_ref[member, shifted, groups + k : groups + k + 1, :].astype(jnp.int32)
            for k in range(top_count)
        ]
        for g in range(groups):
            expert = row_id + g * SUBLANES
            hit = named[0] == expert
            for k in range(1, top_count):
                hit = hit | (named[k] == expert)
            dense_ref[d, pl.ds(SUBLANES * g, SUBLANES), :] = hit.astype(jnp.float32)
        return tuple(new)

    sums = lax.fori_loop(0, devices, start, (zero,) * tiles, unroll=2)

    for k in range(ITERS):
        columns = totals(sums)
        factors = []
        for i in range(tiles):
            column_ref[k, pl.ds(SUBLANES * i, SUBLANES), :] = columns[i]
            factors.append(targets[min(i, 1)] / columns[i])

        def step(d, sums, k=k, factors=factors):
            new = []
            for i in range(tiles):
                rows = pl.ds(SUBLANES * i, SUBLANES)
                scaled = level_ref[k, d, rows, :] * factors[i]
                inverse = 1.0 / jnp.sum(scaled, 0, keepdims=True)
                inverse_ref[k, d, pl.ds(i, 1), :] = inverse
                level = scaled * inverse
                level_ref[k + 1, d, rows, :] = level
                new.append(sums[i] + level)
            return tuple(new)

        sums = lax.fori_loop(0, devices, step, (zero,) * tiles, unroll=4)

    experts = groups * SUBLANES
    earlier = (
        lax.broadcasted_iota(jnp.int32, (LANES, LANES), 0)
        < lax.broadcasted_iota(jnp.int32, (LANES, LANES), 1)
    ).astype(jnp.bfloat16)
    before_ref[...] = jnp.dot(
        dense_ref[...].reshape(devices * experts, LANES).astype(jnp.bfloat16),
        earlier,
        preferred_element_type=jnp.float32,
    ).reshape(devices, experts, LANES)

    per_block = LANES // capacity
    slot_id = lax.broadcasted_iota(jnp.int32, (capacity, LANES), 0)
    me = half * near + inner

    def finish(d, unused):
        picks = []
        total = jnp.zeros((1, LANES), jnp.float32)
        for g in range(groups):
            hit = dense_ref[d, pl.ds(SUBLANES * g, SUBLANES), :]
            pick_p = hit * level_ref[ITERS, d, g : g + 1, :]
            pick_q = hit * level_ref[ITERS, d, tile_rows(g), :]
            pair = pick_p * pick_q
            total = total + jnp.sum(pair, 0, keepdims=True)
            picks.append((pick_p, pick_q, pair))
        hit_me = dense_ref[d, pl.ds(me, 1), :]
        before_me = before_ref[d, pl.ds(me, 1), :].astype(jnp.int32)
        for g in range(groups):
            rows = pl.ds(SUBLANES * g, SUBLANES)
            pick_p, pick_q, pair = picks[g]
            seed_q_ref[d, rows, :] = pick_p / total
            seed_p_ref[d, rows, :] = pick_q / total
            dense_ref[d, rows, :] = pair / total
            position = before_ref[d, rows, :].astype(jnp.int32)
            lane = lax.rem(d, per_block) * capacity + position
            where_ref[d, rows, :] = jnp.minimum(lane, LANES - 1)
        gate_me = dense_ref[d, pl.ds(me, 1), :].astype(jnp.bfloat16).astype(jnp.float32)
        taken = jnp.where((before_me == slot_id) & (hit_me > 0.0), gate_me, 0.0)
        gate_ref[pl.ds(d * capacity, capacity), :] = jnp.sum(taken, 1, keepdims=True) + jnp.zeros(
            (capacity, LANES), jnp.float32
        )
        return unused

    lax.fori_loop(0, devices, finish, 0)
    for i in range(tiles):
        rows = pl.ds(SUBLANES * i, SUBLANES)
        logits = all_ref[inner, 0, rows, :]
        own_ref[rows, :] = level_ref[0, me, rows, :] * squashing(logits)


def forward(everyone, groups, top_count, capacity, targets, after):
    near, halves, rows, lanes = everyone.shape
    devices = near * halves
    experts = groups * SUBLANES
    f32 = jnp.float32
    shapes = [
        ((ITERS + 1, devices, rows, lanes), f32),
        ((ITERS, devices, SUBLANES, lanes), f32),
        ((ITERS, rows, lanes), f32),
        ((devices, experts, lanes), f32),
        ((devices, experts, lanes), f32),
        ((devices, experts, lanes), jnp.int32),
        ((devices * capacity, lanes), f32),
        ((rows, lanes), f32),
    ]
    vmem = pl.BlockSpec(memory_space=pltpu.VMEM)
    return pl.pallas_call(
        partial(
            forward_kernel,
            groups=groups,
            top_count=top_count,
            capacity=capacity,
            targets=targets,
            extra=len(after),
        ),
        out_shape=[jax.ShapeDtypeStruct(s, d) for s, d in shapes],
        in_specs=[vmem] + [pl.BlockSpec(memory_space=pl.ANY)] * len(after),
        out_specs=[vmem] * len(shapes),
        scratch_shapes=[
            pltpu.VMEM((devices, experts, lanes), f32),
            pltpu.VMEM((devices, experts, lanes), f32),
        ],
        cost_estimate=pl.CostEstimate(flops=10_000_000, bytes_accessed=8_000_000, transcendentals=0),
        name="forward",
    )(everyone, *after)


def product_kernel(table_ref, *refs, carried, last, extra):
    refs = list(refs)
    rows_ref, weight_ref = refs[:2]
    del refs[:2]
    unscaled = lax.dot_general(
        rows_ref[...],
        weight_ref[...],
        (((1,), (1,)), ((), ())),
        preferred_element_type=jnp.float32,
    )
    if carried:
        unscaled = unscaled + refs.pop(0)[...]
    if not last:
        refs[extra][...] = unscaled
        return
    saved_ref, gate_ref = refs[:2]
    grad_ref, slot_ref, sum_ref = refs[-3:]
    grad_ref[...] = (gate_ref[:, :1] * unscaled).astype(grad_ref.dtype)
    partial_sums = unscaled * saved_ref[...].astype(jnp.float32)
    folded = partial_sums[:, :LANES]
    for j in range(1, partial_sums.shape[1] // LANES):
        folded = folded + partial_sums[:, j * LANES : (j + 1) * LANES]
    first = pl.program_id(0) == 0

    @pl.when(first)
    def _():
        sum_ref[...] = folded

    @pl.when(jnp.logical_not(first))
    def _():
        sum_ref[...] = sum_ref[...] + folded

    @pl.when(pl.program_id(0) == pl.num_programs(0) - 1)
    def _():
        slot_ref[0] = jnp.sum(sum_ref[...].T, 0, keepdims=True)


def product(
    table, entry, rows, weight, saved, gates, part=0, carried=None, last=True, earlier=None, after=()
):
    slots, width = rows.shape
    hidden = weight.shape[0]
    total = saved.shape[0]
    block = 256 if hidden % 256 == 0 else hidden
    row_block = pl.BlockSpec((slots, block), lambda i, table: (table[entry], i))
    own_block = pl.BlockSpec((slots, block), lambda i, table: (0, i))
    operands = [rows, weight]
    in_specs = [
        pl.BlockSpec((slots, width), lambda i, table: (0, 0)),
        pl.BlockSpec((block, width), lambda i, table: (i, part)),
    ]
    aliases = {}
    if carried is not None:
        operands.append(carried)
        in_specs.append(own_block)
    if last:
        operands += [saved, gates]
        in_specs += [row_block, pl.BlockSpec((slots, LANES), lambda i, table: (table[entry], 0))]
        if earlier is not None:
            aliases = {len(operands) + 1 + i: i for i in range(2)}
            operands += earlier
            in_specs += [pl.BlockSpec(memory_space=pl.ANY)] * 2
        out_shape = [
            jax.ShapeDtypeStruct((total, hidden), jnp.bfloat16),
            jax.ShapeDtypeStruct((total // slots, 1, slots), jnp.float32),
        ]
        out_specs = [row_block, pl.BlockSpec((1, 1, slots), lambda i, table: (table[entry], 0, 0))]
        scratch = [pltpu.VMEM((slots, LANES), jnp.float32)]
    else:
        out_shape = jax.ShapeDtypeStruct((slots, hidden), jnp.float32)
        out_specs = own_block
        scratch = []
    operands += after
    in_specs += [pl.BlockSpec(memory_space=pl.ANY)] * len(after)
    return pl.pallas_call(
        partial(product_kernel, carried=carried is not None, last=last, extra=len(after)),
        out_shape=out_shape,
        grid_spec=pltpu.PrefetchScalarGridSpec(
            num_scalar_prefetch=1,
            grid=(hidden // block,),
            in_specs=in_specs,
            out_specs=out_specs,
            scratch_shapes=scratch,
        ),
        input_output_aliases=aliases,
        cost_estimate=pl.CostEstimate(
            flops=2 * slots * width * hidden,
            bytes_accessed=2 * (slots * width + hidden * width + 2 * slots * hidden),
            transcendentals=0,
        ),
        name="product",
    )(table, *operands)


def adjoint_kernel(
    slot_ref, level_ref, inverse_ref, column_ref, seed_q_ref, seed_p_ref, where_ref,
    own_ref, group_ref, expert_ref, carry_ref, *, groups, capacity, targets
):
    devices = level_ref.shape[1]
    tiles = groups + 1
    tile = (SUBLANES, LANES)
    row_id = lax.broadcasted_iota(jnp.int32, tile, 0)
    zero = jnp.zeros(tile, jnp.float32)
    per_block = LANES // capacity

    def seeds(d):
        block = pl.ds(pl.multiple_of(lax.div(d, per_block) * LANES, LANES), LANES)
        grads = []
        mixed = jnp.zeros((1, LANES), jnp.float32)
        for g in range(groups):
            rows = pl.ds(SUBLANES * g, SUBLANES)
            grad = jnp.take_along_axis(slot_ref[rows, block], where_ref[d, rows, :], axis=1)
            gate = seed_q_ref[d, rows, :] * level_ref[ITERS, d, tile_rows(g), :]
            mixed = mixed + jnp.sum(gate * grad, 0, keepdims=True)
            grads.append(grad)
        out = [zero]
        for g in range(groups):
            rows = pl.ds(SUBLANES * g, SUBLANES)
            grad = grads[g] - mixed
            out.append(seed_q_ref[d, rows, :] * grad)
            level = jnp.sum(seed_p_ref[d, rows, :] * grad, 0, keepdims=True)
            out[0] = jnp.where(row_id == g, level, out[0])
        return out

    def factors_of(k):
        out = []
        for i in range(tiles):
            column = column_ref[k, pl.ds(SUBLANES * i, SUBLANES), :]
            factor = targets[min(i, 1)] / column
            if i == 0:
                factor = jnp.where(row_id < groups, factor, 0.0)
            out.append((factor, column))
        return out

    inner = None
    for k in reversed(range(ITERS)):
        if inner is not None:
            scale = []
            for i, (factor, column) in enumerate(factors_of(k + 1)):
                total = jnp.sum(inner[i], 1, keepdims=True) + zero
                scale.append((factor, total / column))

        def step(d, sums, k=k):
            if k == ITERS - 1:
                grads = seeds(d)
            else:
                grads = [
                    scale[i][0] * (carry_ref[d, pl.ds(SUBLANES * i, SUBLANES), :] - scale[i][1])
                    for i in range(tiles)
                ]
            new = []
            for i in range(tiles):
                rows = pl.ds(SUBLANES * i, SUBLANES)
                along = jnp.sum(grads[i] * level_ref[k + 1, d, rows, :], 0, keepdims=True)
                scaled = (grads[i] - along) * inverse_ref[k, d, pl.ds(i, 1), :]
                carry_ref[d, rows, :] = scaled
                new.append(sums[i] + scaled * level_ref[k, d, rows, :])
            return tuple(new)

        inner = lax.fori_loop(0, devices, step, (zero,) * tiles, unroll=4)

    me = lax.axis_index(AXES)
    for i, (factor, column) in enumerate(factors_of(0)):
        rows = pl.ds(SUBLANES * i, SUBLANES)
        total = jnp.sum(inner[i], 1, keepdims=True) + zero
        carry_ref[0, rows, :] = (
            factor * (carry_ref[me, rows, :] - total / column) * own_ref[rows, :]
        )
    group_ref[...] = carry_ref[0, :groups, :]
    expert_ref[...] = carry_ref[0, SUBLANES:, :]


def adjoint(slot_grads, saved, own, groups, capacity, targets):
    level = saved[0]
    _, lanes = level.shape[2:]
    vmem = pl.BlockSpec(memory_space=pltpu.VMEM)
    return pl.pallas_call(
        partial(adjoint_kernel, groups=groups, capacity=capacity, targets=targets),
        out_shape=[
            jax.ShapeDtypeStruct((groups, lanes), jnp.float32),
            jax.ShapeDtypeStruct((groups * SUBLANES, lanes), jnp.float32),
        ],
        in_specs=[vmem] * (2 + len(saved)),
        out_specs=[vmem, vmem],
        scratch_shapes=[pltpu.VMEM(level.shape[1:], jnp.float32)],
        cost_estimate=pl.CostEstimate(flops=10_000_000, bytes_accessed=8_000_000, transcendentals=0),
        name="adjoint",
    )(slot_grads, *saved, own)


def spread(block, axes):
    copies = jnp.broadcast_to(block[None], (lax.axis_size(axes),) + block.shape)
    return lax.all_to_all(copies, axes, split_axis=0, concat_axis=0)


def replicated(group_logits, expert_logits, expert_ids, cotangent, hidden_saved, w_down):
    groups = lax.axis_size(("half", "plane"))
    per_group = lax.axis_size("expert")
    near = lax.axis_size(NEAR)
    experts = groups * per_group
    tokens_here, top_count = expert_ids.shape
    width = cotangent.shape[1]
    capacity = hidden_saved.shape[1] // experts
    targets = (float(tokens_here * per_group), float(tokens_here * groups))
    half = lax.axis_index("half")
    table = jnp.stack([half, 1 - half]).astype(jnp.int32)

    def swap(block):
        return lax.ppermute(block, "half", [(0, 1), (1, 0)])

    mine = pl.pallas_call(
        mine_kernel,
        out_shape=jax.ShapeDtypeStruct((SUBLANES + experts, tokens_here), jnp.float32),
        name="mine",
    )(group_logits.T, expert_ids.T, expert_logits.T)
    other = swap(mine)

    parts = 2 if width % (2 * LANES) == 0 else 1
    part = width // parts
    swapped = []
    for i in range(parts):
        block = cotangent[:, i * part : (i + 1) * part]
        swapped.append(swap(block))

    everyone = spread(jnp.stack([mine, other]), NEAR)

    def send(small, rows, after=()):
        packed = pack_rows(small, rows, near, capacity, groups, top_count, after)
        packed = packed.reshape(near, capacity, -1)
        got = lax.all_to_all(packed, NEAR, split_axis=0, concat_axis=0)
        return got.reshape(near * capacity, -1)

    weight, hidden = w_down[0], hidden_saved[0]
    rows = send(mine, cotangent)
    *saved, gates, own = forward(everyone, groups, top_count, capacity, targets, ())
    result = product(table, 0, rows, weight, hidden, gates)
    carried = None
    for i in range(parts):
        last = i == parts - 1
        rows = send(other, swapped[i])
        carried = product(
            table, 1, rows, weight, hidden, gates, i, carried, last,
            list(result) if last else None, () if last else (result[1],),
        )
    hidden_grad, slot_grad = carried
    slot_grads = spread(slot_grad, AXES).reshape(experts, -1)
    d_group, d_expert = adjoint(slot_grads, saved, own, groups, capacity, targets)
    return (hidden_grad[None], d_group.T, d_expert.T)


def per_device(group_logits, expert_logits, expert_ids, cotangent, hidden_saved, w_down):
    groups = lax.axis_size(("half", "plane"))
    per_group = lax.axis_size("expert")
    tokens_here, top_count = expert_ids.shape
    capacity = hidden_saved.shape[1] // (groups * per_group)
    everyone_bytes = 4 * tokens_here * (groups * per_group) * (groups * per_group + SUBLANES)
    fits = (
        tokens_here == LANES
        and lax.axis_size("half") == 2
        and per_group == SUBLANES
        and groups + top_count <= SUBLANES
        and LANES % capacity == 0
        and capacity % SUBLANES == 0
        and everyone_bytes <= REPLICATED_BYTES
    )
    form = replicated if fits else distributed
    return form(group_logits, expert_logits, expert_ids, cotangent, hidden_saved, w_down)


def solution(mesh):
    groups, per_group = mesh.shape["group"], mesh.shape["expert"]
    halves = 2 if groups % 2 == 0 else 1
    parts = Mesh(mesh.devices.reshape(halves, groups // halves, per_group), AXES)
    rows = P(AXES, None)
    blocks = P(AXES, None, None)
    return jax.shard_map(
        per_device,
        mesh=parts,
        in_specs=(rows, rows, rows, rows, blocks, blocks),
        out_specs=(blocks, rows, rows),
        check_vma=False,
    )
```

```python
from functools import partial

import jax
import jax.numpy as jnp
from jax import lax
from jax.experimental import pallas as pl
from jax.experimental.pallas import tpu as pltpu
from jax.sharding import Mesh
from jax.sharding import PartitionSpec as P

ITERS = 5
SOFTCAP = 4.0
LANES = 128
SUBLANES = 8
AXES = ("half", "plane", "expert")
NEAR = ("plane", "expert")
REPLICATED_BYTES = 1 << 20


def capped(logits):
    return jnp.exp(SOFTCAP * jnp.tanh(logits / SOFTCAP))


def squashing(logits):
    bounded = jnp.tanh(logits / SOFTCAP)
    return 1.0 - bounded * bounded


def balance_level(level_in, target, column_sum):
    scaled = level_in * (target / column_sum)
    return (scaled, jnp.sum(scaled, -1, keepdims=True))


def adjoint_local(out_grad, level_in, target, column_sum):
    scaled, row_total = balance_level(level_in, target, column_sum)
    level_out = scaled / row_total
    scaled_grad = (out_grad - jnp.sum(out_grad * level_out, -1, keepdims=True)) / row_total
    return (scaled_grad, jnp.sum(scaled_grad * level_in, 0))


def adjoint_finish(scaled_grad, inner, target, column_sum):
    return target / column_sum * (scaled_grad - inner / column_sum)


def balance_step(targets, current, unused):
    target_group, target_expert = targets
    group_in, expert_in = current
    group_cols, expert_cols = lax.psum((jnp.sum(group_in, 0), jnp.sum(expert_in, 0)), AXES)
    scaled_g, rowsum_g = balance_level(group_in, target_group, group_cols)
    scaled_e, rowsum_e = balance_level(expert_in, target_expert, expert_cols)
    return (
        (scaled_g / rowsum_g, scaled_e / rowsum_e),
        (group_in, expert_in, group_cols, expert_cols),
    )


def adjoint_step(targets, carried, stored_step):
    target_group, target_expert = targets
    grad_g, grad_e = carried
    group_in, expert_in, group_cols, expert_cols = stored_step
    scaled_g, inner_g = adjoint_local(grad_g, group_in, target_group, group_cols)
    scaled_e, inner_e = adjoint_local(grad_e, expert_in, target_expert, expert_cols)
    inner_g, inner_e = lax.psum((inner_g, inner_e), AXES)
    next_g = adjoint_finish(scaled_g, inner_g, target_group, group_cols)
    next_e = adjoint_finish(scaled_e, inner_e, target_expert, expert_cols)
    return ((next_g, next_e), None)


def slots_of(expert_ids, experts, capacity):
    flat_ids = expert_ids.reshape(-1)
    picked = (flat_ids[:, None] == jnp.arange(experts, dtype=jnp.int32)[None, :]).astype(jnp.int32)
    positions = jnp.sum((jnp.cumsum(picked, 0) - picked) * picked, 1)
    return flat_ids * capacity + positions


def distributed(group_logits, expert_logits, expert_ids, cotangent, hidden_saved, w_down):
    groups = lax.axis_size(("half", "plane"))
    per_group = lax.axis_size("expert")
    experts = groups * per_group
    tokens_here, top_count = expert_ids.shape
    capacity = hidden_saved.shape[1] // experts
    slots = experts * capacity
    targets = (float(tokens_here * per_group), float(tokens_here * groups))
    slot_index = slots_of(expert_ids, experts, capacity)
    serial = jnp.arange(slot_index.shape[0], dtype=jnp.int32)
    source_index = jnp.zeros((slots,), jnp.int32).at[slot_index].set(serial)
    filled = jnp.zeros((slots,), jnp.int32).at[slot_index].set(1)
    fetched = jnp.take(cotangent, source_index // top_count, axis=0)
    send_rows = jnp.where(filled[:, None] > 0, fetched, jnp.zeros_like(fetched))
    expert_rows = lax.all_to_all(send_rows, AXES, split_axis=0, concat_axis=0, tiled=True)
    group_of = expert_ids // per_group
    group_aff = capped(group_logits)
    expert_aff = capped(expert_logits).reshape(tokens_here, groups, per_group)
    (group_prob, expert_prob), stored = lax.scan(
        partial(balance_step, targets), (group_aff, expert_aff), None, length=ITERS
    )
    pick_group = jnp.take_along_axis(group_prob, group_of, 1)
    pick_expert = jnp.take_along_axis(expert_prob.reshape(tokens_here, experts), expert_ids, 1)
    pair_prob = pick_group * pick_expert
    total_prob = jnp.sum(pair_prob, 1, keepdims=True)
    gate_prob = pair_prob / total_prob
    gate_sent = (
        jnp.zeros((slots,), jnp.bfloat16)
        .at[slot_index]
        .set(gate_prob.astype(jnp.bfloat16).reshape(-1))
    )
    got_gates = lax.all_to_all(gate_sent, AXES, split_axis=0, concat_axis=0, tiled=True)
    unscaled = lax.dot_general(
        expert_rows, w_down[0], (((1,), (1,)), ((), ())), preferred_element_type=jnp.float32
    )
    slot_grad = jnp.sum(unscaled * hidden_saved[0].astype(jnp.float32), 1)
    grad_rows = (got_gates.reshape(-1, 1).astype(jnp.float32) * unscaled).astype(jnp.bfloat16)
    answers = lax.all_to_all(slot_grad, AXES, split_axis=0, concat_axis=0, tiled=True)
    gate_grad = answers[slot_index].reshape(tokens_here, top_count)
    pair_grad = (gate_grad - jnp.sum(gate_prob * gate_grad, 1, keepdims=True)) / total_prob
    group_pick = (
        group_of[:, :, None] == jnp.arange(groups, dtype=jnp.int32)[None, None, :]
    ).astype(jnp.float32)
    seed_group = jnp.sum(group_pick * (pair_grad * pick_expert)[:, :, None], 1)
    expert_pick = (
        expert_ids[:, :, None] == jnp.arange(experts, dtype=jnp.int32)[None, None, :]
    ).astype(jnp.float32)
    seed_expert = jnp.sum(expert_pick * (pair_grad * pick_group)[:, :, None], 1).reshape(
        tokens_here, groups, per_group
    )
    (grad_group, grad_expert), unused = lax.scan(
        partial(adjoint_step, targets), (seed_group, seed_expert), stored, reverse=True
    )
    d_group_logits = grad_group * group_aff * squashing(group_logits)
    d_expert_logits = (grad_expert * expert_aff).reshape(tokens_here, experts) * squashing(
        expert_logits
    )
    return (grad_rows[None], d_group_logits, d_expert_logits)


def place_rows(ids, first, experts, capacity):
    lanes = ids[0].shape[1]
    expert = lax.broadcasted_iota(jnp.int32, (experts, lanes), 0)
    hits = [(row - first) == expert for row in ids]
    picked = sum(hit.astype(jnp.float32) for hit in hits)
    earlier = (
        lax.broadcasted_iota(jnp.int32, (lanes, lanes), 0)
        < lax.broadcasted_iota(jnp.int32, (lanes, lanes), 1)
    ).astype(jnp.bfloat16)
    before = jnp.dot(picked.astype(jnp.bfloat16), earlier, preferred_element_type=jnp.float32)
    slot_of = (expert * capacity).astype(jnp.float32) + before
    slot_at = lax.broadcasted_iota(jnp.int32, (experts * capacity, lanes), 0)
    place = jnp.zeros((experts * capacity, lanes), jnp.float32)
    for row, hit in zip(ids, hits):
        slot = jnp.sum(jnp.where(hit, slot_of, 0.0), 0, keepdims=True).astype(jnp.int32)
        here = (row >= first) & (row < first + experts)
        slot = jnp.where(here, slot, -1)
        place = place + (slot == slot_at).astype(jnp.float32)
    return place.astype(jnp.bfloat16)


def mine_kernel(group_ref, ids_ref, expert_ref, out_ref):
    groups, top_count = group_ref.shape[0], ids_ref.shape[0]
    out_ref[:SUBLANES, :] = jnp.zeros((SUBLANES, out_ref.shape[1]), jnp.float32)
    out_ref[:groups, :] = group_ref[...]
    out_ref[groups : groups + top_count, :] = ids_ref[...].astype(jnp.float32)
    out_ref[SUBLANES:, :] = expert_ref[...]


def pack_kernel(small_ref, *refs, near, capacity, first_id, top_count):
    *rows_refs, out_ref, place_ref = refs

    @pl.when(pl.program_id(0) == 0)
    def _():
        ids = [
            small_ref[first_id + k : first_id + k + 1, :].astype(jnp.int32)
            for k in range(top_count)
        ]
        place_ref[...] = place_rows(ids, lax.axis_index("half") * near, near, capacity)

    rows = rows_refs[0][...]
    for rows_ref in rows_refs[1:]:
        rows = rows + rows_ref[...]
    out_ref[...] = jnp.dot(
        place_ref[...], rows, preferred_element_type=jnp.float32
    ).astype(out_ref.dtype)


def pack_rows(small, rows, near, capacity, first_id, top_count):
    tokens, width = rows[0].shape
    dtype = rows[0].dtype
    slots = near * capacity
    block = max(n for n in range(LANES, 8 * LANES, LANES) if width % n == 0)
    return pl.pallas_call(
        partial(
            pack_kernel, near=near, capacity=capacity, first_id=first_id, top_count=top_count
        ),
        out_shape=jax.ShapeDtypeStruct((slots, width), dtype),
        grid=(width // block,),
        in_specs=[pl.BlockSpec(small.shape, lambda i: (0, 0))]
        + [pl.BlockSpec((tokens, block), lambda i: (0, i))] * len(rows),
        out_specs=pl.BlockSpec((slots, block), lambda i: (0, i)),
        scratch_shapes=[pltpu.VMEM((slots, tokens), dtype)],
        cost_estimate=pl.CostEstimate(
            flops=2 * tokens * slots * width,
            bytes_accessed=2 * width * (tokens + slots),
            transcendentals=0,
        ),
        name="pack_rows",
    )(small, *rows)


def tile_rows(g):
    return pl.ds(SUBLANES * (g + 1), SUBLANES)


def forward_kernel(
    all_ref, *refs, groups, top_count, capacity, targets, cube
):
    (level_ref, inverse_ref, column_ref, seed_q_ref, seed_p_ref, where_ref,
     gate_ref, own_ref, dense_ref, before_ref) = refs
    devices = all_ref.shape[0]
    tiles = groups + 1
    me = lax.axis_index(AXES)

    def block(d):
        across = jnp.bitwise_xor(d, me)
        place = jnp.int32(0)
        for step, bit in enumerate(cube):
            flag = jnp.bitwise_and(lax.shift_right_logical(across, jnp.int32(bit)), 1)
            place = place + flag * (1 << step)
        return place

    tile = (SUBLANES, LANES)
    row_id = lax.broadcasted_iota(jnp.int32, tile, 0)
    zero = jnp.zeros(tile, jnp.float32)

    def totals(sums):
        out = []
        for i in range(tiles):
            column = jnp.sum(sums[i], 1, keepdims=True) + zero
            out.append(jnp.where(row_id < groups, column, 1.0) if i == 0 else column)
        return out

    def start(d, sums):
        new = []
        place = block(d)
        for i in range(tiles):
            rows = pl.ds(SUBLANES * i, SUBLANES)
            level = capped(all_ref[place, rows, :])
            if i == 0:
                level = jnp.where(row_id < groups, level, 0.0)
            level_ref[0, d, rows, :] = level
            new.append(sums[i] + level)
        named = [
            all_ref[place, groups + k : groups + k + 1, :].astype(jnp.int32)
            for k in range(top_count)
        ]
        for g in range(groups):
            expert = row_id + g * SUBLANES
            hit = named[0] == expert
            for k in range(1, top_count):
                hit = hit | (named[k] == expert)
            dense_ref[d, pl.ds(SUBLANES * g, SUBLANES), :] = hit.astype(jnp.float32)
        return tuple(new)

    sums = lax.fori_loop(0, devices, start, (zero,) * tiles, unroll=2)

    for k in range(ITERS):
        columns = totals(sums)
        factors = []
        for i in range(tiles):
            column_ref[k, pl.ds(SUBLANES * i, SUBLANES), :] = columns[i]
            factors.append(targets[min(i, 1)] / columns[i])

        def step(d, sums, k=k, factors=factors):
            new = []
            for i in range(tiles):
                rows = pl.ds(SUBLANES * i, SUBLANES)
                scaled = level_ref[k, d, rows, :] * factors[i]
                inverse = 1.0 / jnp.sum(scaled, 0, keepdims=True)
                inverse_ref[k, d, pl.ds(i, 1), :] = inverse
                level = scaled * inverse
                level_ref[k + 1, d, rows, :] = level
                new.append(sums[i] + level)
            return tuple(new)

        sums = lax.fori_loop(0, devices, step, (zero,) * tiles, unroll=4)

    experts = groups * SUBLANES
    earlier = (
        lax.broadcasted_iota(jnp.int32, (LANES, LANES), 0)
        < lax.broadcasted_iota(jnp.int32, (LANES, LANES), 1)
    ).astype(jnp.bfloat16)
    before_ref[...] = jnp.dot(
        dense_ref[...].reshape(devices * experts, LANES).astype(jnp.bfloat16),
        earlier,
        preferred_element_type=jnp.float32,
    ).reshape(devices, experts, LANES)

    per_block = LANES // capacity
    slot_id = lax.broadcasted_iota(jnp.int32, (capacity, LANES), 0)

    def finish(d, unused):
        picks = []
        total = jnp.zeros((1, LANES), jnp.float32)
        for g in range(groups):
            hit = dense_ref[d, pl.ds(SUBLANES * g, SUBLANES), :]
            pick_p = hit * level_ref[ITERS, d, g : g + 1, :]
            pick_q = hit * level_ref[ITERS, d, tile_rows(g), :]
            pair = pick_p * pick_q
            total = total + jnp.sum(pair, 0, keepdims=True)
            picks.append((pick_p, pick_q, pair))
        hit_me = dense_ref[d, pl.ds(me, 1), :]
        before_me = before_ref[d, pl.ds(me, 1), :].astype(jnp.int32)
        for g in range(groups):
            rows = pl.ds(SUBLANES * g, SUBLANES)
            pick_p, pick_q, pair = picks[g]
            seed_q_ref[d, rows, :] = pick_p / total
            seed_p_ref[d, rows, :] = pick_q / total
            dense_ref[d, rows, :] = pair / total
            position = before_ref[d, rows, :].astype(jnp.int32)
            lane = lax.rem(d, per_block) * capacity + position
            where_ref[d, rows, :] = jnp.minimum(lane, LANES - 1)
        gate_me = dense_ref[d, pl.ds(me, 1), :].astype(jnp.bfloat16).astype(jnp.float32)
        taken = jnp.where((before_me == slot_id) & (hit_me > 0.0), gate_me, 0.0)
        gate_ref[pl.ds(d * capacity, capacity), :] = jnp.sum(taken, 1, keepdims=True) + jnp.zeros(
            (capacity, LANES), jnp.float32
        )
        return unused

    lax.fori_loop(0, devices, finish, 0)
    for i in range(tiles):
        rows = pl.ds(SUBLANES * i, SUBLANES)
        logits = all_ref[0, rows, :]
        own_ref[rows, :] = level_ref[0, me, rows, :] * squashing(logits)


def forward(everyone, cube, groups, top_count, capacity, targets):
    devices, rows, lanes = everyone.shape
    experts = groups * SUBLANES
    f32 = jnp.float32
    shapes = [
        ((ITERS + 1, devices, rows, lanes), f32),
        ((ITERS, devices, SUBLANES, lanes), f32),
        ((ITERS, rows, lanes), f32),
        ((devices, experts, lanes), f32),
        ((devices, experts, lanes), f32),
        ((devices, experts, lanes), jnp.int32),
        ((devices * capacity, lanes), f32),
        ((rows, lanes), f32),
    ]
    vmem = pl.BlockSpec(memory_space=pltpu.VMEM)
    return pl.pallas_call(
        partial(
            forward_kernel,
            groups=groups,
            top_count=top_count,
            capacity=capacity,
            targets=targets,
            cube=cube,
        ),
        out_shape=[jax.ShapeDtypeStruct(s, d) for s, d in shapes],
        in_specs=[vmem],
        out_specs=[vmem] * len(shapes),
        scratch_shapes=[
            pltpu.VMEM((devices, experts, lanes), f32),
            pltpu.VMEM((devices, experts, lanes), f32),
        ],
        cost_estimate=pl.CostEstimate(flops=10_000_000, bytes_accessed=8_000_000, transcendentals=0),
        name="forward",
    )(everyone)


def product_kernel(table_ref, *refs, carried, last, extra):
    refs = list(refs)
    rows_ref, weight_ref = refs[:2]
    del refs[:2]
    unscaled = lax.dot_general(
        rows_ref[...],
        weight_ref[...],
        (((1,), (1,)), ((), ())),
        preferred_element_type=jnp.float32,
    )
    if carried:
        unscaled = unscaled + refs.pop(0)[...]
    if not last:
        refs[extra][...] = unscaled
        return
    saved_ref, gate_ref = refs[:2]
    grad_ref, slot_ref, sum_ref = refs[-3:]
    grad_ref[...] = (gate_ref[:, :1] * unscaled).astype(grad_ref.dtype)
    partial_sums = unscaled * saved_ref[...].astype(jnp.float32)
    folded = partial_sums[:, :LANES]
    for j in range(1, partial_sums.shape[1] // LANES):
        folded = folded + partial_sums[:, j * LANES : (j + 1) * LANES]
    first = pl.program_id(0) == 0

    @pl.when(first)
    def _():
        sum_ref[...] = folded

    @pl.when(jnp.logical_not(first))
    def _():
        sum_ref[...] = sum_ref[...] + folded

    @pl.when(pl.program_id(0) == pl.num_programs(0) - 1)
    def _():
        slot_ref[0] = jnp.sum(sum_ref[...].T, 0, keepdims=True)


def product(
    table, entry, rows, weight, saved, gates, part=0, carried=None, last=True, earlier=None, after=()
):
    slots, width = rows.shape
    hidden = weight.shape[0]
    total = saved.shape[0]
    block = 256 if hidden % 256 == 0 else hidden
    row_block = pl.BlockSpec((slots, block), lambda i, table: (table[entry], i))
    own_block = pl.BlockSpec((slots, block), lambda i, table: (0, i))
    operands = [rows, weight]
    in_specs = [
        pl.BlockSpec((slots, width), lambda i, table: (0, 0)),
        pl.BlockSpec((block, width), lambda i, table: (i, part)),
    ]
    aliases = {}
    if carried is not None:
        operands.append(carried)
        in_specs.append(own_block)
    if last:
        operands += [saved, gates]
        in_specs += [row_block, pl.BlockSpec((slots, LANES), lambda i, table: (table[entry], 0))]
        if earlier is not None:
            aliases = {len(operands) + 1 + i: i for i in range(2)}
            operands += earlier
            in_specs += [pl.BlockSpec(memory_space=pl.ANY)] * 2
        out_shape = [
            jax.ShapeDtypeStruct((total, hidden), jnp.bfloat16),
            jax.ShapeDtypeStruct((total // slots, 1, slots), jnp.float32),
        ]
        out_specs = [row_block, pl.BlockSpec((1, 1, slots), lambda i, table: (table[entry], 0, 0))]
        scratch = [pltpu.VMEM((slots, LANES), jnp.float32)]
    else:
        out_shape = jax.ShapeDtypeStruct((slots, hidden), jnp.float32)
        out_specs = own_block
        scratch = []
    operands += after
    in_specs += [pl.BlockSpec(memory_space=pl.ANY)] * len(after)
    return pl.pallas_call(
        partial(product_kernel, carried=carried is not None, last=last, extra=len(after)),
        out_shape=out_shape,
        grid_spec=pltpu.PrefetchScalarGridSpec(
            num_scalar_prefetch=1,
            grid=(hidden // block,),
            in_specs=in_specs,
            out_specs=out_specs,
            scratch_shapes=scratch,
        ),
        input_output_aliases=aliases,
        cost_estimate=pl.CostEstimate(
            flops=2 * slots * width * hidden,
            bytes_accessed=2 * (slots * width + hidden * width + 2 * slots * hidden),
            transcendentals=0,
        ),
        name="product",
    )(table, *operands)


def adjoint_kernel(
    slot_ref, level_ref, inverse_ref, column_ref, seed_q_ref, seed_p_ref, where_ref,
    own_ref, group_ref, expert_ref, carry_ref, *, groups, capacity, targets
):
    devices = level_ref.shape[1]
    tiles = groups + 1
    tile = (SUBLANES, LANES)
    row_id = lax.broadcasted_iota(jnp.int32, tile, 0)
    zero = jnp.zeros(tile, jnp.float32)
    per_block = LANES // capacity

    def seeds(d):
        block = pl.ds(pl.multiple_of(lax.div(d, per_block) * LANES, LANES), LANES)
        grads = []
        mixed = jnp.zeros((1, LANES), jnp.float32)
        for g in range(groups):
            rows = pl.ds(SUBLANES * g, SUBLANES)
            grad = jnp.take_along_axis(slot_ref[rows, block], where_ref[d, rows, :], axis=1)
            gate = seed_q_ref[d, rows, :] * level_ref[ITERS, d, tile_rows(g), :]
            mixed = mixed + jnp.sum(gate * grad, 0, keepdims=True)
            grads.append(grad)
        out = [zero]
        for g in range(groups):
            rows = pl.ds(SUBLANES * g, SUBLANES)
            grad = grads[g] - mixed
            out.append(seed_q_ref[d, rows, :] * grad)
            level = jnp.sum(seed_p_ref[d, rows, :] * grad, 0, keepdims=True)
            out[0] = jnp.where(row_id == g, level, out[0])
        return out

    def factors_of(k):
        out = []
        for i in range(tiles):
            column = column_ref[k, pl.ds(SUBLANES * i, SUBLANES), :]
            factor = targets[min(i, 1)] / column
            if i == 0:
                factor = jnp.where(row_id < groups, factor, 0.0)
            out.append((factor, column))
        return out

    inner = None
    for k in reversed(range(ITERS)):
        if inner is not None:
            scale = []
            for i, (factor, column) in enumerate(factors_of(k + 1)):
                total = jnp.sum(inner[i], 1, keepdims=True) + zero
                scale.append((factor, total / column))

        def step(d, sums, k=k):
            if k == ITERS - 1:
                grads = seeds(d)
            else:
                grads = [
                    scale[i][0] * (carry_ref[d, pl.ds(SUBLANES * i, SUBLANES), :] - scale[i][1])
                    for i in range(tiles)
                ]
            new = []
            for i in range(tiles):
                rows = pl.ds(SUBLANES * i, SUBLANES)
                along = jnp.sum(grads[i] * level_ref[k + 1, d, rows, :], 0, keepdims=True)
                scaled = (grads[i] - along) * inverse_ref[k, d, pl.ds(i, 1), :]
                carry_ref[d, rows, :] = scaled
                new.append(sums[i] + scaled * level_ref[k, d, rows, :])
            return tuple(new)

        inner = lax.fori_loop(0, devices, step, (zero,) * tiles, unroll=4)

    me = lax.axis_index(AXES)
    for i, (factor, column) in enumerate(factors_of(0)):
        rows = pl.ds(SUBLANES * i, SUBLANES)
        total = jnp.sum(inner[i], 1, keepdims=True) + zero
        carry_ref[0, rows, :] = (
            factor * (carry_ref[me, rows, :] - total / column) * own_ref[rows, :]
        )
    group_ref[...] = carry_ref[0, :groups, :]
    expert_ref[...] = carry_ref[0, SUBLANES:, :]


def adjoint(slot_grads, saved, own, groups, capacity, targets):
    level = saved[0]
    _, lanes = level.shape[2:]
    vmem = pl.BlockSpec(memory_space=pltpu.VMEM)
    return pl.pallas_call(
        partial(adjoint_kernel, groups=groups, capacity=capacity, targets=targets),
        out_shape=[
            jax.ShapeDtypeStruct((groups, lanes), jnp.float32),
            jax.ShapeDtypeStruct((groups * SUBLANES, lanes), jnp.float32),
        ],
        in_specs=[vmem] * (2 + len(saved)),
        out_specs=[vmem, vmem],
        scratch_shapes=[pltpu.VMEM(level.shape[1:], jnp.float32)],
        cost_estimate=pl.CostEstimate(flops=10_000_000, bytes_accessed=8_000_000, transcendentals=0),
        name="adjoint",
    )(slot_grads, *saved, own)


def spread(block, axes):
    copies = jnp.broadcast_to(block[None], (lax.axis_size(axes),) + block.shape)
    return lax.all_to_all(copies, axes, split_axis=0, concat_axis=0)


def cube_bits(groups, per_group):
    low = per_group.bit_length() - 1
    high = (groups * per_group).bit_length() - 1
    return [*range(low, high), *range(low)]


def replicated(group_logits, expert_logits, expert_ids, cotangent, hidden_saved, w_down):
    groups = lax.axis_size(("half", "plane"))
    per_group = lax.axis_size("expert")
    near = lax.axis_size(NEAR)
    experts = groups * per_group
    tokens_here, top_count = expert_ids.shape
    capacity = hidden_saved.shape[1] // experts
    targets = (float(tokens_here * per_group), float(tokens_here * groups))
    half = lax.axis_index("half")
    table = jnp.stack([half, 1 - half]).astype(jnp.int32)

    planes = lax.axis_size("plane")

    mine = pl.pallas_call(
        mine_kernel,
        out_shape=jax.ShapeDtypeStruct((SUBLANES + experts, tokens_here), jnp.float32),
        name="mine",
    )(group_logits.T, expert_ids.T, expert_logits.T)
    column = [mine]
    for across in range(1, groups):
        pairs = [(d, d ^ (across * per_group)) for d in range(experts)]
        column.append(lax.ppermute(mine, AXES, pairs))
    other = column[planes]
    cube = cube_bits(groups, per_group)
    everyone = jnp.stack(column)
    for bit in cube[groups.bit_length() - 1 :]:
        pairs = [(d, d ^ (1 << bit)) for d in range(experts)]
        everyone = jnp.concatenate([everyone, lax.ppermute(everyone, AXES, pairs)])

    swapped = []
    for j in range(planes):
        up, down = (j, j + planes), (2 * planes - 1 - j, planes - 1 - j)
        swapped.append(lax.ppermute(cotangent, ("half", "plane"), [up, down]))

    def send(small, rows):
        packed = pack_rows(small, rows, near, capacity, groups, top_count)
        packed = packed.reshape(near, capacity, -1)
        got = lax.all_to_all(packed, NEAR, split_axis=0, concat_axis=0)
        return got.reshape(near * capacity, -1)

    weight, hidden = w_down[0], hidden_saved[0]
    own_rows = send(mine, [cotangent])
    other_rows = send(other, swapped)
    *saved, gates, own = forward(everyone, cube, groups, top_count, capacity, targets)
    result = product(table, 0, own_rows, weight, hidden, gates)
    result = product(table, 1, other_rows, weight, hidden, gates, earlier=list(result))
    hidden_grad, slot_grad = result
    slot_grads = spread(slot_grad, AXES).reshape(experts, -1)
    d_group, d_expert = adjoint(slot_grads, saved, own, groups, capacity, targets)
    return (hidden_grad[None], d_group.T, d_expert.T)


def per_device(group_logits, expert_logits, expert_ids, cotangent, hidden_saved, w_down):
    groups = lax.axis_size(("half", "plane"))
    per_group = lax.axis_size("expert")
    tokens_here, top_count = expert_ids.shape
    capacity = hidden_saved.shape[1] // (groups * per_group)
    everyone_bytes = 4 * tokens_here * (groups * per_group) * (groups * per_group + SUBLANES)
    fits = (
        tokens_here == LANES
        and groups in (2, 4)
        and per_group == SUBLANES
        and groups + top_count <= SUBLANES
        and LANES % capacity == 0
        and capacity % SUBLANES == 0
        and everyone_bytes <= REPLICATED_BYTES
    )
    form = replicated if fits else distributed
    return form(group_logits, expert_logits, expert_ids, cotangent, hidden_saved, w_down)


def solution(mesh):
    groups, per_group = mesh.shape["group"], mesh.shape["expert"]
    halves = 2 if groups % 2 == 0 else 1
    parts = Mesh(mesh.devices.reshape(halves, groups // halves, per_group), AXES)
    rows = P(AXES, None)
    blocks = P(AXES, None, None)
    return jax.shard_map(
        per_device,
        mesh=parts,
        in_specs=(rows, rows, rows, rows, blocks, blocks),
        out_specs=(blocks, rows, rows),
        check_vma=False,
    )
```

```python
from functools import partial

import jax
import jax.numpy as jnp
from jax import lax
from jax.experimental import pallas as pl
from jax.experimental.pallas import tpu as pltpu
from jax.sharding import Mesh
from jax.sharding import PartitionSpec as P

ITERS = 5
SOFTCAP = 4.0
LANES = 128
SUBLANES = 8
AXES = ("half", "plane", "expert")
NEAR = ("plane", "expert")
REPLICATED_BYTES = 1 << 20
PRODUCT_VMEM = 58880 << 10


def capped(logits):
    return jnp.exp(SOFTCAP * jnp.tanh(logits / SOFTCAP))


def squashing(logits):
    bounded = jnp.tanh(logits / SOFTCAP)
    return 1.0 - bounded * bounded


def balance_level(level_in, target, column_sum):
    scaled = level_in * (target / column_sum)
    return (scaled, jnp.sum(scaled, -1, keepdims=True))


def adjoint_local(out_grad, level_in, target, column_sum):
    scaled, row_total = balance_level(level_in, target, column_sum)
    level_out = scaled / row_total
    scaled_grad = (out_grad - jnp.sum(out_grad * level_out, -1, keepdims=True)) / row_total
    return (scaled_grad, jnp.sum(scaled_grad * level_in, 0))


def adjoint_finish(scaled_grad, inner, target, column_sum):
    return target / column_sum * (scaled_grad - inner / column_sum)


def balance_step(targets, current, unused):
    target_group, target_expert = targets
    group_in, expert_in = current
    group_cols, expert_cols = lax.psum((jnp.sum(group_in, 0), jnp.sum(expert_in, 0)), AXES)
    scaled_g, rowsum_g = balance_level(group_in, target_group, group_cols)
    scaled_e, rowsum_e = balance_level(expert_in, target_expert, expert_cols)
    return (
        (scaled_g / rowsum_g, scaled_e / rowsum_e),
        (group_in, expert_in, group_cols, expert_cols),
    )


def adjoint_step(targets, carried, stored_step):
    target_group, target_expert = targets
    grad_g, grad_e = carried
    group_in, expert_in, group_cols, expert_cols = stored_step
    scaled_g, inner_g = adjoint_local(grad_g, group_in, target_group, group_cols)
    scaled_e, inner_e = adjoint_local(grad_e, expert_in, target_expert, expert_cols)
    inner_g, inner_e = lax.psum((inner_g, inner_e), AXES)
    next_g = adjoint_finish(scaled_g, inner_g, target_group, group_cols)
    next_e = adjoint_finish(scaled_e, inner_e, target_expert, expert_cols)
    return ((next_g, next_e), None)


def slots_of(expert_ids, experts, capacity):
    flat_ids = expert_ids.reshape(-1)
    picked = (flat_ids[:, None] == jnp.arange(experts, dtype=jnp.int32)[None, :]).astype(jnp.int32)
    positions = jnp.sum((jnp.cumsum(picked, 0) - picked) * picked, 1)
    return flat_ids * capacity + positions


def distributed(group_logits, expert_logits, expert_ids, cotangent, hidden_saved, w_down):
    groups = lax.axis_size(("half", "plane"))
    per_group = lax.axis_size("expert")
    experts = groups * per_group
    tokens_here, top_count = expert_ids.shape
    capacity = hidden_saved.shape[1] // experts
    slots = experts * capacity
    targets = (float(tokens_here * per_group), float(tokens_here * groups))
    slot_index = slots_of(expert_ids, experts, capacity)
    serial = jnp.arange(slot_index.shape[0], dtype=jnp.int32)
    source_index = jnp.zeros((slots,), jnp.int32).at[slot_index].set(serial)
    filled = jnp.zeros((slots,), jnp.int32).at[slot_index].set(1)
    fetched = jnp.take(cotangent, source_index // top_count, axis=0)
    send_rows = jnp.where(filled[:, None] > 0, fetched, jnp.zeros_like(fetched))
    expert_rows = lax.all_to_all(send_rows, AXES, split_axis=0, concat_axis=0, tiled=True)
    group_of = expert_ids // per_group
    group_aff = capped(group_logits)
    expert_aff = capped(expert_logits).reshape(tokens_here, groups, per_group)
    (group_prob, expert_prob), stored = lax.scan(
        partial(balance_step, targets), (group_aff, expert_aff), None, length=ITERS
    )
    pick_group = jnp.take_along_axis(group_prob, group_of, 1)
    pick_expert = jnp.take_along_axis(expert_prob.reshape(tokens_here, experts), expert_ids, 1)
    pair_prob = pick_group * pick_expert
    total_prob = jnp.sum(pair_prob, 1, keepdims=True)
    gate_prob = pair_prob / total_prob
    gate_sent = (
        jnp.zeros((slots,), jnp.bfloat16)
        .at[slot_index]
        .set(gate_prob.astype(jnp.bfloat16).reshape(-1))
    )
    got_gates = lax.all_to_all(gate_sent, AXES, split_axis=0, concat_axis=0, tiled=True)
    unscaled = lax.dot_general(
        expert_rows, w_down[0], (((1,), (1,)), ((), ())), preferred_element_type=jnp.float32
    )
    slot_grad = jnp.sum(unscaled * hidden_saved[0].astype(jnp.float32), 1)
    grad_rows = (got_gates.reshape(-1, 1).astype(jnp.float32) * unscaled).astype(jnp.bfloat16)
    answers = lax.all_to_all(slot_grad, AXES, split_axis=0, concat_axis=0, tiled=True)
    gate_grad = answers[slot_index].reshape(tokens_here, top_count)
    pair_grad = (gate_grad - jnp.sum(gate_prob * gate_grad, 1, keepdims=True)) / total_prob
    group_pick = (
        group_of[:, :, None] == jnp.arange(groups, dtype=jnp.int32)[None, None, :]
    ).astype(jnp.float32)
    seed_group = jnp.sum(group_pick * (pair_grad * pick_expert)[:, :, None], 1)
    expert_pick = (
        expert_ids[:, :, None] == jnp.arange(experts, dtype=jnp.int32)[None, None, :]
    ).astype(jnp.float32)
    seed_expert = jnp.sum(expert_pick * (pair_grad * pick_group)[:, :, None], 1).reshape(
        tokens_here, groups, per_group
    )
    (grad_group, grad_expert), unused = lax.scan(
        partial(adjoint_step, targets), (seed_group, seed_expert), stored, reverse=True
    )
    d_group_logits = grad_group * group_aff * squashing(group_logits)
    d_expert_logits = (grad_expert * expert_aff).reshape(tokens_here, experts) * squashing(
        expert_logits
    )
    return (grad_rows[None], d_group_logits, d_expert_logits)


def place_rows(ids, first, experts, capacity):
    lanes = ids[0].shape[1]
    expert = lax.broadcasted_iota(jnp.int32, (experts, lanes), 0)
    hits = [(row - first) == expert for row in ids]
    picked = sum(hit.astype(jnp.float32) for hit in hits)
    earlier = (
        lax.broadcasted_iota(jnp.int32, (lanes, lanes), 0)
        < lax.broadcasted_iota(jnp.int32, (lanes, lanes), 1)
    ).astype(jnp.bfloat16)
    before = jnp.dot(picked.astype(jnp.bfloat16), earlier, preferred_element_type=jnp.float32)
    slot_of = (expert * capacity).astype(jnp.float32) + before
    slot_at = lax.broadcasted_iota(jnp.int32, (experts * capacity, lanes), 0)
    place = jnp.zeros((experts * capacity, lanes), jnp.float32)
    for row, hit in zip(ids, hits):
        slot = jnp.sum(jnp.where(hit, slot_of, 0.0), 0, keepdims=True).astype(jnp.int32)
        here = (row >= first) & (row < first + experts)
        slot = jnp.where(here, slot, -1)
        place = place + (slot == slot_at).astype(jnp.float32)
    return place.astype(jnp.bfloat16)


def mine_kernel(group_ref, ids_ref, expert_ref, out_ref):
    groups, top_count = group_ref.shape[0], ids_ref.shape[0]
    out_ref[:SUBLANES, :] = jnp.zeros((SUBLANES, out_ref.shape[1]), jnp.float32)
    out_ref[:groups, :] = group_ref[...]
    out_ref[groups : groups + top_count, :] = ids_ref[...].astype(jnp.float32)
    out_ref[SUBLANES:, :] = expert_ref[...]


def pack_kernel(small_ref, *refs, near, capacity, first_id, top_count):
    *rows_refs, out_ref, place_ref = refs

    @pl.when(pl.program_id(0) == 0)
    def _():
        ids = [
            small_ref[first_id + k : first_id + k + 1, :].astype(jnp.int32)
            for k in range(top_count)
        ]
        place_ref[...] = place_rows(ids, lax.axis_index("half") * near, near, capacity)

    rows = rows_refs[0][...]
    for rows_ref in rows_refs[1:]:
        rows = rows + rows_ref[...]
    out_ref[...] = jnp.dot(
        place_ref[...], rows, preferred_element_type=jnp.float32
    ).astype(out_ref.dtype)


def pack_rows(small, rows, near, capacity, first_id, top_count):
    tokens, width = rows[0].shape
    dtype = rows[0].dtype
    slots = near * capacity
    block = max(n for n in range(LANES, 8 * LANES, LANES) if width % n == 0)
    return pl.pallas_call(
        partial(
            pack_kernel, near=near, capacity=capacity, first_id=first_id, top_count=top_count
        ),
        out_shape=jax.ShapeDtypeStruct((slots, width), dtype),
        grid=(width // block,),
        in_specs=[pl.BlockSpec(small.shape, lambda i: (0, 0))]
        + [pl.BlockSpec((tokens, block), lambda i: (0, i))] * len(rows),
        out_specs=pl.BlockSpec((slots, block), lambda i: (0, i)),
        scratch_shapes=[pltpu.VMEM((slots, tokens), dtype)],
        cost_estimate=pl.CostEstimate(
            flops=2 * tokens * slots * width,
            bytes_accessed=2 * width * (tokens + slots),
            transcendentals=0,
        ),
        name="pack_rows",
    )(small, *rows)


def tile_rows(g):
    return pl.ds(SUBLANES * (g + 1), SUBLANES)


def forward_kernel(
    all_ref, *refs, groups, top_count, capacity, targets, cube
):
    (level_ref, inverse_ref, column_ref, seed_q_ref, seed_p_ref, where_ref,
     gate_ref, own_ref, dense_ref, before_ref) = refs
    devices = all_ref.shape[0]
    tiles = groups + 1
    me = lax.axis_index(AXES)

    def block(d):
        across = jnp.bitwise_xor(d, me)
        place = jnp.int32(0)
        for step, bit in enumerate(cube):
            flag = jnp.bitwise_and(lax.shift_right_logical(across, jnp.int32(bit)), 1)
            place = place + flag * (1 << step)
        return place

    tile = (SUBLANES, LANES)
    row_id = lax.broadcasted_iota(jnp.int32, tile, 0)
    zero = jnp.zeros(tile, jnp.float32)

    def totals(sums):
        out = []
        for i in range(tiles):
            column = jnp.sum(sums[i], 1, keepdims=True) + zero
            out.append(jnp.where(row_id < groups, column, 1.0) if i == 0 else column)
        return out

    def start(d, sums):
        new = []
        place = block(d)
        for i in range(tiles):
            rows = pl.ds(SUBLANES * i, SUBLANES)
            level = capped(all_ref[place, rows, :])
            if i == 0:
                level = jnp.where(row_id < groups, level, 0.0)
            level_ref[0, d, rows, :] = level
            new.append(sums[i] + level)
        named = [
            all_ref[place, groups + k : groups + k + 1, :].astype(jnp.int32)
            for k in range(top_count)
        ]
        for g in range(groups):
            expert = row_id + g * SUBLANES
            hit = named[0] == expert
            for k in range(1, top_count):
                hit = hit | (named[k] == expert)
            dense_ref[d, pl.ds(SUBLANES * g, SUBLANES), :] = hit.astype(jnp.float32)
        return tuple(new)

    sums = lax.fori_loop(0, devices, start, (zero,) * tiles, unroll=2)

    for k in range(ITERS):
        columns = totals(sums)
        factors = []
        for i in range(tiles):
            column_ref[k, pl.ds(SUBLANES * i, SUBLANES), :] = columns[i]
            factors.append(targets[min(i, 1)] / columns[i])

        def step(d, sums, k=k, factors=factors):
            new = []
            for i in range(tiles):
                rows = pl.ds(SUBLANES * i, SUBLANES)
                scaled = level_ref[k, d, rows, :] * factors[i]
                inverse = 1.0 / jnp.sum(scaled, 0, keepdims=True)
                inverse_ref[k, d, pl.ds(i, 1), :] = inverse
                level = scaled * inverse
                level_ref[k + 1, d, rows, :] = level
                new.append(sums[i] + level)
            return tuple(new)

        sums = lax.fori_loop(0, devices, step, (zero,) * tiles, unroll=4)

    experts = groups * SUBLANES
    earlier = (
        lax.broadcasted_iota(jnp.int32, (LANES, LANES), 0)
        < lax.broadcasted_iota(jnp.int32, (LANES, LANES), 1)
    ).astype(jnp.bfloat16)
    before_ref[...] = jnp.dot(
        dense_ref[...].reshape(devices * experts, LANES).astype(jnp.bfloat16),
        earlier,
        preferred_element_type=jnp.float32,
    ).reshape(devices, experts, LANES)

    per_block = LANES // capacity
    slot_id = lax.broadcasted_iota(jnp.int32, (capacity, LANES), 0)

    def finish(d, unused):
        picks = []
        total = jnp.zeros((1, LANES), jnp.float32)
        for g in range(groups):
            hit = dense_ref[d, pl.ds(SUBLANES * g, SUBLANES), :]
            pick_p = hit * level_ref[ITERS, d, g : g + 1, :]
            pick_q = hit * level_ref[ITERS, d, tile_rows(g), :]
            pair = pick_p * pick_q
            total = total + jnp.sum(pair, 0, keepdims=True)
            picks.append((pick_p, pick_q, pair))
        hit_me = dense_ref[d, pl.ds(me, 1), :]
        before_me = before_ref[d, pl.ds(me, 1), :].astype(jnp.int32)
        for g in range(groups):
            rows = pl.ds(SUBLANES * g, SUBLANES)
            pick_p, pick_q, pair = picks[g]
            seed_q_ref[d, rows, :] = pick_p / total
            seed_p_ref[d, rows, :] = pick_q / total
            dense_ref[d, rows, :] = pair / total
            position = before_ref[d, rows, :].astype(jnp.int32)
            lane = lax.rem(d, per_block) * capacity + position
            where_ref[d, rows, :] = jnp.minimum(lane, LANES - 1)
        gate_me = dense_ref[d, pl.ds(me, 1), :].astype(jnp.bfloat16).astype(jnp.float32)
        taken = jnp.where((before_me == slot_id) & (hit_me > 0.0), gate_me, 0.0)
        gate_ref[pl.ds(d * capacity, capacity), :] = jnp.sum(taken, 1, keepdims=True) + jnp.zeros(
            (capacity, LANES), jnp.float32
        )
        return unused

    lax.fori_loop(0, devices, finish, 0)
    for i in range(tiles):
        rows = pl.ds(SUBLANES * i, SUBLANES)
        logits = all_ref[0, rows, :]
        own_ref[rows, :] = level_ref[0, me, rows, :] * squashing(logits)


def forward(everyone, cube, groups, top_count, capacity, targets):
    devices, rows, lanes = everyone.shape
    experts = groups * SUBLANES
    f32 = jnp.float32
    shapes = [
        ((ITERS + 1, devices, rows, lanes), f32),
        ((ITERS, devices, SUBLANES, lanes), f32),
        ((ITERS, rows, lanes), f32),
        ((devices, experts, lanes), f32),
        ((devices, experts, lanes), f32),
        ((devices, experts, lanes), jnp.int32),
        ((devices * capacity, lanes), f32),
        ((rows, lanes), f32),
    ]
    vmem = pl.BlockSpec(memory_space=pltpu.VMEM)
    return pl.pallas_call(
        partial(
            forward_kernel,
            groups=groups,
            top_count=top_count,
            capacity=capacity,
            targets=targets,
            cube=cube,
        ),
        out_shape=[jax.ShapeDtypeStruct(s, d) for s, d in shapes],
        in_specs=[vmem],
        out_specs=[vmem] * len(shapes),
        scratch_shapes=[
            pltpu.VMEM((devices, experts, lanes), f32),
            pltpu.VMEM((devices, experts, lanes), f32),
        ],
        cost_estimate=pl.CostEstimate(flops=10_000_000, bytes_accessed=8_000_000, transcendentals=0),
        name="forward",
    )(everyone)


def product_kernel(table_ref, rows_ref, weight_ref, saved_ref, gate_ref, *refs):
    grad_ref, slot_ref, sum_ref = refs[-3:]
    unscaled = lax.dot_general(
        rows_ref[...],
        weight_ref[...],
        (((1,), (1,)), ((), ())),
        preferred_element_type=jnp.float32,
    )
    grad_ref[...] = (gate_ref[:, :1] * unscaled).astype(grad_ref.dtype)
    partial_sums = unscaled * saved_ref[...].astype(jnp.float32)
    folded = partial_sums[:, :LANES]
    for j in range(1, partial_sums.shape[1] // LANES):
        folded = folded + partial_sums[:, j * LANES : (j + 1) * LANES]
    first = pl.program_id(0) == 0

    @pl.when(first)
    def _():
        sum_ref[...] = folded

    @pl.when(jnp.logical_not(first))
    def _():
        sum_ref[...] = sum_ref[...] + folded

    @pl.when(pl.program_id(0) == pl.num_programs(0) - 1)
    def _():
        sums = jnp.sum(sum_ref[...].T, 0, keepdims=True)
        for d in range(slot_ref.shape[0]):
            slot_ref[d, 0] = sums


def product(table, entry, rows, weight, saved, gates, copies, earlier=()):
    slots, width = rows.shape
    hidden = weight.shape[0]
    total = saved.shape[0]
    block = 512 if hidden % 512 == 0 else hidden
    row_block = pl.BlockSpec((slots, block), lambda i, table: (table[entry], i))
    return pl.pallas_call(
        product_kernel,
        out_shape=[
            jax.ShapeDtypeStruct((total, hidden), jnp.bfloat16),
            jax.ShapeDtypeStruct((copies, total // slots, 1, slots), jnp.float32),
        ],
        grid_spec=pltpu.PrefetchScalarGridSpec(
            num_scalar_prefetch=1,
            grid=(hidden // block,),
            in_specs=[
                pl.BlockSpec((slots, width), lambda i, table: (0, 0)),
                pl.BlockSpec((block, width), lambda i, table: (i, 0)),
                row_block,
                pl.BlockSpec((slots, LANES), lambda i, table: (table[entry], 0)),
            ]
            + [pl.BlockSpec(memory_space=pl.ANY)] * len(earlier),
            out_specs=[
                row_block,
                pl.BlockSpec((copies, 1, 1, slots), lambda i, table: (0, table[entry], 0, 0)),
            ],
            scratch_shapes=[pltpu.VMEM((slots, LANES), jnp.float32)],
        ),
        input_output_aliases={5 + i: i for i in range(len(earlier))},
        compiler_params=pltpu.CompilerParams(vmem_limit_bytes=PRODUCT_VMEM),
        cost_estimate=pl.CostEstimate(
            flops=2 * slots * width * hidden,
            bytes_accessed=2 * (slots * width + hidden * width + 2 * slots * hidden),
            transcendentals=0,
        ),
        name="product",
    )(table, rows, weight, saved, gates, *earlier)


def adjoint_kernel(
    answer_ref, level_ref, inverse_ref, column_ref, seed_q_ref, seed_p_ref, where_ref,
    own_ref, group_ref, expert_ref, carry_ref, slot_ref, *, groups, capacity, targets
):
    devices = level_ref.shape[1]
    tiles = groups + 1
    tile = (SUBLANES, LANES)
    row_id = lax.broadcasted_iota(jnp.int32, tile, 0)
    zero = jnp.zeros(tile, jnp.float32)
    per_block = LANES // capacity
    width = answer_ref.shape[3]
    for e in range(answer_ref.shape[0]):
        for h in range(answer_ref.shape[1]):
            slot_ref[e : e + 1, h * width : (h + 1) * width] = answer_ref[e, h]

    def seeds(d):
        block = pl.ds(pl.multiple_of(lax.div(d, per_block) * LANES, LANES), LANES)
        grads = []
        mixed = jnp.zeros((1, LANES), jnp.float32)
        for g in range(groups):
            rows = pl.ds(SUBLANES * g, SUBLANES)
            grad = jnp.take_along_axis(slot_ref[rows, block], where_ref[d, rows, :], axis=1)
            gate = seed_q_ref[d, rows, :] * level_ref[ITERS, d, tile_rows(g), :]
            mixed = mixed + jnp.sum(gate * grad, 0, keepdims=True)
            grads.append(grad)
        out = [zero]
        for g in range(groups):
            rows = pl.ds(SUBLANES * g, SUBLANES)
            grad = grads[g] - mixed
            out.append(seed_q_ref[d, rows, :] * grad)
            level = jnp.sum(seed_p_ref[d, rows, :] * grad, 0, keepdims=True)
            out[0] = jnp.where(row_id == g, level, out[0])
        return out

    def factors_of(k):
        out = []
        for i in range(tiles):
            column = column_ref[k, pl.ds(SUBLANES * i, SUBLANES), :]
            factor = targets[min(i, 1)] / column
            if i == 0:
                factor = jnp.where(row_id < groups, factor, 0.0)
            out.append((factor, column))
        return out

    inner = None
    for k in reversed(range(ITERS)):
        if inner is not None:
            scale = []
            for i, (factor, column) in enumerate(factors_of(k + 1)):
                total = jnp.sum(inner[i], 1, keepdims=True) + zero
                scale.append((factor, total / column))

        def step(d, sums, k=k):
            if k == ITERS - 1:
                grads = seeds(d)
            else:
                grads = [
                    scale[i][0] * (carry_ref[d, pl.ds(SUBLANES * i, SUBLANES), :] - scale[i][1])
                    for i in range(tiles)
                ]
            new = []
            for i in range(tiles):
                rows = pl.ds(SUBLANES * i, SUBLANES)
                along = jnp.sum(grads[i] * level_ref[k + 1, d, rows, :], 0, keepdims=True)
                scaled = (grads[i] - along) * inverse_ref[k, d, pl.ds(i, 1), :]
                carry_ref[d, rows, :] = scaled
                new.append(sums[i] + scaled * level_ref[k, d, rows, :])
            return tuple(new)

        inner = lax.fori_loop(0, devices, step, (zero,) * tiles, unroll=4)

    me = lax.axis_index(AXES)
    for i, (factor, column) in enumerate(factors_of(0)):
        rows = pl.ds(SUBLANES * i, SUBLANES)
        total = jnp.sum(inner[i], 1, keepdims=True) + zero
        carry_ref[0, rows, :] = (
            factor * (carry_ref[me, rows, :] - total / column) * own_ref[rows, :]
        )
    group_ref[...] = carry_ref[0, :groups, :]
    expert_ref[...] = carry_ref[0, SUBLANES:, :]


def adjoint(slot_grads, saved, own, groups, capacity, targets):
    level = saved[0]
    _, lanes = level.shape[2:]
    vmem = pl.BlockSpec(memory_space=pltpu.VMEM)
    return pl.pallas_call(
        partial(adjoint_kernel, groups=groups, capacity=capacity, targets=targets),
        out_shape=[
            jax.ShapeDtypeStruct((groups, lanes), jnp.float32),
            jax.ShapeDtypeStruct((groups * SUBLANES, lanes), jnp.float32),
        ],
        in_specs=[vmem] * (2 + len(saved)),
        out_specs=[vmem, vmem],
        scratch_shapes=[
            pltpu.VMEM(level.shape[1:], jnp.float32),
            pltpu.VMEM((groups * SUBLANES, level.shape[1] * capacity), jnp.float32),
        ],
        compiler_params=pltpu.CompilerParams(vmem_limit_bytes=24 << 20),
        cost_estimate=pl.CostEstimate(flops=10_000_000, bytes_accessed=8_000_000, transcendentals=0),
        name="adjoint",
    )(slot_grads, *saved, own)


def cube_bits(groups, per_group):
    low = per_group.bit_length() - 1
    high = (groups * per_group).bit_length() - 1
    return [*range(low, high), *range(low)]


def replicated(group_logits, expert_logits, expert_ids, cotangent, hidden_saved, w_down):
    groups = lax.axis_size(("half", "plane"))
    per_group = lax.axis_size("expert")
    near = lax.axis_size(NEAR)
    experts = groups * per_group
    tokens_here, top_count = expert_ids.shape
    capacity = hidden_saved.shape[1] // experts
    targets = (float(tokens_here * per_group), float(tokens_here * groups))
    half = lax.axis_index("half")
    table = jnp.stack([half, 1 - half]).astype(jnp.int32)

    planes = lax.axis_size("plane")

    mine = pl.pallas_call(
        mine_kernel,
        out_shape=jax.ShapeDtypeStruct((SUBLANES + experts, tokens_here), jnp.float32),
        name="mine",
    )(group_logits.T, expert_ids.T, expert_logits.T)
    column = [mine]
    for across in range(1, groups):
        pairs = [(d, d ^ (across * per_group)) for d in range(experts)]
        column.append(lax.ppermute(mine, AXES, pairs))
    other = column[planes]
    cube = cube_bits(groups, per_group)
    everyone = jnp.stack(column)
    for bit in cube[groups.bit_length() - 1 :]:
        pairs = [(d, d ^ (1 << bit)) for d in range(experts)]
        everyone = jnp.concatenate([everyone, lax.ppermute(everyone, AXES, pairs)])

    swapped = []
    for j in range(planes):
        up, down = (j, j + planes), (2 * planes - 1 - j, planes - 1 - j)
        swapped.append(lax.ppermute(cotangent, ("half", "plane"), [up, down]))

    def send(small, rows):
        packed = pack_rows(small, rows, near, capacity, groups, top_count)
        packed = packed.reshape(near, capacity, -1)
        got = lax.all_to_all(packed, NEAR, split_axis=0, concat_axis=0)
        return got.reshape(near * capacity, -1)

    weight, hidden = w_down[0], hidden_saved[0]
    own_rows = send(mine, [cotangent])
    other_rows = send(other, swapped)
    *saved, gates, own = forward(everyone, cube, groups, top_count, capacity, targets)
    result = product(table, 0, own_rows, weight, hidden, gates, experts)
    result = product(table, 1, other_rows, weight, hidden, gates, experts, result)
    hidden_grad, slot_grad = result
    slot_grads = lax.all_to_all(slot_grad, AXES, split_axis=0, concat_axis=0)
    d_group, d_expert = adjoint(slot_grads, saved, own, groups, capacity, targets)
    return (hidden_grad[None], d_group.T, d_expert.T)


def per_device(group_logits, expert_logits, expert_ids, cotangent, hidden_saved, w_down):
    groups = lax.axis_size(("half", "plane"))
    per_group = lax.axis_size("expert")
    tokens_here, top_count = expert_ids.shape
    capacity = hidden_saved.shape[1] // (groups * per_group)
    everyone_bytes = 4 * tokens_here * (groups * per_group) * (groups * per_group + SUBLANES)
    fits = (
        tokens_here == LANES
        and groups in (2, 4)
        and per_group == SUBLANES
        and groups + top_count <= SUBLANES
        and LANES % capacity == 0
        and capacity % SUBLANES == 0
        and everyone_bytes <= REPLICATED_BYTES
    )
    form = replicated if fits else distributed
    return form(group_logits, expert_logits, expert_ids, cotangent, hidden_saved, w_down)


def solution(mesh):
    groups, per_group = mesh.shape["group"], mesh.shape["expert"]
    halves = 2 if groups % 2 == 0 else 1
    parts = Mesh(mesh.devices.reshape(halves, groups // halves, per_group), AXES)
    rows = P(AXES, None)
    blocks = P(AXES, None, None)
    return jax.shard_map(
        per_device,
        mesh=parts,
        in_specs=(rows, rows, rows, rows, blocks, blocks),
        out_specs=(blocks, rows, rows),
        check_vma=False,
    )
```

```python
from functools import partial

import jax
import jax.numpy as jnp
from jax import lax
from jax.experimental import pallas as pl
from jax.experimental.pallas import tpu as pltpu
from jax.sharding import Mesh
from jax.sharding import PartitionSpec as P

ITERS = 5
SOFTCAP = 4.0
LANES = 128
SUBLANES = 8
AXES = ("half", "plane", "expert")
NEAR = ("plane", "expert")
REPLICATED_BYTES = 1 << 20
OWN_VMEM = 24 << 20
OTHER_VMEM = 58880 << 10


def capped(logits):
    return jnp.exp(SOFTCAP * jnp.tanh(logits / SOFTCAP))


def squashing(logits):
    bounded = jnp.tanh(logits / SOFTCAP)
    return 1.0 - bounded * bounded


def balance_level(level_in, target, column_sum):
    scaled = level_in * (target / column_sum)
    return (scaled, jnp.sum(scaled, -1, keepdims=True))


def adjoint_local(out_grad, level_in, target, column_sum):
    scaled, row_total = balance_level(level_in, target, column_sum)
    level_out = scaled / row_total
    scaled_grad = (out_grad - jnp.sum(out_grad * level_out, -1, keepdims=True)) / row_total
    return (scaled_grad, jnp.sum(scaled_grad * level_in, 0))


def adjoint_finish(scaled_grad, inner, target, column_sum):
    return target / column_sum * (scaled_grad - inner / column_sum)


def balance_step(targets, current, unused):
    target_group, target_expert = targets
    group_in, expert_in = current
    group_cols, expert_cols = lax.psum((jnp.sum(group_in, 0), jnp.sum(expert_in, 0)), AXES)
    scaled_g, rowsum_g = balance_level(group_in, target_group, group_cols)
    scaled_e, rowsum_e = balance_level(expert_in, target_expert, expert_cols)
    return (
        (scaled_g / rowsum_g, scaled_e / rowsum_e),
        (group_in, expert_in, group_cols, expert_cols),
    )


def adjoint_step(targets, carried, stored_step):
    target_group, target_expert = targets
    grad_g, grad_e = carried
    group_in, expert_in, group_cols, expert_cols = stored_step
    scaled_g, inner_g = adjoint_local(grad_g, group_in, target_group, group_cols)
    scaled_e, inner_e = adjoint_local(grad_e, expert_in, target_expert, expert_cols)
    inner_g, inner_e = lax.psum((inner_g, inner_e), AXES)
    next_g = adjoint_finish(scaled_g, inner_g, target_group, group_cols)
    next_e = adjoint_finish(scaled_e, inner_e, target_expert, expert_cols)
    return ((next_g, next_e), None)


def slots_of(expert_ids, experts, capacity):
    flat_ids = expert_ids.reshape(-1)
    picked = (flat_ids[:, None] == jnp.arange(experts, dtype=jnp.int32)[None, :]).astype(jnp.int32)
    positions = jnp.sum((jnp.cumsum(picked, 0) - picked) * picked, 1)
    return flat_ids * capacity + positions


def distributed(group_logits, expert_logits, expert_ids, cotangent, hidden_saved, w_down):
    groups = lax.axis_size(("half", "plane"))
    per_group = lax.axis_size("expert")
    experts = groups * per_group
    tokens_here, top_count = expert_ids.shape
    capacity = hidden_saved.shape[1] // experts
    slots = experts * capacity
    targets = (float(tokens_here * per_group), float(tokens_here * groups))
    slot_index = slots_of(expert_ids, experts, capacity)
    serial = jnp.arange(slot_index.shape[0], dtype=jnp.int32)
    source_index = jnp.zeros((slots,), jnp.int32).at[slot_index].set(serial)
    filled = jnp.zeros((slots,), jnp.int32).at[slot_index].set(1)
    fetched = jnp.take(cotangent, source_index // top_count, axis=0)
    send_rows = jnp.where(filled[:, None] > 0, fetched, jnp.zeros_like(fetched))
    expert_rows = lax.all_to_all(send_rows, AXES, split_axis=0, concat_axis=0, tiled=True)
    group_of = expert_ids // per_group
    group_aff = capped(group_logits)
    expert_aff = capped(expert_logits).reshape(tokens_here, groups, per_group)
    (group_prob, expert_prob), stored = lax.scan(
        partial(balance_step, targets), (group_aff, expert_aff), None, length=ITERS
    )
    pick_group = jnp.take_along_axis(group_prob, group_of, 1)
    pick_expert = jnp.take_along_axis(expert_prob.reshape(tokens_here, experts), expert_ids, 1)
    pair_prob = pick_group * pick_expert
    total_prob = jnp.sum(pair_prob, 1, keepdims=True)
    gate_prob = pair_prob / total_prob
    gate_sent = (
        jnp.zeros((slots,), jnp.bfloat16)
        .at[slot_index]
        .set(gate_prob.astype(jnp.bfloat16).reshape(-1))
    )
    got_gates = lax.all_to_all(gate_sent, AXES, split_axis=0, concat_axis=0, tiled=True)
    unscaled = lax.dot_general(
        expert_rows, w_down[0], (((1,), (1,)), ((), ())), preferred_element_type=jnp.float32
    )
    slot_grad = jnp.sum(unscaled * hidden_saved[0].astype(jnp.float32), 1)
    grad_rows = (got_gates.reshape(-1, 1).astype(jnp.float32) * unscaled).astype(jnp.bfloat16)
    answers = lax.all_to_all(slot_grad, AXES, split_axis=0, concat_axis=0, tiled=True)
    gate_grad = answers[slot_index].reshape(tokens_here, top_count)
    pair_grad = (gate_grad - jnp.sum(gate_prob * gate_grad, 1, keepdims=True)) / total_prob
    group_pick = (
        group_of[:, :, None] == jnp.arange(groups, dtype=jnp.int32)[None, None, :]
    ).astype(jnp.float32)
    seed_group = jnp.sum(group_pick * (pair_grad * pick_expert)[:, :, None], 1)
    expert_pick = (
        expert_ids[:, :, None] == jnp.arange(experts, dtype=jnp.int32)[None, None, :]
    ).astype(jnp.float32)
    seed_expert = jnp.sum(expert_pick * (pair_grad * pick_group)[:, :, None], 1).reshape(
        tokens_here, groups, per_group
    )
    (grad_group, grad_expert), unused = lax.scan(
        partial(adjoint_step, targets), (seed_group, seed_expert), stored, reverse=True
    )
    d_group_logits = grad_group * group_aff * squashing(group_logits)
    d_expert_logits = (grad_expert * expert_aff).reshape(tokens_here, experts) * squashing(
        expert_logits
    )
    return (grad_rows[None], d_group_logits, d_expert_logits)


def place_rows(ids, first, experts, capacity):
    lanes = ids[0].shape[1]
    expert = lax.broadcasted_iota(jnp.int32, (experts, lanes), 0)
    hits = [(row - first) == expert for row in ids]
    picked = sum(hit.astype(jnp.float32) for hit in hits)
    earlier = (
        lax.broadcasted_iota(jnp.int32, (lanes, lanes), 0)
        < lax.broadcasted_iota(jnp.int32, (lanes, lanes), 1)
    ).astype(jnp.bfloat16)
    before = jnp.dot(picked.astype(jnp.bfloat16), earlier, preferred_element_type=jnp.float32)
    slot_of = (expert * capacity).astype(jnp.float32) + before
    slot_at = lax.broadcasted_iota(jnp.int32, (experts * capacity, lanes), 0)
    place = jnp.zeros((experts * capacity, lanes), jnp.float32)
    for row, hit in zip(ids, hits):
        slot = jnp.sum(jnp.where(hit, slot_of, 0.0), 0, keepdims=True).astype(jnp.int32)
        here = (row >= first) & (row < first + experts)
        slot = jnp.where(here, slot, -1)
        place = place + (slot == slot_at).astype(jnp.float32)
    return place.astype(jnp.bfloat16)


def mine_kernel(group_ref, ids_ref, expert_ref, out_ref):
    groups, top_count = group_ref.shape[0], ids_ref.shape[0]
    out_ref[:SUBLANES, :] = jnp.zeros((SUBLANES, out_ref.shape[1]), jnp.float32)
    out_ref[:groups, :] = group_ref[...]
    out_ref[groups : groups + top_count, :] = ids_ref[...].astype(jnp.float32)
    out_ref[SUBLANES:, :] = expert_ref[...]


def pack_kernel(small_ref, *refs, near, capacity, first_id, top_count, pieces):
    *sources, out_ref, rows_ref, packed_ref, in_sem, out_sem = refs
    width = out_ref.shape[1] // pieces
    incoming, outgoing = [], []
    for c in range(pieces):
        at = pl.ds(c * width, width)
        incoming.append(
            [
                pltpu.make_async_copy(source.at[:, at], rows_ref.at[s, :, at], in_sem.at[s, c])
                for s, source in enumerate(sources)
            ]
        )
        outgoing.append(
            pltpu.make_async_copy(packed_ref.at[:, at], out_ref.at[:, at], out_sem.at[c])
        )
    for copies in incoming:
        for copy in copies:
            copy.start()
    ids = [
        small_ref[first_id + k : first_id + k + 1, :].astype(jnp.int32) for k in range(top_count)
    ]
    place = place_rows(ids, lax.axis_index("half") * near, near, capacity)
    for c in range(pieces):
        at = pl.ds(c * width, width)
        for copy in incoming[c]:
            copy.wait()
        rows = rows_ref[0, :, at]
        for s in range(1, len(sources)):
            rows = rows + rows_ref[s, :, at]
        packed_ref[:, at] = jnp.dot(place, rows, preferred_element_type=jnp.float32).astype(
            packed_ref.dtype
        )
        outgoing[c].start()
    for copy in outgoing:
        copy.wait()


def pack_rows(small, rows, near, capacity, first_id, top_count):
    tokens, width = rows[0].shape
    dtype = rows[0].dtype
    slots = near * capacity
    pieces = max(n for n in range(1, SUBLANES) if width % (n * LANES) == 0)
    anywhere = pl.BlockSpec(memory_space=pl.ANY)
    return pl.pallas_call(
        partial(
            pack_kernel,
            near=near,
            capacity=capacity,
            first_id=first_id,
            top_count=top_count,
            pieces=pieces,
        ),
        out_shape=jax.ShapeDtypeStruct((slots, width), dtype),
        in_specs=[pl.BlockSpec(memory_space=pltpu.VMEM)] + [anywhere] * len(rows),
        out_specs=anywhere,
        scratch_shapes=[
            pltpu.VMEM((len(rows), tokens, width), dtype),
            pltpu.VMEM((slots, width), dtype),
            pltpu.SemaphoreType.DMA((len(rows), pieces)),
            pltpu.SemaphoreType.DMA((pieces,)),
        ],
        cost_estimate=pl.CostEstimate(
            flops=2 * tokens * slots * width,
            bytes_accessed=2 * width * (tokens + slots),
            transcendentals=0,
        ),
        name="pack_rows",
    )(small, *rows)


def tile_rows(g):
    return pl.ds(SUBLANES * (g + 1), SUBLANES)


def forward_kernel(
    all_ref, *refs, groups, top_count, capacity, targets, cube
):
    (level_ref, inverse_ref, column_ref, seed_q_ref, seed_p_ref, where_ref,
     gate_ref, own_ref, dense_ref, before_ref) = refs
    devices = all_ref.shape[0]
    tiles = groups + 1
    me = lax.axis_index(AXES)

    def block(d):
        across = jnp.bitwise_xor(d, me)
        place = jnp.int32(0)
        for step, bit in enumerate(cube):
            flag = jnp.bitwise_and(lax.shift_right_logical(across, jnp.int32(bit)), 1)
            place = place + flag * (1 << step)
        return place

    tile = (SUBLANES, LANES)
    row_id = lax.broadcasted_iota(jnp.int32, tile, 0)
    zero = jnp.zeros(tile, jnp.float32)

    def totals(sums):
        out = []
        for i in range(tiles):
            column = jnp.sum(sums[i], 1, keepdims=True) + zero
            out.append(jnp.where(row_id < groups, column, 1.0) if i == 0 else column)
        return out

    def start(d, sums):
        new = []
        place = block(d)
        for i in range(tiles):
            rows = pl.ds(SUBLANES * i, SUBLANES)
            level = capped(all_ref[place, rows, :])
            if i == 0:
                level = jnp.where(row_id < groups, level, 0.0)
            level_ref[0, d, rows, :] = level
            new.append(sums[i] + level)
        named = [
            all_ref[place, groups + k : groups + k + 1, :].astype(jnp.int32)
            for k in range(top_count)
        ]
        for g in range(groups):
            expert = row_id + g * SUBLANES
            hit = named[0] == expert
            for k in range(1, top_count):
                hit = hit | (named[k] == expert)
            dense_ref[d, pl.ds(SUBLANES * g, SUBLANES), :] = hit.astype(jnp.float32)
        return tuple(new)

    sums = lax.fori_loop(0, devices, start, (zero,) * tiles, unroll=2)

    for k in range(ITERS):
        columns = totals(sums)
        factors = []
        for i in range(tiles):
            column_ref[k, pl.ds(SUBLANES * i, SUBLANES), :] = columns[i]
            factors.append(targets[min(i, 1)] / columns[i])

        def step(d, sums, k=k, factors=factors):
            new = []
            for i in range(tiles):
                rows = pl.ds(SUBLANES * i, SUBLANES)
                scaled = level_ref[k, d, rows, :] * factors[i]
                inverse = 1.0 / jnp.sum(scaled, 0, keepdims=True)
                inverse_ref[k, d, pl.ds(i, 1), :] = inverse
                level = scaled * inverse
                level_ref[k + 1, d, rows, :] = level
                new.append(sums[i] + level)
            return tuple(new)

        sums = lax.fori_loop(0, devices, step, (zero,) * tiles, unroll=4)

    experts = groups * SUBLANES
    earlier = (
        lax.broadcasted_iota(jnp.int32, (LANES, LANES), 0)
        < lax.broadcasted_iota(jnp.int32, (LANES, LANES), 1)
    ).astype(jnp.bfloat16)
    before_ref[...] = jnp.dot(
        dense_ref[...].reshape(devices * experts, LANES).astype(jnp.bfloat16),
        earlier,
        preferred_element_type=jnp.float32,
    ).reshape(devices, experts, LANES)

    per_block = LANES // capacity
    slot_id = lax.broadcasted_iota(jnp.int32, (capacity, LANES), 0)

    def finish(d, unused):
        picks = []
        total = jnp.zeros((1, LANES), jnp.float32)
        for g in range(groups):
            hit = dense_ref[d, pl.ds(SUBLANES * g, SUBLANES), :]
            pick_p = hit * level_ref[ITERS, d, g : g + 1, :]
            pick_q = hit * level_ref[ITERS, d, tile_rows(g), :]
            pair = pick_p * pick_q
            total = total + jnp.sum(pair, 0, keepdims=True)
            picks.append((pick_p, pick_q, pair))
        hit_me = dense_ref[d, pl.ds(me, 1), :]
        before_me = before_ref[d, pl.ds(me, 1), :].astype(jnp.int32)
        for g in range(groups):
            rows = pl.ds(SUBLANES * g, SUBLANES)
            pick_p, pick_q, pair = picks[g]
            seed_q_ref[d, rows, :] = pick_p / total
            seed_p_ref[d, rows, :] = pick_q / total
            dense_ref[d, rows, :] = pair / total
            position = before_ref[d, rows, :].astype(jnp.int32)
            lane = lax.rem(d, per_block) * capacity + position
            where_ref[d, rows, :] = jnp.minimum(lane, LANES - 1)
        gate_me = dense_ref[d, pl.ds(me, 1), :].astype(jnp.bfloat16).astype(jnp.float32)
        taken = jnp.where((before_me == slot_id) & (hit_me > 0.0), gate_me, 0.0)
        gate_ref[pl.ds(d * capacity, capacity), :] = jnp.sum(taken, 1, keepdims=True) + jnp.zeros(
            (capacity, LANES), jnp.float32
        )
        return unused

    lax.fori_loop(0, devices, finish, 0)
    for i in range(tiles):
        rows = pl.ds(SUBLANES * i, SUBLANES)
        logits = all_ref[0, rows, :]
        own_ref[rows, :] = level_ref[0, me, rows, :] * squashing(logits)


def forward(everyone, cube, groups, top_count, capacity, targets):
    devices, rows, lanes = everyone.shape
    experts = groups * SUBLANES
    f32 = jnp.float32
    shapes = [
        ((ITERS + 1, devices, rows, lanes), f32),
        ((ITERS, devices, SUBLANES, lanes), f32),
        ((ITERS, rows, lanes), f32),
        ((devices, experts, lanes), f32),
        ((devices, experts, lanes), f32),
        ((devices, experts, lanes), jnp.int32),
        ((devices * capacity, lanes), f32),
        ((rows, lanes), f32),
    ]
    vmem = pl.BlockSpec(memory_space=pltpu.VMEM)
    return pl.pallas_call(
        partial(
            forward_kernel,
            groups=groups,
            top_count=top_count,
            capacity=capacity,
            targets=targets,
            cube=cube,
        ),
        out_shape=[jax.ShapeDtypeStruct(s, d) for s, d in shapes],
        in_specs=[vmem],
        out_specs=[vmem] * len(shapes),
        scratch_shapes=[
            pltpu.VMEM((devices, experts, lanes), f32),
            pltpu.VMEM((devices, experts, lanes), f32),
        ],
        cost_estimate=pl.CostEstimate(flops=10_000_000, bytes_accessed=8_000_000, transcendentals=0),
        name="forward",
    )(everyone)


def product_kernel(table_ref, rows_ref, weight_ref, saved_ref, gate_ref, *refs):
    grad_ref, slot_ref, sum_ref = refs[-3:]
    unscaled = lax.dot_general(
        rows_ref[...],
        weight_ref[...],
        (((1,), (1,)), ((), ())),
        preferred_element_type=jnp.float32,
    )
    grad_ref[...] = (gate_ref[:, :1] * unscaled).astype(grad_ref.dtype)
    partial_sums = unscaled * saved_ref[...].astype(jnp.float32)
    folded = partial_sums[:, :LANES]
    for j in range(1, partial_sums.shape[1] // LANES):
        folded = folded + partial_sums[:, j * LANES : (j + 1) * LANES]
    first = pl.program_id(0) == 0

    @pl.when(first)
    def _():
        sum_ref[...] = folded

    @pl.when(jnp.logical_not(first))
    def _():
        sum_ref[...] = sum_ref[...] + folded

    @pl.when(pl.program_id(0) == pl.num_programs(0) - 1)
    def _():
        sums = jnp.sum(sum_ref[...].T, 0, keepdims=True)
        for d in range(slot_ref.shape[0]):
            slot_ref[d, 0] = sums


def product(table, entry, rows, weight, saved, gates, copies, grant, earlier=()):
    slots, width = rows.shape
    hidden = weight.shape[0]
    total = saved.shape[0]
    block = 512 if hidden % 512 == 0 else hidden
    row_block = pl.BlockSpec((slots, block), lambda i, table: (table[entry], i))
    return pl.pallas_call(
        product_kernel,
        out_shape=[
            jax.ShapeDtypeStruct((total, hidden), jnp.bfloat16),
            jax.ShapeDtypeStruct((copies, total // slots, 1, slots), jnp.float32),
        ],
        grid_spec=pltpu.PrefetchScalarGridSpec(
            num_scalar_prefetch=1,
            grid=(hidden // block,),
            in_specs=[
                pl.BlockSpec((slots, width), lambda i, table: (0, 0)),
                pl.BlockSpec((block, width), lambda i, table: (i, 0)),
                row_block,
                pl.BlockSpec((slots, LANES), lambda i, table: (table[entry], 0)),
            ]
            + [pl.BlockSpec(memory_space=pl.ANY)] * len(earlier),
            out_specs=[
                row_block,
                pl.BlockSpec((copies, 1, 1, slots), lambda i, table: (0, table[entry], 0, 0)),
            ],
            scratch_shapes=[pltpu.VMEM((slots, LANES), jnp.float32)],
        ),
        input_output_aliases={5 + i: i for i in range(len(earlier))},
        compiler_params=pltpu.CompilerParams(vmem_limit_bytes=grant),
        cost_estimate=pl.CostEstimate(
            flops=2 * slots * width * hidden,
            bytes_accessed=2 * (slots * width + hidden * width + 2 * slots * hidden),
            transcendentals=0,
        ),
        name="product",
    )(table, rows, weight, saved, gates, *earlier)


def adjoint_kernel(
    answer_ref, level_ref, inverse_ref, column_ref, seed_q_ref, seed_p_ref, where_ref,
    own_ref, group_ref, expert_ref, carry_ref, slot_ref, *, groups, capacity, targets
):
    devices = level_ref.shape[1]
    tiles = groups + 1
    tile = (SUBLANES, LANES)
    row_id = lax.broadcasted_iota(jnp.int32, tile, 0)
    zero = jnp.zeros(tile, jnp.float32)
    per_block = LANES // capacity
    width = answer_ref.shape[3]
    for e in range(answer_ref.shape[0]):
        for h in range(answer_ref.shape[1]):
            slot_ref[e : e + 1, h * width : (h + 1) * width] = answer_ref[e, h]

    def seeds(d):
        block = pl.ds(pl.multiple_of(lax.div(d, per_block) * LANES, LANES), LANES)
        grads = []
        mixed = jnp.zeros((1, LANES), jnp.float32)
        for g in range(groups):
            rows = pl.ds(SUBLANES * g, SUBLANES)
            grad = jnp.take_along_axis(slot_ref[rows, block], where_ref[d, rows, :], axis=1)
            gate = seed_q_ref[d, rows, :] * level_ref[ITERS, d, tile_rows(g), :]
            mixed = mixed + jnp.sum(gate * grad, 0, keepdims=True)
            grads.append(grad)
        out = [zero]
        for g in range(groups):
            rows = pl.ds(SUBLANES * g, SUBLANES)
            grad = grads[g] - mixed
            out.append(seed_q_ref[d, rows, :] * grad)
            level = jnp.sum(seed_p_ref[d, rows, :] * grad, 0, keepdims=True)
            out[0] = jnp.where(row_id == g, level, out[0])
        return out

    def factors_of(k):
        out = []
        for i in range(tiles):
            column = column_ref[k, pl.ds(SUBLANES * i, SUBLANES), :]
            factor = targets[min(i, 1)] / column
            if i == 0:
                factor = jnp.where(row_id < groups, factor, 0.0)
            out.append((factor, column))
        return out

    inner = None
    for k in reversed(range(ITERS)):
        if inner is not None:
            scale = []
            for i, (factor, column) in enumerate(factors_of(k + 1)):
                total = jnp.sum(inner[i], 1, keepdims=True) + zero
                scale.append((factor, total / column))

        def step(d, sums, k=k):
            if k == ITERS - 1:
                grads = seeds(d)
            else:
                grads = [
                    scale[i][0] * (carry_ref[d, pl.ds(SUBLANES * i, SUBLANES), :] - scale[i][1])
                    for i in range(tiles)
                ]
            new = []
            for i in range(tiles):
                rows = pl.ds(SUBLANES * i, SUBLANES)
                along = jnp.sum(grads[i] * level_ref[k + 1, d, rows, :], 0, keepdims=True)
                scaled = (grads[i] - along) * inverse_ref[k, d, pl.ds(i, 1), :]
                carry_ref[d, rows, :] = scaled
                new.append(sums[i] + scaled * level_ref[k, d, rows, :])
            return tuple(new)

        inner = lax.fori_loop(0, devices, step, (zero,) * tiles, unroll=4)

    me = lax.axis_index(AXES)
    for i, (factor, column) in enumerate(factors_of(0)):
        rows = pl.ds(SUBLANES * i, SUBLANES)
        total = jnp.sum(inner[i], 1, keepdims=True) + zero
        carry_ref[0, rows, :] = (
            factor * (carry_ref[me, rows, :] - total / column) * own_ref[rows, :]
        )
    group_ref[...] = carry_ref[0, :groups, :]
    expert_ref[...] = carry_ref[0, SUBLANES:, :]


def adjoint(slot_grads, saved, own, groups, capacity, targets):
    level = saved[0]
    _, lanes = level.shape[2:]
    vmem = pl.BlockSpec(memory_space=pltpu.VMEM)
    return pl.pallas_call(
        partial(adjoint_kernel, groups=groups, capacity=capacity, targets=targets),
        out_shape=[
            jax.ShapeDtypeStruct((groups, lanes), jnp.float32),
            jax.ShapeDtypeStruct((groups * SUBLANES, lanes), jnp.float32),
        ],
        in_specs=[vmem] * (2 + len(saved)),
        out_specs=[vmem, vmem],
        scratch_shapes=[
            pltpu.VMEM(level.shape[1:], jnp.float32),
            pltpu.VMEM((groups * SUBLANES, level.shape[1] * capacity), jnp.float32),
        ],
        compiler_params=pltpu.CompilerParams(vmem_limit_bytes=24 << 20),
        cost_estimate=pl.CostEstimate(flops=10_000_000, bytes_accessed=8_000_000, transcendentals=0),
        name="adjoint",
    )(slot_grads, *saved, own)


def cube_bits(groups, per_group):
    low = per_group.bit_length() - 1
    high = (groups * per_group).bit_length() - 1
    return [*range(low, high), *range(low)]


def replicated(group_logits, expert_logits, expert_ids, cotangent, hidden_saved, w_down):
    groups = lax.axis_size(("half", "plane"))
    per_group = lax.axis_size("expert")
    near = lax.axis_size(NEAR)
    experts = groups * per_group
    tokens_here, top_count = expert_ids.shape
    capacity = hidden_saved.shape[1] // experts
    targets = (float(tokens_here * per_group), float(tokens_here * groups))
    half = lax.axis_index("half")
    table = jnp.stack([half, 1 - half]).astype(jnp.int32)

    planes = lax.axis_size("plane")

    mine = pl.pallas_call(
        mine_kernel,
        out_shape=jax.ShapeDtypeStruct((SUBLANES + experts, tokens_here), jnp.float32),
        name="mine",
    )(group_logits.T, expert_ids.T, expert_logits.T)
    column = [mine]
    for across in range(1, groups):
        pairs = [(d, d ^ (across * per_group)) for d in range(experts)]
        column.append(lax.ppermute(mine, AXES, pairs))
    other = column[planes]
    cube = cube_bits(groups, per_group)
    everyone = jnp.stack(column)
    for bit in cube[groups.bit_length() - 1 :]:
        pairs = [(d, d ^ (1 << bit)) for d in range(experts)]
        everyone = jnp.concatenate([everyone, lax.ppermute(everyone, AXES, pairs)])

    swapped = []
    for j in range(planes):
        up, down = (j, j + planes), (2 * planes - 1 - j, planes - 1 - j)
        swapped.append(lax.ppermute(cotangent, ("half", "plane"), [up, down]))

    def send(small, rows):
        packed = pack_rows(small, rows, near, capacity, groups, top_count)
        packed = packed.reshape(near, capacity, -1)
        got = lax.all_to_all(packed, NEAR, split_axis=0, concat_axis=0)
        return got.reshape(near * capacity, -1)

    weight, hidden = w_down[0], hidden_saved[0]
    own_rows = send(mine, [cotangent])
    other_rows = send(other, swapped)
    *saved, gates, own = forward(everyone, cube, groups, top_count, capacity, targets)
    result = product(table, 0, own_rows, weight, hidden, gates, experts, OWN_VMEM)
    result = product(table, 1, other_rows, weight, hidden, gates, experts, OTHER_VMEM, result)
    hidden_grad, slot_grad = result
    slot_grads = lax.all_to_all(slot_grad, AXES, split_axis=0, concat_axis=0)
    d_group, d_expert = adjoint(slot_grads, saved, own, groups, capacity, targets)
    return (hidden_grad[None], d_group.T, d_expert.T)


def per_device(group_logits, expert_logits, expert_ids, cotangent, hidden_saved, w_down):
    groups = lax.axis_size(("half", "plane"))
    per_group = lax.axis_size("expert")
    tokens_here, top_count = expert_ids.shape
    capacity = hidden_saved.shape[1] // (groups * per_group)
    everyone_bytes = 4 * tokens_here * (groups * per_group) * (groups * per_group + SUBLANES)
    fits = (
        tokens_here == LANES
        and groups in (2, 4)
        and per_group == SUBLANES
        and groups + top_count <= SUBLANES
        and LANES % capacity == 0
        and capacity % SUBLANES == 0
        and everyone_bytes <= REPLICATED_BYTES
    )
    form = replicated if fits else distributed
    return form(group_logits, expert_logits, expert_ids, cotangent, hidden_saved, w_down)


def solution(mesh):
    groups, per_group = mesh.shape["group"], mesh.shape["expert"]
    halves = 2 if groups % 2 == 0 else 1
    parts = Mesh(mesh.devices.reshape(halves, groups // halves, per_group), AXES)
    rows = P(AXES, None)
    blocks = P(AXES, None, None)
    return jax.shard_map(
        per_device,
        mesh=parts,
        in_specs=(rows, rows, rows, rows, blocks, blocks),
        out_specs=(blocks, rows, rows),
        check_vma=False,
    )
```

```python
from functools import partial

import jax
import jax.numpy as jnp
from jax import lax
from jax.experimental import pallas as pl
from jax.experimental.pallas import tpu as pltpu
from jax.sharding import Mesh
from jax.sharding import PartitionSpec as P

ITERS = 5
SOFTCAP = 4.0
LANES = 128
SUBLANES = 8
AXES = ("half", "plane", "expert")
NEAR = ("plane", "expert")
REPLICATED_BYTES = 1 << 20
OWN_VMEM = 24 << 20
OTHER_VMEM = 58880 << 10


def capped(logits):
    return jnp.exp(SOFTCAP * jnp.tanh(logits / SOFTCAP))


def squashing(logits):
    bounded = jnp.tanh(logits / SOFTCAP)
    return 1.0 - bounded * bounded


def balance_level(level_in, target, column_sum):
    scaled = level_in * (target / column_sum)
    return (scaled, jnp.sum(scaled, -1, keepdims=True))


def adjoint_local(out_grad, level_in, target, column_sum):
    scaled, row_total = balance_level(level_in, target, column_sum)
    level_out = scaled / row_total
    scaled_grad = (out_grad - jnp.sum(out_grad * level_out, -1, keepdims=True)) / row_total
    return (scaled_grad, jnp.sum(scaled_grad * level_in, 0))


def adjoint_finish(scaled_grad, inner, target, column_sum):
    return target / column_sum * (scaled_grad - inner / column_sum)


def balance_step(targets, current, unused):
    target_group, target_expert = targets
    group_in, expert_in = current
    group_cols, expert_cols = lax.psum((jnp.sum(group_in, 0), jnp.sum(expert_in, 0)), AXES)
    scaled_g, rowsum_g = balance_level(group_in, target_group, group_cols)
    scaled_e, rowsum_e = balance_level(expert_in, target_expert, expert_cols)
    return (
        (scaled_g / rowsum_g, scaled_e / rowsum_e),
        (group_in, expert_in, group_cols, expert_cols),
    )


def adjoint_step(targets, carried, stored_step):
    target_group, target_expert = targets
    grad_g, grad_e = carried
    group_in, expert_in, group_cols, expert_cols = stored_step
    scaled_g, inner_g = adjoint_local(grad_g, group_in, target_group, group_cols)
    scaled_e, inner_e = adjoint_local(grad_e, expert_in, target_expert, expert_cols)
    inner_g, inner_e = lax.psum((inner_g, inner_e), AXES)
    next_g = adjoint_finish(scaled_g, inner_g, target_group, group_cols)
    next_e = adjoint_finish(scaled_e, inner_e, target_expert, expert_cols)
    return ((next_g, next_e), None)


def slots_of(expert_ids, experts, capacity):
    flat_ids = expert_ids.reshape(-1)
    picked = (flat_ids[:, None] == jnp.arange(experts, dtype=jnp.int32)[None, :]).astype(jnp.int32)
    positions = jnp.sum((jnp.cumsum(picked, 0) - picked) * picked, 1)
    return flat_ids * capacity + positions


def distributed(group_logits, expert_logits, expert_ids, cotangent, hidden_saved, w_down):
    groups = lax.axis_size(("half", "plane"))
    per_group = lax.axis_size("expert")
    experts = groups * per_group
    tokens_here, top_count = expert_ids.shape
    capacity = hidden_saved.shape[1] // experts
    slots = experts * capacity
    targets = (float(tokens_here * per_group), float(tokens_here * groups))
    slot_index = slots_of(expert_ids, experts, capacity)
    serial = jnp.arange(slot_index.shape[0], dtype=jnp.int32)
    source_index = jnp.zeros((slots,), jnp.int32).at[slot_index].set(serial)
    filled = jnp.zeros((slots,), jnp.int32).at[slot_index].set(1)
    fetched = jnp.take(cotangent, source_index // top_count, axis=0)
    send_rows = jnp.where(filled[:, None] > 0, fetched, jnp.zeros_like(fetched))
    expert_rows = lax.all_to_all(send_rows, AXES, split_axis=0, concat_axis=0, tiled=True)
    group_of = expert_ids // per_group
    group_aff = capped(group_logits)
    expert_aff = capped(expert_logits).reshape(tokens_here, groups, per_group)
    (group_prob, expert_prob), stored = lax.scan(
        partial(balance_step, targets), (group_aff, expert_aff), None, length=ITERS
    )
    pick_group = jnp.take_along_axis(group_prob, group_of, 1)
    pick_expert = jnp.take_along_axis(expert_prob.reshape(tokens_here, experts), expert_ids, 1)
    pair_prob = pick_group * pick_expert
    total_prob = jnp.sum(pair_prob, 1, keepdims=True)
    gate_prob = pair_prob / total_prob
    gate_sent = (
        jnp.zeros((slots,), jnp.bfloat16)
        .at[slot_index]
        .set(gate_prob.astype(jnp.bfloat16).reshape(-1))
    )
    got_gates = lax.all_to_all(gate_sent, AXES, split_axis=0, concat_axis=0, tiled=True)
    unscaled = lax.dot_general(
        expert_rows, w_down[0], (((1,), (1,)), ((), ())), preferred_element_type=jnp.float32
    )
    slot_grad = jnp.sum(unscaled * hidden_saved[0].astype(jnp.float32), 1)
    grad_rows = (got_gates.reshape(-1, 1).astype(jnp.float32) * unscaled).astype(jnp.bfloat16)
    answers = lax.all_to_all(slot_grad, AXES, split_axis=0, concat_axis=0, tiled=True)
    gate_grad = answers[slot_index].reshape(tokens_here, top_count)
    pair_grad = (gate_grad - jnp.sum(gate_prob * gate_grad, 1, keepdims=True)) / total_prob
    group_pick = (
        group_of[:, :, None] == jnp.arange(groups, dtype=jnp.int32)[None, None, :]
    ).astype(jnp.float32)
    seed_group = jnp.sum(group_pick * (pair_grad * pick_expert)[:, :, None], 1)
    expert_pick = (
        expert_ids[:, :, None] == jnp.arange(experts, dtype=jnp.int32)[None, None, :]
    ).astype(jnp.float32)
    seed_expert = jnp.sum(expert_pick * (pair_grad * pick_group)[:, :, None], 1).reshape(
        tokens_here, groups, per_group
    )
    (grad_group, grad_expert), unused = lax.scan(
        partial(adjoint_step, targets), (seed_group, seed_expert), stored, reverse=True
    )
    d_group_logits = grad_group * group_aff * squashing(group_logits)
    d_expert_logits = (grad_expert * expert_aff).reshape(tokens_here, experts) * squashing(
        expert_logits
    )
    return (grad_rows[None], d_group_logits, d_expert_logits)


def place_rows(ids, first, experts, capacity):
    lanes = ids[0].shape[1]
    expert = lax.broadcasted_iota(jnp.int32, (experts, lanes), 0)
    hits = [(row - first) == expert for row in ids]
    picked = sum(hit.astype(jnp.float32) for hit in hits)
    earlier = (
        lax.broadcasted_iota(jnp.int32, (lanes, lanes), 0)
        < lax.broadcasted_iota(jnp.int32, (lanes, lanes), 1)
    ).astype(jnp.bfloat16)
    before = jnp.dot(picked.astype(jnp.bfloat16), earlier, preferred_element_type=jnp.float32)
    slot_of = (expert * capacity).astype(jnp.float32) + before
    slot_at = lax.broadcasted_iota(jnp.int32, (experts * capacity, lanes), 0)
    place = jnp.zeros((experts * capacity, lanes), jnp.float32)
    for row, hit in zip(ids, hits):
        slot = jnp.sum(jnp.where(hit, slot_of, 0.0), 0, keepdims=True).astype(jnp.int32)
        here = (row >= first) & (row < first + experts)
        slot = jnp.where(here, slot, -1)
        place = place + (slot == slot_at).astype(jnp.float32)
    return place.astype(jnp.bfloat16)


def row_copies(source, rows_ref, in_sem, packed_ref, out_ref, out_sem, pieces):
    width = out_ref.shape[1] // pieces
    incoming, outgoing = [], []
    for c in range(pieces):
        at = pl.ds(c * width, width)
        incoming.append(
            pltpu.make_async_copy(source.at[:, at], rows_ref.at[:, at], in_sem.at[c])
        )
        outgoing.append(
            pltpu.make_async_copy(packed_ref.at[:, at], out_ref.at[:, at], out_sem.at[c])
        )
    return incoming, outgoing


def pack_pieces(place, rows_ref, packed_ref, incoming, outgoing, cuts=()):
    width = packed_ref.shape[1] // len(incoming)
    for c, copy in enumerate(incoming):
        at = pl.ds(c * width, width)
        copy.wait()
        packed_ref[:, at] = jnp.dot(
            place, rows_ref[:, at], preferred_element_type=jnp.float32
        ).astype(packed_ref.dtype)
        outgoing[c].start()
        if cuts and (c + 1) * len(cuts) % len(incoming) == 0:
            cuts[(c + 1) * len(cuts) // len(incoming) - 1].start()
    for copy in [*outgoing, *cuts]:
        copy.wait()


def first_kernel(
    group_ref, ids_ref, expert_ref, cotangent_ref, mine_ref, out_ref, *refs, near, capacity,
    pieces, parts
):
    blocks, refs = refs[:parts], refs[parts:]
    *small_refs, small_sem, block_sem, rows_ref, packed_ref, in_sem, out_sem = refs
    small = [
        pltpu.make_async_copy(source, target, small_sem.at[i])
        for i, (source, target) in enumerate(zip((group_ref, ids_ref, expert_ref), small_refs))
    ]
    incoming, outgoing = row_copies(
        cotangent_ref, rows_ref, in_sem, packed_ref, out_ref, out_sem, pieces
    )
    part = rows_ref.shape[1] // parts
    cuts = [
        pltpu.make_async_copy(
            rows_ref.at[:, pl.ds(i * part, part)], block, block_sem.at[i]
        )
        for i, block in enumerate(blocks)
    ]
    for copy in small + incoming:
        copy.start()
    for copy in small:
        copy.wait()
    group_on, ids_on, expert_on = small_refs
    groups, top_count = group_on.shape[0], ids_on.shape[0]
    mine_ref[:SUBLANES, :] = jnp.zeros((SUBLANES, mine_ref.shape[1]), jnp.float32)
    mine_ref[:groups, :] = group_on[...]
    mine_ref[groups : groups + top_count, :] = ids_on[...].astype(jnp.float32)
    mine_ref[SUBLANES:, :] = expert_on[...]
    ids = [ids_on[k : k + 1, :] for k in range(top_count)]
    place = place_rows(ids, lax.axis_index("half") * near, near, capacity)
    pack_pieces(place, rows_ref, packed_ref, incoming, outgoing, cuts)


def first_rows(group_logits, expert_ids, expert_logits, cotangent, near, capacity, parts):
    width, dtype = cotangent.shape[1], cotangent.dtype
    slots = near * capacity
    pieces = max(n for n in range(parts, SUBLANES, parts) if width % (n * LANES) == 0)
    small = [group_logits.T, expert_ids.T, expert_logits.T]
    experts, tokens = small[2].shape
    anywhere = pl.BlockSpec(memory_space=pl.ANY)
    return pl.pallas_call(
        partial(first_kernel, near=near, capacity=capacity, pieces=pieces, parts=parts),
        out_shape=[
            jax.ShapeDtypeStruct((SUBLANES + experts, tokens), jnp.float32),
            jax.ShapeDtypeStruct((slots, width), dtype),
        ]
        + [jax.ShapeDtypeStruct((tokens, width // parts), dtype)] * parts,
        in_specs=[anywhere] * 4,
        out_specs=[pl.BlockSpec(memory_space=pltpu.VMEM)] + [anywhere] * (1 + parts),
        scratch_shapes=[pltpu.VMEM(x.shape, x.dtype) for x in small]
        + [pltpu.SemaphoreType.DMA((len(small),)), pltpu.SemaphoreType.DMA((parts,))]
        + [
            pltpu.VMEM((tokens, width), dtype),
            pltpu.VMEM((slots, width), dtype),
            pltpu.SemaphoreType.DMA((pieces,)),
            pltpu.SemaphoreType.DMA((pieces,)),
        ],
        cost_estimate=pl.CostEstimate(
            flops=2 * tokens * slots * width,
            bytes_accessed=2 * width * (tokens + slots),
            transcendentals=0,
        ),
        name="first_rows",
    )(*small, cotangent)


def pack_kernel(small_ref, *refs, near, capacity, first_id, top_count):
    *rows_refs, out_ref, place_ref = refs

    @pl.when(pl.program_id(0) == 0)
    def _():
        ids = [
            small_ref[first_id + k : first_id + k + 1, :].astype(jnp.int32)
            for k in range(top_count)
        ]
        place_ref[...] = place_rows(ids, lax.axis_index("half") * near, near, capacity)

    rows = rows_refs[0][...]
    for rows_ref in rows_refs[1:]:
        rows = rows + rows_ref[...]
    out_ref[...] = jnp.dot(
        place_ref[...], rows, preferred_element_type=jnp.float32
    ).astype(out_ref.dtype)


def pack_rows(small, rows, near, capacity, first_id, top_count):
    tokens, width = rows[0].shape
    dtype = rows[0].dtype
    slots = near * capacity
    block = max(n for n in range(LANES, 8 * LANES, LANES) if width % n == 0)
    return pl.pallas_call(
        partial(
            pack_kernel, near=near, capacity=capacity, first_id=first_id, top_count=top_count
        ),
        out_shape=jax.ShapeDtypeStruct((slots, width), dtype),
        grid=(width // block,),
        in_specs=[pl.BlockSpec(small.shape, lambda i: (0, 0))]
        + [pl.BlockSpec((tokens, block), lambda i: (0, i))] * len(rows),
        out_specs=pl.BlockSpec((slots, block), lambda i: (0, i)),
        scratch_shapes=[pltpu.VMEM((slots, tokens), dtype)],
        compiler_params=pltpu.CompilerParams(vmem_limit_bytes=OWN_VMEM),
        cost_estimate=pl.CostEstimate(
            flops=2 * tokens * slots * width,
            bytes_accessed=2 * width * (tokens + slots),
            transcendentals=0,
        ),
        name="pack_rows",
    )(small, *rows)


def tile_rows(g):
    return pl.ds(SUBLANES * (g + 1), SUBLANES)


def forward_kernel(
    all_ref, *refs, groups, top_count, capacity, targets, cube
):
    (level_out, inverse_out, column_ref, seed_q_ref, seed_p_ref, where_ref,
     gate_ref, own_ref, dense_ref, before_ref, level_ref, inverse_ref, level_sem) = refs
    outgoing = [
        pltpu.make_async_copy(level_ref.at[k], level_out.at[k], level_sem.at[k])
        for k in range(ITERS + 1)
    ]
    outgoing.append(pltpu.make_async_copy(inverse_ref, inverse_out, level_sem.at[ITERS + 1]))
    devices = all_ref.shape[0]
    tiles = groups + 1
    me = lax.axis_index(AXES)

    def block(d):
        across = jnp.bitwise_xor(d, me)
        place = jnp.int32(0)
        for step, bit in enumerate(cube):
            flag = jnp.bitwise_and(lax.shift_right_logical(across, jnp.int32(bit)), 1)
            place = place + flag * (1 << step)
        return place

    tile = (SUBLANES, LANES)
    row_id = lax.broadcasted_iota(jnp.int32, tile, 0)
    zero = jnp.zeros(tile, jnp.float32)

    def totals(sums):
        out = []
        for i in range(tiles):
            column = jnp.sum(sums[i], 1, keepdims=True) + zero
            out.append(jnp.where(row_id < groups, column, 1.0) if i == 0 else column)
        return out

    def start(d, sums):
        new = []
        place = block(d)
        for i in range(tiles):
            rows = pl.ds(SUBLANES * i, SUBLANES)
            level = capped(all_ref[place, rows, :])
            if i == 0:
                level = jnp.where(row_id < groups, level, 0.0)
            level_ref[0, d, rows, :] = level
            new.append(sums[i] + level)
        named = [
            all_ref[place, groups + k : groups + k + 1, :].astype(jnp.int32)
            for k in range(top_count)
        ]
        for g in range(groups):
            expert = row_id + g * SUBLANES
            hit = named[0] == expert
            for k in range(1, top_count):
                hit = hit | (named[k] == expert)
            dense_ref[d, pl.ds(SUBLANES * g, SUBLANES), :] = hit.astype(jnp.float32)
        return tuple(new)

    sums = lax.fori_loop(0, devices, start, (zero,) * tiles, unroll=4)
    outgoing[0].start()

    for k in range(ITERS):
        columns = totals(sums)
        factors = []
        for i in range(tiles):
            column_ref[k, pl.ds(SUBLANES * i, SUBLANES), :] = columns[i]
            factors.append(targets[min(i, 1)] / columns[i])

        def step(d, sums, k=k, factors=factors):
            new = []
            for i in range(tiles):
                rows = pl.ds(SUBLANES * i, SUBLANES)
                scaled = level_ref[k, d, rows, :] * factors[i]
                inverse = 1.0 / jnp.sum(scaled, 0, keepdims=True)
                inverse_ref[k, d, pl.ds(i, 1), :] = inverse
                level = scaled * inverse
                level_ref[k + 1, d, rows, :] = level
                new.append(sums[i] + level)
            return tuple(new)

        sums = lax.fori_loop(0, devices, step, (zero,) * tiles, unroll=4)
        outgoing[k + 1].start()
    outgoing[ITERS + 1].start()

    experts = groups * SUBLANES
    earlier = (
        lax.broadcasted_iota(jnp.int32, (LANES, LANES), 0)
        < lax.broadcasted_iota(jnp.int32, (LANES, LANES), 1)
    ).astype(jnp.bfloat16)
    before_ref[...] = jnp.dot(
        dense_ref[...].reshape(devices * experts, LANES).astype(jnp.bfloat16),
        earlier,
        preferred_element_type=jnp.float32,
    ).reshape(devices, experts, LANES)

    per_block = LANES // capacity
    slot_id = lax.broadcasted_iota(jnp.int32, (capacity, LANES), 0)

    def finish(d, unused):
        picks = []
        total = jnp.zeros((1, LANES), jnp.float32)
        for g in range(groups):
            hit = dense_ref[d, pl.ds(SUBLANES * g, SUBLANES), :]
            pick_p = hit * level_ref[ITERS, d, g : g + 1, :]
            pick_q = hit * level_ref[ITERS, d, tile_rows(g), :]
            pair = pick_p * pick_q
            total = total + jnp.sum(pair, 0, keepdims=True)
            picks.append((pick_p, pick_q, pair))
        share = 1.0 / total
        hit_me = dense_ref[d, pl.ds(me, 1), :]
        before_me = before_ref[d, pl.ds(me, 1), :].astype(jnp.int32)
        for g in range(groups):
            rows = pl.ds(SUBLANES * g, SUBLANES)
            pick_p, pick_q, pair = picks[g]
            seed_q_ref[d, rows, :] = pick_p * share
            seed_p_ref[d, rows, :] = pick_q * share
            dense_ref[d, rows, :] = pair * share
            position = before_ref[d, rows, :].astype(jnp.int32)
            lane = lax.rem(d, per_block) * capacity + position
            where_ref[d, rows, :] = jnp.minimum(lane, LANES - 1)
        gate_me = dense_ref[d, pl.ds(me, 1), :].astype(jnp.bfloat16).astype(jnp.float32)
        taken = jnp.where((before_me == slot_id) & (hit_me > 0.0), gate_me, 0.0)
        gate_ref[pl.ds(d * capacity, capacity), :] = jnp.sum(taken, 1, keepdims=True) + jnp.zeros(
            (capacity, LANES), jnp.float32
        )
        return unused

    lax.fori_loop(0, devices, finish, 0, unroll=4)
    for i in range(tiles):
        rows = pl.ds(SUBLANES * i, SUBLANES)
        logits = all_ref[0, rows, :]
        own_ref[rows, :] = level_ref[0, me, rows, :] * squashing(logits)
    for copy in outgoing:
        copy.wait()


def forward(everyone, cube, groups, top_count, capacity, targets):
    devices, rows, lanes = everyone.shape
    experts = groups * SUBLANES
    f32 = jnp.float32
    shapes = [
        ((ITERS + 1, devices, rows, lanes), f32),
        ((ITERS, devices, SUBLANES, lanes), f32),
        ((ITERS, rows, lanes), f32),
        ((devices, experts, lanes), f32),
        ((devices, experts, lanes), f32),
        ((devices, experts, lanes), jnp.int32),
        ((devices * capacity, lanes), f32),
        ((rows, lanes), f32),
    ]
    vmem = pl.BlockSpec(memory_space=pltpu.VMEM)
    return pl.pallas_call(
        partial(
            forward_kernel,
            groups=groups,
            top_count=top_count,
            capacity=capacity,
            targets=targets,
            cube=cube,
        ),
        out_shape=[jax.ShapeDtypeStruct(s, d) for s, d in shapes],
        in_specs=[vmem],
        out_specs=[pl.BlockSpec(memory_space=pl.ANY)] * 2 + [vmem] * (len(shapes) - 2),
        scratch_shapes=[
            pltpu.VMEM((devices, experts, lanes), f32),
            pltpu.VMEM((devices, experts, lanes), f32),
            pltpu.VMEM(shapes[0][0], f32),
            pltpu.VMEM(shapes[1][0], f32),
            pltpu.SemaphoreType.DMA((ITERS + 2,)),
        ],
        cost_estimate=pl.CostEstimate(flops=10_000_000, bytes_accessed=8_000_000, transcendentals=0),
        name="forward",
    )(everyone)


def product_kernel(table_ref, rows_ref, weight_ref, *refs, carried, last):
    refs = list(refs)
    unscaled = lax.dot_general(
        rows_ref[...],
        weight_ref[...],
        (((1,), (1,)), ((), ())),
        preferred_element_type=jnp.float32,
    )
    if carried:
        unscaled = unscaled + refs.pop(0)[...]
    if not last:
        refs[-1][...] = unscaled
        return
    saved_ref, gate_ref = refs[:2]
    grad_ref, slot_ref, sum_ref = refs[-3:]
    grad_ref[...] = (gate_ref[:, :1] * unscaled).astype(grad_ref.dtype)
    partial_sums = unscaled * saved_ref[...].astype(jnp.float32)
    folded = partial_sums[:, :LANES]
    for j in range(1, partial_sums.shape[1] // LANES):
        folded = folded + partial_sums[:, j * LANES : (j + 1) * LANES]
    first = pl.program_id(0) == 0

    @pl.when(first)
    def _():
        sum_ref[...] = folded

    @pl.when(jnp.logical_not(first))
    def _():
        sum_ref[...] = sum_ref[...] + folded

    @pl.when(pl.program_id(0) == pl.num_programs(0) - 1)
    def _():
        sums = jnp.sum(sum_ref[...].T, 0, keepdims=True)
        for d in range(slot_ref.shape[0]):
            slot_ref[d, 0] = sums


def product(
    table, entry, rows, weight, saved, gates, copies, grant, earlier=(), part=0, carried=None,
    last=True
):
    slots, width = rows.shape
    hidden = weight.shape[0]
    total = saved.shape[0]
    block = 512 if hidden % 512 == 0 else hidden
    row_block = pl.BlockSpec((slots, block), lambda i, table: (table[entry], i))
    own_block = pl.BlockSpec((slots, block), lambda i, table: (0, i))
    operands = [rows, weight]
    in_specs = [
        pl.BlockSpec((slots, width), lambda i, table: (0, 0)),
        pl.BlockSpec((block, width), lambda i, table: (i, part)),
    ]
    if carried is not None:
        operands.append(carried)
        in_specs.append(own_block)
    if last:
        operands += [saved, gates]
        in_specs += [row_block, pl.BlockSpec((slots, LANES), lambda i, table: (table[entry], 0))]
        out_shape = [
            jax.ShapeDtypeStruct((total, hidden), jnp.bfloat16),
            jax.ShapeDtypeStruct((copies, total // slots, 1, slots), jnp.float32),
        ]
        out_specs = [
            row_block,
            pl.BlockSpec((copies, 1, 1, slots), lambda i, table: (0, table[entry], 0, 0)),
        ]
        scratch = [pltpu.VMEM((slots, LANES), jnp.float32)]
    else:
        out_shape = jax.ShapeDtypeStruct((slots, hidden), jnp.float32)
        out_specs = own_block
        scratch = []
    first = 1 + len(operands)
    return pl.pallas_call(
        partial(product_kernel, carried=carried is not None, last=last),
        out_shape=out_shape,
        grid_spec=pltpu.PrefetchScalarGridSpec(
            num_scalar_prefetch=1,
            grid=(hidden // block,),
            in_specs=in_specs + [pl.BlockSpec(memory_space=pl.ANY)] * len(earlier),
            out_specs=out_specs,
            scratch_shapes=scratch,
        ),
        input_output_aliases={first + i: i for i in range(len(earlier))},
        compiler_params=pltpu.CompilerParams(vmem_limit_bytes=grant),
        cost_estimate=pl.CostEstimate(
            flops=2 * slots * width * hidden,
            bytes_accessed=2 * (slots * width + hidden * width + 2 * slots * hidden),
            transcendentals=0,
        ),
        name="product",
    )(table, *operands, *earlier)


def adjoint_kernel(
    answer_ref, level_ref, inverse_ref, column_ref, seed_q_ref, seed_p_ref, where_ref,
    own_ref, group_ref, expert_ref, carry_ref, slot_ref, *, groups, capacity, targets
):
    devices = level_ref.shape[1]
    tiles = groups + 1
    tile = (SUBLANES, LANES)
    row_id = lax.broadcasted_iota(jnp.int32, tile, 0)
    zero = jnp.zeros(tile, jnp.float32)
    per_block = LANES // capacity
    width = answer_ref.shape[3]
    for e in range(answer_ref.shape[0]):
        for h in range(answer_ref.shape[1]):
            slot_ref[e : e + 1, h * width : (h + 1) * width] = answer_ref[e, h]

    def seeds(d):
        block = pl.ds(pl.multiple_of(lax.div(d, per_block) * LANES, LANES), LANES)
        grads = []
        mixed = jnp.zeros((1, LANES), jnp.float32)
        for g in range(groups):
            rows = pl.ds(SUBLANES * g, SUBLANES)
            grad = jnp.take_along_axis(slot_ref[rows, block], where_ref[d, rows, :], axis=1)
            gate = seed_q_ref[d, rows, :] * level_ref[ITERS, d, tile_rows(g), :]
            mixed = mixed + jnp.sum(gate * grad, 0, keepdims=True)
            grads.append(grad)
        out = [zero]
        for g in range(groups):
            rows = pl.ds(SUBLANES * g, SUBLANES)
            grad = grads[g] - mixed
            out.append(seed_q_ref[d, rows, :] * grad)
            level = jnp.sum(seed_p_ref[d, rows, :] * grad, 0, keepdims=True)
            out[0] = jnp.where(row_id == g, level, out[0])
        return out

    def factors_of(k):
        out = []
        for i in range(tiles):
            column = column_ref[k, pl.ds(SUBLANES * i, SUBLANES), :]
            factor = targets[min(i, 1)] / column
            if i == 0:
                factor = jnp.where(row_id < groups, factor, 0.0)
            out.append((factor, column))
        return out

    inner = None
    for k in reversed(range(ITERS)):
        if inner is not None:
            scale = []
            for i, (factor, column) in enumerate(factors_of(k + 1)):
                total = jnp.sum(inner[i], 1, keepdims=True) + zero
                scale.append((factor, total / column))

        def step(d, sums, k=k):
            if k == ITERS - 1:
                grads = seeds(d)
            else:
                grads = [
                    scale[i][0] * (carry_ref[d, pl.ds(SUBLANES * i, SUBLANES), :] - scale[i][1])
                    for i in range(tiles)
                ]
            new = []
            for i in range(tiles):
                rows = pl.ds(SUBLANES * i, SUBLANES)
                along = jnp.sum(grads[i] * level_ref[k + 1, d, rows, :], 0, keepdims=True)
                scaled = (grads[i] - along) * inverse_ref[k, d, pl.ds(i, 1), :]
                carry_ref[d, rows, :] = scaled
                new.append(sums[i] + scaled * level_ref[k, d, rows, :])
            return tuple(new)

        inner = lax.fori_loop(0, devices, step, (zero,) * tiles, unroll=4)

    me = lax.axis_index(AXES)
    for i, (factor, column) in enumerate(factors_of(0)):
        rows = pl.ds(SUBLANES * i, SUBLANES)
        total = jnp.sum(inner[i], 1, keepdims=True) + zero
        carry_ref[0, rows, :] = (
            factor * (carry_ref[me, rows, :] - total / column) * own_ref[rows, :]
        )
    group_ref[...] = carry_ref[0, :groups, :]
    expert_ref[...] = carry_ref[0, SUBLANES:, :]


def adjoint(slot_grads, saved, own, groups, capacity, targets):
    level = saved[0]
    _, lanes = level.shape[2:]
    vmem = pl.BlockSpec(memory_space=pltpu.VMEM)
    return pl.pallas_call(
        partial(adjoint_kernel, groups=groups, capacity=capacity, targets=targets),
        out_shape=[
            jax.ShapeDtypeStruct((groups, lanes), jnp.float32),
            jax.ShapeDtypeStruct((groups * SUBLANES, lanes), jnp.float32),
        ],
        in_specs=[vmem] * (2 + len(saved)),
        out_specs=[vmem, vmem],
        scratch_shapes=[
            pltpu.VMEM(level.shape[1:], jnp.float32),
            pltpu.VMEM((groups * SUBLANES, level.shape[1] * capacity), jnp.float32),
        ],
        compiler_params=pltpu.CompilerParams(vmem_limit_bytes=24 << 20),
        cost_estimate=pl.CostEstimate(flops=10_000_000, bytes_accessed=8_000_000, transcendentals=0),
        name="adjoint",
    )(slot_grads, *saved, own)


def column_parts(width):
    return 2 if width % (2 * LANES) == 0 else 1


def cube_bits(groups, per_group):
    low = per_group.bit_length() - 1
    high = (groups * per_group).bit_length() - 1
    return [*range(low, high), *range(low)]


def replicated(group_logits, expert_logits, expert_ids, cotangent, hidden_saved, w_down):
    groups = lax.axis_size(("half", "plane"))
    per_group = lax.axis_size("expert")
    near = lax.axis_size(NEAR)
    experts = groups * per_group
    tokens_here, top_count = expert_ids.shape
    width = cotangent.shape[1]
    capacity = hidden_saved.shape[1] // experts
    targets = (float(tokens_here * per_group), float(tokens_here * groups))
    half = lax.axis_index("half")
    table = jnp.stack([half, 1 - half]).astype(jnp.int32)

    planes = lax.axis_size("plane")

    parts = column_parts(width)

    mine, own_packed, *cut_rows = first_rows(
        group_logits, expert_ids, expert_logits, cotangent, near, capacity, parts
    )
    column = [mine]
    for across in range(1, groups):
        pairs = [(d, d ^ (across * per_group)) for d in range(experts)]
        column.append(lax.ppermute(mine, AXES, pairs))
    other = column[planes]
    cube = cube_bits(groups, per_group)
    everyone = jnp.stack(column)
    for bit in cube[groups.bit_length() - 1 :]:
        pairs = [(d, d ^ (1 << bit)) for d in range(experts)]
        everyone = jnp.concatenate([everyone, lax.ppermute(everyone, AXES, pairs)])

    swapped = []
    for i, block in enumerate(cut_rows):
        swapped.append([])
        for j in range(planes):
            up, down = (j, j + planes), (2 * planes - 1 - j, planes - 1 - j)
            swapped[i].append(lax.ppermute(block, ("half", "plane"), [up, down]))

    def send(packed):
        packed = packed.reshape(near, capacity, -1)
        got = lax.all_to_all(packed, NEAR, split_axis=0, concat_axis=0)
        return got.reshape(near * capacity, -1)

    weight, hidden = w_down[0], hidden_saved[0]
    own_rows = send(own_packed)
    other_rows = []
    for i in range(parts):
        other_packed = pack_rows(other, swapped[i], near, capacity, groups, top_count)
        other_rows.append(send(other_packed))
    *saved, gates, own = forward(everyone, cube, groups, top_count, capacity, targets)
    result = product(table, 0, own_rows, weight, hidden, gates, experts, OWN_VMEM)
    carried = None
    for i in range(parts):
        last = i == parts - 1
        carried = product(
            table, 1, other_rows[i], weight, hidden, gates, experts,
            OTHER_VMEM if last else OWN_VMEM, result if last else (), i, carried, last,
        )
    result = carried
    hidden_grad, slot_grad = result
    slot_grads = lax.all_to_all(slot_grad, AXES, split_axis=0, concat_axis=0)
    d_group, d_expert = adjoint(slot_grads, saved, own, groups, capacity, targets)
    return (hidden_grad[None], d_group.T, d_expert.T)


def per_device(group_logits, expert_logits, expert_ids, cotangent, hidden_saved, w_down):
    groups = lax.axis_size(("half", "plane"))
    per_group = lax.axis_size("expert")
    tokens_here, top_count = expert_ids.shape
    capacity = hidden_saved.shape[1] // (groups * per_group)
    everyone_bytes = 4 * tokens_here * (groups * per_group) * (groups * per_group + SUBLANES)
    fits = (
        tokens_here == LANES
        and groups in (2, 4)
        and column_parts(cotangent.shape[1]) == 2
        and per_group == SUBLANES
        and groups + top_count <= SUBLANES
        and LANES % capacity == 0
        and capacity % SUBLANES == 0
        and everyone_bytes <= REPLICATED_BYTES
    )
    form = replicated if fits else distributed
    return form(group_logits, expert_logits, expert_ids, cotangent, hidden_saved, w_down)


def solution(mesh):
    groups, per_group = mesh.shape["group"], mesh.shape["expert"]
    halves = 2 if groups % 2 == 0 else 1
    parts = Mesh(mesh.devices.reshape(halves, groups // halves, per_group), AXES)
    rows = P(AXES, None)
    blocks = P(AXES, None, None)
    return jax.shard_map(
        per_device,
        mesh=parts,
        in_specs=(rows, rows, rows, rows, blocks, blocks),
        out_specs=(blocks, rows, rows),
        check_vma=False,
    )
```

```python
from functools import partial

import jax
import jax.numpy as jnp
from jax import lax
from jax.experimental import pallas as pl
from jax.experimental.pallas import tpu as pltpu
from jax.sharding import Mesh
from jax.sharding import PartitionSpec as P

ITERS = 5
SOFTCAP = 4.0
LANES = 128
SUBLANES = 8
AXES = ("half", "plane", "expert")
NEAR = ("plane", "expert")
REPLICATED_BYTES = 1 << 20
OWN_VMEM = 24 << 20
OTHER_VMEM = 58880 << 10


def capped(logits):
    return jnp.exp(SOFTCAP * jnp.tanh(logits / SOFTCAP))


def squashing(logits):
    bounded = jnp.tanh(logits / SOFTCAP)
    return 1.0 - bounded * bounded


def balance_level(level_in, target, column_sum):
    scaled = level_in * (target / column_sum)
    return (scaled, jnp.sum(scaled, -1, keepdims=True))


def adjoint_local(out_grad, level_in, target, column_sum):
    scaled, row_total = balance_level(level_in, target, column_sum)
    level_out = scaled / row_total
    scaled_grad = (out_grad - jnp.sum(out_grad * level_out, -1, keepdims=True)) / row_total
    return (scaled_grad, jnp.sum(scaled_grad * level_in, 0))


def adjoint_finish(scaled_grad, inner, target, column_sum):
    return target / column_sum * (scaled_grad - inner / column_sum)


def balance_step(targets, current, unused):
    target_group, target_expert = targets
    group_in, expert_in = current
    group_cols, expert_cols = lax.psum((jnp.sum(group_in, 0), jnp.sum(expert_in, 0)), AXES)
    scaled_g, rowsum_g = balance_level(group_in, target_group, group_cols)
    scaled_e, rowsum_e = balance_level(expert_in, target_expert, expert_cols)
    return (
        (scaled_g / rowsum_g, scaled_e / rowsum_e),
        (group_in, expert_in, group_cols, expert_cols),
    )


def adjoint_step(targets, carried, stored_step):
    target_group, target_expert = targets
    grad_g, grad_e = carried
    group_in, expert_in, group_cols, expert_cols = stored_step
    scaled_g, inner_g = adjoint_local(grad_g, group_in, target_group, group_cols)
    scaled_e, inner_e = adjoint_local(grad_e, expert_in, target_expert, expert_cols)
    inner_g, inner_e = lax.psum((inner_g, inner_e), AXES)
    next_g = adjoint_finish(scaled_g, inner_g, target_group, group_cols)
    next_e = adjoint_finish(scaled_e, inner_e, target_expert, expert_cols)
    return ((next_g, next_e), None)


def slots_of(expert_ids, experts, capacity):
    flat_ids = expert_ids.reshape(-1)
    picked = (flat_ids[:, None] == jnp.arange(experts, dtype=jnp.int32)[None, :]).astype(jnp.int32)
    positions = jnp.sum((jnp.cumsum(picked, 0) - picked) * picked, 1)
    return flat_ids * capacity + positions


def distributed(group_logits, expert_logits, expert_ids, cotangent, hidden_saved, w_down):
    groups = lax.axis_size(("half", "plane"))
    per_group = lax.axis_size("expert")
    experts = groups * per_group
    tokens_here, top_count = expert_ids.shape
    capacity = hidden_saved.shape[1] // experts
    slots = experts * capacity
    targets = (float(tokens_here * per_group), float(tokens_here * groups))
    slot_index = slots_of(expert_ids, experts, capacity)
    serial = jnp.arange(slot_index.shape[0], dtype=jnp.int32)
    source_index = jnp.zeros((slots,), jnp.int32).at[slot_index].set(serial)
    filled = jnp.zeros((slots,), jnp.int32).at[slot_index].set(1)
    fetched = jnp.take(cotangent, source_index // top_count, axis=0)
    send_rows = jnp.where(filled[:, None] > 0, fetched, jnp.zeros_like(fetched))
    expert_rows = lax.all_to_all(send_rows, AXES, split_axis=0, concat_axis=0, tiled=True)
    group_of = expert_ids // per_group
    group_aff = capped(group_logits)
    expert_aff = capped(expert_logits).reshape(tokens_here, groups, per_group)
    (group_prob, expert_prob), stored = lax.scan(
        partial(balance_step, targets), (group_aff, expert_aff), None, length=ITERS
    )
    pick_group = jnp.take_along_axis(group_prob, group_of, 1)
    pick_expert = jnp.take_along_axis(expert_prob.reshape(tokens_here, experts), expert_ids, 1)
    pair_prob = pick_group * pick_expert
    total_prob = jnp.sum(pair_prob, 1, keepdims=True)
    gate_prob = pair_prob / total_prob
    gate_sent = (
        jnp.zeros((slots,), jnp.bfloat16)
        .at[slot_index]
        .set(gate_prob.astype(jnp.bfloat16).reshape(-1))
    )
    got_gates = lax.all_to_all(gate_sent, AXES, split_axis=0, concat_axis=0, tiled=True)
    unscaled = lax.dot_general(
        expert_rows, w_down[0], (((1,), (1,)), ((), ())), preferred_element_type=jnp.float32
    )
    slot_grad = jnp.sum(unscaled * hidden_saved[0].astype(jnp.float32), 1)
    grad_rows = (got_gates.reshape(-1, 1).astype(jnp.float32) * unscaled).astype(jnp.bfloat16)
    answers = lax.all_to_all(slot_grad, AXES, split_axis=0, concat_axis=0, tiled=True)
    gate_grad = answers[slot_index].reshape(tokens_here, top_count)
    pair_grad = (gate_grad - jnp.sum(gate_prob * gate_grad, 1, keepdims=True)) / total_prob
    group_pick = (
        group_of[:, :, None] == jnp.arange(groups, dtype=jnp.int32)[None, None, :]
    ).astype(jnp.float32)
    seed_group = jnp.sum(group_pick * (pair_grad * pick_expert)[:, :, None], 1)
    expert_pick = (
        expert_ids[:, :, None] == jnp.arange(experts, dtype=jnp.int32)[None, None, :]
    ).astype(jnp.float32)
    seed_expert = jnp.sum(expert_pick * (pair_grad * pick_group)[:, :, None], 1).reshape(
        tokens_here, groups, per_group
    )
    (grad_group, grad_expert), unused = lax.scan(
        partial(adjoint_step, targets), (seed_group, seed_expert), stored, reverse=True
    )
    d_group_logits = grad_group * group_aff * squashing(group_logits)
    d_expert_logits = (grad_expert * expert_aff).reshape(tokens_here, experts) * squashing(
        expert_logits
    )
    return (grad_rows[None], d_group_logits, d_expert_logits)


def place_rows(ids, first, experts, capacity):
    lanes = ids[0].shape[1]
    expert = lax.broadcasted_iota(jnp.int32, (experts, lanes), 0)
    hits = [(row - first) == expert for row in ids]
    picked = sum(hit.astype(jnp.float32) for hit in hits)
    earlier = (
        lax.broadcasted_iota(jnp.int32, (lanes, lanes), 0)
        < lax.broadcasted_iota(jnp.int32, (lanes, lanes), 1)
    ).astype(jnp.bfloat16)
    before = jnp.dot(picked.astype(jnp.bfloat16), earlier, preferred_element_type=jnp.float32)
    slot_of = (expert * capacity).astype(jnp.float32) + before
    slot_at = lax.broadcasted_iota(jnp.int32, (experts * capacity, lanes), 0)
    place = jnp.zeros((experts * capacity, lanes), jnp.float32)
    for row, hit in zip(ids, hits):
        slot = jnp.sum(jnp.where(hit, slot_of, 0.0), 0, keepdims=True).astype(jnp.int32)
        here = (row >= first) & (row < first + experts)
        slot = jnp.where(here, slot, -1)
        place = place + (slot == slot_at).astype(jnp.float32)
    return place.astype(jnp.bfloat16)


def row_copies(source, rows_ref, in_sem, packed_ref, out_ref, out_sem, pieces):
    width = out_ref.shape[1] // pieces
    incoming, outgoing = [], []
    for c in range(pieces):
        at = pl.ds(c * width, width)
        incoming.append(
            pltpu.make_async_copy(source.at[:, at], rows_ref.at[:, at], in_sem.at[c])
        )
        outgoing.append(
            pltpu.make_async_copy(packed_ref.at[:, at], out_ref.at[:, at], out_sem.at[c])
        )
    return incoming, outgoing


def pack_pieces(place, rows_ref, packed_ref, incoming, outgoing, cuts=()):
    width = packed_ref.shape[1] // len(incoming)
    for c, copy in enumerate(incoming):
        at = pl.ds(c * width, width)
        copy.wait()
        packed_ref[:, at] = jnp.dot(
            place, rows_ref[:, at], preferred_element_type=jnp.float32
        ).astype(packed_ref.dtype)
        outgoing[c].start()
        if cuts and (c + 1) * len(cuts) % len(incoming) == 0:
            cuts[(c + 1) * len(cuts) // len(incoming) - 1].start()
    for copy in [*outgoing, *cuts]:
        copy.wait()


def first_kernel(
    group_ref, ids_ref, expert_ref, cotangent_ref, mine_ref, out_ref, *refs, near, capacity,
    pieces, parts
):
    blocks, refs = refs[:parts], refs[parts:]
    *small_refs, small_sem, block_sem, rows_ref, packed_ref, in_sem, out_sem = refs
    small = [
        pltpu.make_async_copy(source, target, small_sem.at[i])
        for i, (source, target) in enumerate(zip((group_ref, ids_ref, expert_ref), small_refs))
    ]
    incoming, outgoing = row_copies(
        cotangent_ref, rows_ref, in_sem, packed_ref, out_ref, out_sem, pieces
    )
    part = rows_ref.shape[1] // parts
    cuts = [
        pltpu.make_async_copy(
            rows_ref.at[:, pl.ds(i * part, part)], block, block_sem.at[i]
        )
        for i, block in enumerate(blocks)
    ]
    for copy in small + incoming:
        copy.start()
    for copy in small:
        copy.wait()
    group_on, ids_on, expert_on = small_refs
    groups, top_count = group_on.shape[0], ids_on.shape[0]
    mine_ref[:SUBLANES, :] = jnp.zeros((SUBLANES, mine_ref.shape[1]), jnp.float32)
    mine_ref[:groups, :] = group_on[...]
    mine_ref[groups : groups + top_count, :] = ids_on[...].astype(jnp.float32)
    mine_ref[SUBLANES:, :] = expert_on[...]
    ids = [ids_on[k : k + 1, :] for k in range(top_count)]
    place = place_rows(ids, lax.axis_index("half") * near, near, capacity)
    pack_pieces(place, rows_ref, packed_ref, incoming, outgoing, cuts)


def first_rows(group_logits, expert_ids, expert_logits, cotangent, near, capacity, parts):
    width, dtype = cotangent.shape[1], cotangent.dtype
    slots = near * capacity
    pieces = max(n for n in range(parts, SUBLANES, parts) if width % (n * LANES) == 0)
    small = [group_logits.T, expert_ids.T, expert_logits.T]
    experts, tokens = small[2].shape
    anywhere = pl.BlockSpec(memory_space=pl.ANY)
    return pl.pallas_call(
        partial(first_kernel, near=near, capacity=capacity, pieces=pieces, parts=parts),
        out_shape=[
            jax.ShapeDtypeStruct((SUBLANES + experts, tokens), jnp.float32),
            jax.ShapeDtypeStruct((slots, width), dtype),
        ]
        + [jax.ShapeDtypeStruct((tokens, width // parts), dtype)] * parts,
        in_specs=[anywhere] * 4,
        out_specs=[pl.BlockSpec(memory_space=pltpu.VMEM)] + [anywhere] * (1 + parts),
        scratch_shapes=[pltpu.VMEM(x.shape, x.dtype) for x in small]
        + [pltpu.SemaphoreType.DMA((len(small),)), pltpu.SemaphoreType.DMA((parts,))]
        + [
            pltpu.VMEM((tokens, width), dtype),
            pltpu.VMEM((slots, width), dtype),
            pltpu.SemaphoreType.DMA((pieces,)),
            pltpu.SemaphoreType.DMA((pieces,)),
        ],
        cost_estimate=pl.CostEstimate(
            flops=2 * tokens * slots * width,
            bytes_accessed=2 * width * (tokens + slots),
            transcendentals=0,
        ),
        name="first_rows",
    )(*small, cotangent)


def pack_kernel(small_ref, *refs, near, capacity, first_id, top_count):
    *rows_refs, out_ref, place_ref = refs

    @pl.when(pl.program_id(0) == 0)
    def _():
        ids = [
            small_ref[first_id + k : first_id + k + 1, :].astype(jnp.int32)
            for k in range(top_count)
        ]
        place_ref[...] = place_rows(ids, lax.axis_index("half") * near, near, capacity)

    rows = rows_refs[0][...]
    for rows_ref in rows_refs[1:]:
        rows = rows + rows_ref[...]
    out_ref[...] = jnp.dot(
        place_ref[...], rows, preferred_element_type=jnp.float32
    ).astype(out_ref.dtype)


def pack_rows(small, rows, near, capacity, first_id, top_count):
    tokens, width = rows[0].shape
    dtype = rows[0].dtype
    slots = near * capacity
    block = max(n for n in range(LANES, 8 * LANES, LANES) if width % n == 0)
    return pl.pallas_call(
        partial(
            pack_kernel, near=near, capacity=capacity, first_id=first_id, top_count=top_count
        ),
        out_shape=jax.ShapeDtypeStruct((slots, width), dtype),
        grid=(width // block,),
        in_specs=[pl.BlockSpec(small.shape, lambda i: (0, 0))]
        + [pl.BlockSpec((tokens, block), lambda i: (0, i))] * len(rows),
        out_specs=pl.BlockSpec((slots, block), lambda i: (0, i)),
        scratch_shapes=[pltpu.VMEM((slots, tokens), dtype)],
        compiler_params=pltpu.CompilerParams(vmem_limit_bytes=OWN_VMEM),
        cost_estimate=pl.CostEstimate(
            flops=2 * tokens * slots * width,
            bytes_accessed=2 * width * (tokens + slots),
            transcendentals=0,
        ),
        name="pack_rows",
    )(small, *rows)


def tile_rows(g):
    return pl.ds(SUBLANES * (g + 1), SUBLANES)


def forward_kernel(
    all_ref, *refs, groups, top_count, capacity, targets, cube
):
    (level_out, inverse_ref, column_ref, seed_q_ref, seed_p_ref, where_ref,
     gate_ref, own_ref, dense_ref, before_ref, level_ref, level_sem) = refs
    outgoing = [
        pltpu.make_async_copy(level_ref.at[k], level_out.at[k], level_sem.at[k])
        for k in range(ITERS + 1)
    ]
    devices = all_ref.shape[0]
    tiles = groups + 1
    me = lax.axis_index(AXES)

    def block(d):
        across = jnp.bitwise_xor(d, me)
        place = jnp.int32(0)
        for step, bit in enumerate(cube):
            flag = jnp.bitwise_and(lax.shift_right_logical(across, jnp.int32(bit)), 1)
            place = place + flag * (1 << step)
        return place

    tile = (SUBLANES, LANES)
    row_id = lax.broadcasted_iota(jnp.int32, tile, 0)
    zero = jnp.zeros(tile, jnp.float32)

    def totals(sums):
        out = []
        for i in range(tiles):
            column = jnp.sum(sums[i], 1, keepdims=True) + zero
            out.append(jnp.where(row_id < groups, column, 1.0) if i == 0 else column)
        return out

    def start(d, sums):
        new = []
        place = block(d)
        for i in range(tiles):
            rows = pl.ds(SUBLANES * i, SUBLANES)
            level = capped(all_ref[place, rows, :])
            if i == 0:
                level = jnp.where(row_id < groups, level, 0.0)
            level_ref[0, d, rows, :] = level
            new.append(sums[i] + level)
        named = [
            all_ref[place, groups + k : groups + k + 1, :].astype(jnp.int32)
            for k in range(top_count)
        ]
        for g in range(groups):
            expert = row_id + g * SUBLANES
            hit = named[0] == expert
            for k in range(1, top_count):
                hit = hit | (named[k] == expert)
            dense_ref[d, pl.ds(SUBLANES * g, SUBLANES), :] = hit.astype(jnp.float32)
        return tuple(new)

    sums = lax.fori_loop(0, devices, start, (zero,) * tiles, unroll=4)
    outgoing[0].start()

    for k in range(ITERS):
        columns = totals(sums)
        factors = []
        for i in range(tiles):
            column_ref[k, pl.ds(SUBLANES * i, SUBLANES), :] = columns[i]
            factors.append(targets[min(i, 1)] / columns[i])

        def step(d, sums, k=k, factors=factors):
            new = []
            for i in range(tiles):
                rows = pl.ds(SUBLANES * i, SUBLANES)
                scaled = level_ref[k, d, rows, :] * factors[i]
                inverse = 1.0 / jnp.sum(scaled, 0, keepdims=True)
                inverse_ref[k, d, pl.ds(i, 1), :] = inverse
                level = scaled * inverse
                level_ref[k + 1, d, rows, :] = level
                new.append(sums[i] + level)
            return tuple(new)

        sums = lax.fori_loop(0, devices, step, (zero,) * tiles, unroll=4)
        outgoing[k + 1].start()

    experts = groups * SUBLANES
    earlier = (
        lax.broadcasted_iota(jnp.int32, (LANES, LANES), 0)
        < lax.broadcasted_iota(jnp.int32, (LANES, LANES), 1)
    ).astype(jnp.bfloat16)
    before_ref[...] = jnp.dot(
        dense_ref[...].reshape(devices * experts, LANES).astype(jnp.bfloat16),
        earlier,
        preferred_element_type=jnp.float32,
    ).reshape(devices, experts, LANES)

    per_block = LANES // capacity
    slot_id = lax.broadcasted_iota(jnp.int32, (capacity, LANES), 0)

    def finish(d, unused):
        picks = []
        total = jnp.zeros((1, LANES), jnp.float32)
        for g in range(groups):
            hit = dense_ref[d, pl.ds(SUBLANES * g, SUBLANES), :]
            pick_p = hit * level_ref[ITERS, d, g : g + 1, :]
            pick_q = hit * level_ref[ITERS, d, tile_rows(g), :]
            pair = pick_p * pick_q
            total = total + jnp.sum(pair, 0, keepdims=True)
            picks.append((pick_p, pick_q, pair))
        hit_me = dense_ref[d, pl.ds(me, 1), :]
        before_me = before_ref[d, pl.ds(me, 1), :].astype(jnp.int32)
        for g in range(groups):
            rows = pl.ds(SUBLANES * g, SUBLANES)
            pick_p, pick_q, pair = picks[g]
            seed_q_ref[d, rows, :] = pick_p / total
            seed_p_ref[d, rows, :] = pick_q / total
            dense_ref[d, rows, :] = pair / total
            position = before_ref[d, rows, :].astype(jnp.int32)
            lane = lax.rem(d, per_block) * capacity + position
            where_ref[d, rows, :] = jnp.minimum(lane, LANES - 1)
        gate_me = dense_ref[d, pl.ds(me, 1), :].astype(jnp.bfloat16).astype(jnp.float32)
        taken = jnp.where((before_me == slot_id) & (hit_me > 0.0), gate_me, 0.0)
        gate_ref[pl.ds(d * capacity, capacity), :] = jnp.sum(taken, 1, keepdims=True) + jnp.zeros(
            (capacity, LANES), jnp.float32
        )
        return unused

    lax.fori_loop(0, devices, finish, 0, unroll=2)
    for i in range(tiles):
        rows = pl.ds(SUBLANES * i, SUBLANES)
        logits = all_ref[0, rows, :]
        own_ref[rows, :] = level_ref[0, me, rows, :] * squashing(logits)
    for copy in outgoing:
        copy.wait()


def forward(everyone, cube, groups, top_count, capacity, targets):
    devices, rows, lanes = everyone.shape
    experts = groups * SUBLANES
    f32 = jnp.float32
    shapes = [
        ((ITERS + 1, devices, rows, lanes), f32),
        ((ITERS, devices, SUBLANES, lanes), f32),
        ((ITERS, rows, lanes), f32),
        ((devices, experts, lanes), f32),
        ((devices, experts, lanes), f32),
        ((devices, experts, lanes), jnp.int32),
        ((devices * capacity, lanes), f32),
        ((rows, lanes), f32),
    ]
    vmem = pl.BlockSpec(memory_space=pltpu.VMEM)
    return pl.pallas_call(
        partial(
            forward_kernel,
            groups=groups,
            top_count=top_count,
            capacity=capacity,
            targets=targets,
            cube=cube,
        ),
        out_shape=[jax.ShapeDtypeStruct(s, d) for s, d in shapes],
        in_specs=[vmem],
        out_specs=[pl.BlockSpec(memory_space=pl.ANY)] + [vmem] * (len(shapes) - 1),
        scratch_shapes=[
            pltpu.VMEM((devices, experts, lanes), f32),
            pltpu.VMEM((devices, experts, lanes), f32),
            pltpu.VMEM(shapes[0][0], f32),
            pltpu.SemaphoreType.DMA((ITERS + 1,)),
        ],
        cost_estimate=pl.CostEstimate(flops=10_000_000, bytes_accessed=8_000_000, transcendentals=0),
        name="forward",
    )(everyone)


def product_kernel(table_ref, rows_ref, weight_ref, *refs, carried, last):
    refs = list(refs)
    unscaled = lax.dot_general(
        rows_ref[...],
        weight_ref[...],
        (((1,), (1,)), ((), ())),
        preferred_element_type=jnp.float32,
    )
    if carried:
        unscaled = unscaled + refs.pop(0)[...]
    if not last:
        refs[-1][...] = unscaled
        return
    saved_ref, gate_ref = refs[:2]
    grad_ref, slot_ref, sum_ref = refs[-3:]
    grad_ref[...] = (gate_ref[:, :1] * unscaled).astype(grad_ref.dtype)
    partial_sums = unscaled * saved_ref[...].astype(jnp.float32)
    folded = partial_sums[:, :LANES]
    for j in range(1, partial_sums.shape[1] // LANES):
        folded = folded + partial_sums[:, j * LANES : (j + 1) * LANES]
    first = pl.program_id(0) == 0

    @pl.when(first)
    def _():
        sum_ref[...] = folded

    @pl.when(jnp.logical_not(first))
    def _():
        sum_ref[...] = sum_ref[...] + folded

    @pl.when(pl.program_id(0) == pl.num_programs(0) - 1)
    def _():
        sums = jnp.sum(sum_ref[...].T, 0, keepdims=True)
        for d in range(slot_ref.shape[0]):
            slot_ref[d, 0] = sums


def product(
    table, entry, rows, weight, saved, gates, copies, grant, earlier=(), part=0, carried=None,
    last=True
):
    slots, width = rows.shape
    hidden = weight.shape[0]
    total = saved.shape[0]
    block = 512 if hidden % 512 == 0 else hidden
    row_block = pl.BlockSpec((slots, block), lambda i, table: (table[entry], i))
    own_block = pl.BlockSpec((slots, block), lambda i, table: (0, i))
    operands = [rows, weight]
    in_specs = [
        pl.BlockSpec((slots, width), lambda i, table: (0, 0)),
        pl.BlockSpec((block, width), lambda i, table: (i, part)),
    ]
    if carried is not None:
        operands.append(carried)
        in_specs.append(own_block)
    if last:
        operands += [saved, gates]
        in_specs += [row_block, pl.BlockSpec((slots, LANES), lambda i, table: (table[entry], 0))]
        out_shape = [
            jax.ShapeDtypeStruct((total, hidden), jnp.bfloat16),
            jax.ShapeDtypeStruct((copies, total // slots, 1, slots), jnp.float32),
        ]
        out_specs = [
            row_block,
            pl.BlockSpec((copies, 1, 1, slots), lambda i, table: (0, table[entry], 0, 0)),
        ]
        scratch = [pltpu.VMEM((slots, LANES), jnp.float32)]
    else:
        out_shape = jax.ShapeDtypeStruct((slots, hidden), jnp.float32)
        out_specs = own_block
        scratch = []
    first = 1 + len(operands)
    return pl.pallas_call(
        partial(product_kernel, carried=carried is not None, last=last),
        out_shape=out_shape,
        grid_spec=pltpu.PrefetchScalarGridSpec(
            num_scalar_prefetch=1,
            grid=(hidden // block,),
            in_specs=in_specs + [pl.BlockSpec(memory_space=pl.ANY)] * len(earlier),
            out_specs=out_specs,
            scratch_shapes=scratch,
        ),
        input_output_aliases={first + i: i for i in range(len(earlier))},
        compiler_params=pltpu.CompilerParams(vmem_limit_bytes=grant),
        cost_estimate=pl.CostEstimate(
            flops=2 * slots * width * hidden,
            bytes_accessed=2 * (slots * width + hidden * width + 2 * slots * hidden),
            transcendentals=0,
        ),
        name="product",
    )(table, *operands, *earlier)


def adjoint_kernel(
    answer_ref, level_ref, inverse_ref, column_ref, seed_q_ref, seed_p_ref, where_ref,
    own_ref, group_ref, expert_ref, carry_ref, slot_ref, *, groups, capacity, targets
):
    devices = level_ref.shape[1]
    tiles = groups + 1
    tile = (SUBLANES, LANES)
    row_id = lax.broadcasted_iota(jnp.int32, tile, 0)
    zero = jnp.zeros(tile, jnp.float32)
    per_block = LANES // capacity
    width = answer_ref.shape[3]
    for e in range(answer_ref.shape[0]):
        for h in range(answer_ref.shape[1]):
            slot_ref[e : e + 1, h * width : (h + 1) * width] = answer_ref[e, h]

    def seeds(d):
        block = pl.ds(pl.multiple_of(lax.div(d, per_block) * LANES, LANES), LANES)
        grads = []
        mixed = jnp.zeros((1, LANES), jnp.float32)
        for g in range(groups):
            rows = pl.ds(SUBLANES * g, SUBLANES)
            grad = jnp.take_along_axis(slot_ref[rows, block], where_ref[d, rows, :], axis=1)
            gate = seed_q_ref[d, rows, :] * level_ref[ITERS, d, tile_rows(g), :]
            mixed = mixed + jnp.sum(gate * grad, 0, keepdims=True)
            grads.append(grad)
        out = [zero]
        for g in range(groups):
            rows = pl.ds(SUBLANES * g, SUBLANES)
            grad = grads[g] - mixed
            out.append(seed_q_ref[d, rows, :] * grad)
            level = jnp.sum(seed_p_ref[d, rows, :] * grad, 0, keepdims=True)
            out[0] = jnp.where(row_id == g, level, out[0])
        return out

    def factors_of(k):
        out = []
        for i in range(tiles):
            column = column_ref[k, pl.ds(SUBLANES * i, SUBLANES), :]
            factor = targets[min(i, 1)] / column
            if i == 0:
                factor = jnp.where(row_id < groups, factor, 0.0)
            out.append((factor, column))
        return out

    inner = None
    for k in reversed(range(ITERS)):
        if inner is not None:
            scale = []
            for i, (factor, column) in enumerate(factors_of(k + 1)):
                total = jnp.sum(inner[i], 1, keepdims=True) + zero
                scale.append((factor, total / column))

        def step(d, sums, k=k):
            if k == ITERS - 1:
                grads = seeds(d)
            else:
                grads = [
                    scale[i][0] * (carry_ref[d, pl.ds(SUBLANES * i, SUBLANES), :] - scale[i][1])
                    for i in range(tiles)
                ]
            new = []
            for i in range(tiles):
                rows = pl.ds(SUBLANES * i, SUBLANES)
                along = jnp.sum(grads[i] * level_ref[k + 1, d, rows, :], 0, keepdims=True)
                scaled = (grads[i] - along) * inverse_ref[k, d, pl.ds(i, 1), :]
                carry_ref[d, rows, :] = scaled
                new.append(sums[i] + scaled * level_ref[k, d, rows, :])
            return tuple(new)

        inner = lax.fori_loop(0, devices, step, (zero,) * tiles, unroll=8)

    me = lax.axis_index(AXES)
    for i, (factor, column) in enumerate(factors_of(0)):
        rows = pl.ds(SUBLANES * i, SUBLANES)
        total = jnp.sum(inner[i], 1, keepdims=True) + zero
        carry_ref[0, rows, :] = (
            factor * (carry_ref[me, rows, :] - total / column) * own_ref[rows, :]
        )
    group_ref[...] = carry_ref[0, :groups, :]
    expert_ref[...] = carry_ref[0, SUBLANES:, :]


def adjoint(slot_grads, saved, own, groups, capacity, targets):
    level = saved[0]
    _, lanes = level.shape[2:]
    vmem = pl.BlockSpec(memory_space=pltpu.VMEM)
    return pl.pallas_call(
        partial(adjoint_kernel, groups=groups, capacity=capacity, targets=targets),
        out_shape=[
            jax.ShapeDtypeStruct((groups, lanes), jnp.float32),
            jax.ShapeDtypeStruct((groups * SUBLANES, lanes), jnp.float32),
        ],
        in_specs=[vmem] * (2 + len(saved)),
        out_specs=[vmem, vmem],
        scratch_shapes=[
            pltpu.VMEM(level.shape[1:], jnp.float32),
            pltpu.VMEM((groups * SUBLANES, level.shape[1] * capacity), jnp.float32),
        ],
        compiler_params=pltpu.CompilerParams(vmem_limit_bytes=24 << 20),
        cost_estimate=pl.CostEstimate(flops=10_000_000, bytes_accessed=8_000_000, transcendentals=0),
        name="adjoint",
    )(slot_grads, *saved, own)


def column_parts(width):
    return 2 if width % (2 * LANES) == 0 else 1


def cube_bits(groups, per_group):
    low = per_group.bit_length() - 1
    high = (groups * per_group).bit_length() - 1
    return [*range(low, high), *range(low)]


def replicated(group_logits, expert_logits, expert_ids, cotangent, hidden_saved, w_down):
    groups = lax.axis_size(("half", "plane"))
    per_group = lax.axis_size("expert")
    near = lax.axis_size(NEAR)
    experts = groups * per_group
    tokens_here, top_count = expert_ids.shape
    width = cotangent.shape[1]
    capacity = hidden_saved.shape[1] // experts
    targets = (float(tokens_here * per_group), float(tokens_here * groups))
    half = lax.axis_index("half")
    table = jnp.stack([half, 1 - half]).astype(jnp.int32)

    planes = lax.axis_size("plane")

    parts = column_parts(width)

    mine, own_packed, *cut_rows = first_rows(
        group_logits, expert_ids, expert_logits, cotangent, near, capacity, parts
    )
    column = [mine]
    for across in range(1, groups):
        pairs = [(d, d ^ (across * per_group)) for d in range(experts)]
        column.append(lax.ppermute(mine, AXES, pairs))
    other = column[planes]
    cube = cube_bits(groups, per_group)
    everyone = jnp.stack(column)
    for bit in cube[groups.bit_length() - 1 :]:
        pairs = [(d, d ^ (1 << bit)) for d in range(experts)]
        everyone = jnp.concatenate([everyone, lax.ppermute(everyone, AXES, pairs)])

    swapped = []
    for i, block in enumerate(cut_rows):
        swapped.append([])
        for j in range(planes):
            up, down = (j, j + planes), (2 * planes - 1 - j, planes - 1 - j)
            swapped[i].append(lax.ppermute(block, ("half", "plane"), [up, down]))

    def send(packed):
        packed = packed.reshape(near, capacity, -1)
        got = lax.all_to_all(packed, NEAR, split_axis=0, concat_axis=0)
        return got.reshape(near * capacity, -1)

    weight, hidden = w_down[0], hidden_saved[0]
    own_rows = send(own_packed)
    other_rows = []
    for i in range(parts):
        other_packed = pack_rows(other, swapped[i], near, capacity, groups, top_count)
        other_rows.append(send(other_packed))
    *saved, gates, own = forward(everyone, cube, groups, top_count, capacity, targets)
    result = product(table, 0, own_rows, weight, hidden, gates, experts, OWN_VMEM)
    carried = None
    for i in range(parts):
        last = i == parts - 1
        carried = product(
            table, 1, other_rows[i], weight, hidden, gates, experts,
            OTHER_VMEM if last else OWN_VMEM, result if last else (), i, carried, last,
        )
    result = carried
    hidden_grad, slot_grad = result
    slot_grads = lax.all_to_all(slot_grad, AXES, split_axis=0, concat_axis=0)
    d_group, d_expert = adjoint(slot_grads, saved, own, groups, capacity, targets)
    return (hidden_grad[None], d_group.T, d_expert.T)


def per_device(group_logits, expert_logits, expert_ids, cotangent, hidden_saved, w_down):
    groups = lax.axis_size(("half", "plane"))
    per_group = lax.axis_size("expert")
    tokens_here, top_count = expert_ids.shape
    capacity = hidden_saved.shape[1] // (groups * per_group)
    everyone_bytes = 4 * tokens_here * (groups * per_group) * (groups * per_group + SUBLANES)
    fits = (
        tokens_here == LANES
        and groups in (2, 4)
        and column_parts(cotangent.shape[1]) == 2
        and per_group == SUBLANES
        and groups + top_count <= SUBLANES
        and LANES % capacity == 0
        and capacity % SUBLANES == 0
        and everyone_bytes <= REPLICATED_BYTES
    )
    form = replicated if fits else distributed
    return form(group_logits, expert_logits, expert_ids, cotangent, hidden_saved, w_down)


def solution(mesh):
    groups, per_group = mesh.shape["group"], mesh.shape["expert"]
    halves = 2 if groups % 2 == 0 else 1
    parts = Mesh(mesh.devices.reshape(halves, groups // halves, per_group), AXES)
    rows = P(AXES, None)
    blocks = P(AXES, None, None)
    return jax.shard_map(
        per_device,
        mesh=parts,
        in_specs=(rows, rows, rows, rows, blocks, blocks),
        out_specs=(blocks, rows, rows),
        check_vma=False,
    )
```
